32 devices in a mesh: req: 8 (over y, x, core), tp: 4 (over z).
Axes of the slice: x: 2, y: 2, z: 4, core: 2. Of those that a mesh axis runs over, the one named last changes fastest.
Arguments:
- suffix_heads: bfloat16 [4096, 3, 2048], P('req', None, 'tp')
- prefix_cache: bfloat16 [4096, 2, 2048], P('req', None, 'tp'), may hold values from -6 to 6
- lengths: int32 [8, 8], P('req'), may hold values from 1 to 128, 512 in all within a row
- groups: int32 [8, 8], P('req'), may hold values from 0 to 3
- owners: int32 [4, 2], replicated, may hold values from 0 to 7, as said below
- out_weight: bfloat16 [2048, 4096], P('tp'), may hold values from -3 to 3
Outputs:
- attention_out: bfloat16 [4096, 4096], P('req', 'tp')
The draws below stay inside these ranges and needn't reach their ends.
Inputs may be any that keep to these rules, and one draw needn't show every extreme that they name: `lengths`: each row sums to 512; the largest length in every row is exactly 128. `owners`: all entries are distinct; the first and the last index of req are always among them.
All inputs are finite; a program needn't handle non-finite values.
Results may differ from the reference program's by a relative error of at most 0.012.
Values may be sent and summed in bfloat16 or wider, within the bound.
No kernel may reach another device: no remote copies, remote signals or barrier semaphores. Data moves between devices by JAX's collectives and lax.ppermute only.
A program may use at most 64 MiB of HBM per device.

```python
import math
import jax
import jax.numpy as jnp
import numpy as np
from jax import lax

D = 4096
HD = 256
ROT = 64
HEADS = 8
S_DEV = 512
R_DEV = 8
BLK = 512
OWNERS = 2
GROUPS = 4
MOST = 128
FEAT = 2048
N_REQ = 8


def draw_suffix_heads(key, part):
    row_count = N_REQ * S_DEV
    key_base = jax.random.fold_in(key, 0)
    drawn = jnp.clip(jax.random.normal(key_base, (row_count, 3, HEADS * HD), jnp.float32), -6.0, 6.0)
    return drawn.astype(jnp.bfloat16)


def draw_owners(key, part):
    key_middle, key_order = jax.random.split(key, 2)
    middle = 1 + jax.random.permutation(key_middle, N_REQ - 2)[:GROUPS * OWNERS - 2]
    chosen = jnp.concatenate([jnp.array([0, N_REQ - 1], dtype=jnp.int32), middle.astype(jnp.int32)])
    chosen = chosen[jax.random.permutation(key_order, GROUPS * OWNERS)]
    return chosen.reshape(GROUPS, OWNERS).astype(jnp.int32)


def plant(values, key, low, largest):
    place = [jax.random.randint(jax.random.fold_in(key, axis), (), 0, length) for axis, length in enumerate(values.shape)]
    widest = values.shape.index(max(values.shape))
    neighbour = place[:widest] + [(place[widest] + 1) % values.shape[widest]] + place[widest + 1:]
    return values.at[tuple(place)].set(low).at[tuple(neighbour)].set(largest)


def shard_levels(key, extent, pieces, least, top_value):
    def one(axis_at, parts):
        steps = jax.random.uniform(jax.random.fold_in(jax.random.fold_in(key, 6), axis_at), (parts,), jnp.float32, least / len(pieces), top_value / len(pieces))
        return jnp.repeat(jnp.exp(steps), extent[axis_at] // parts).reshape((-1,) + (1,) * (len(extent) - axis_at - 1))

    gain = one(*pieces[0])
    for cut in pieces[1:]:
        gain = gain * one(*cut)
    return gain


def split_up(number_of, total, limit, lean):
    weights = [(1 << 20) // math.isqrt(grade ** lean) + 1 for grade in range(2, number_of + 1)]
    rest, given = total - limit - (number_of - 1), [1] * (number_of - 1)
    while rest > 0:
        movable = [i for i in range(number_of - 1) if given[i] < limit]
        pool, budget = sum([weights[i] for i in movable]), rest
        for i in movable:
            more = min(limit - given[i], max(1, budget * weights[i] // pool), rest)
            given[i] = given[i] + more
            rest = rest - more
    return np.array([limit] + given)


def uneven(own_key, number_of, total, reach, skew):
    if number_of == 2:
        one = jax.random.randint(own_key, (), max(1, total - reach), min(reach, total - 1) + 1)
        return jnp.stack([one, total - one])
    tallies = jnp.asarray(split_up(number_of, total, reach, skew), jnp.int32)
    couples = (number_of - 1) // 2
    giver, taker = tallies[1:1 + 2 * couples:2], tallies[2:2 + 2 * couples:2]
    room = jnp.minimum(giver - 1, reach - taker)
    moved = jax.random.randint(jax.random.fold_in(own_key, 1), (couples,), 0, 1 << 20) % (room + 1)
    tallies = tallies.at[1:1 + 2 * couples:2].set(giver - moved).at[2:2 + 2 * couples:2].set(taker + moved)
    return tallies[jax.random.permutation(jax.random.fold_in(own_key, 2), number_of)]


def centred(rng, extent, spread, most, cuts=(), kind=jnp.bfloat16):
    loudness = shard_levels(rng, extent, cuts, -0.22, 0.18) if cuts else 1.0
    result = jax.random.normal(rng, extent, jnp.float32) * spread * loudness
    return jnp.minimum(jnp.maximum(result, -most), most).astype(kind)


def setup_inputs(seed: int = 0) -> dict:
    arg_keys = jax.random.split(jax.random.key(seed), 7)
    return {
        "suffix_heads": draw_suffix_heads(jax.random.fold_in(arg_keys[6], 71), 0),
        "prefix_cache": centred(arg_keys[1], (N_REQ * BLK, 2, FEAT), 1.0, 6.0, ((0, 8), (2, 4))),
        "lengths": jax.vmap(lambda own: uneven(own, R_DEV, S_DEV, MOST, 2))(jax.random.split(arg_keys[2], N_REQ)).reshape((N_REQ, R_DEV)).astype(jnp.int32),
        "groups": plant(jax.random.randint(arg_keys[3], (N_REQ, R_DEV), 0, GROUPS), jax.random.fold_in(arg_keys[3], 1), 0, GROUPS - 1).astype(jnp.int32),
        "owners": draw_owners(jax.random.fold_in(arg_keys[6], 71), 0),
        "out_weight": centred(arg_keys[5], (FEAT, D), 0.5, 3.0, ((0, 4),)),
    }


NEG_FILL = -1.0e30
ROPE_BASE = 10000.0


def stored(values):
    rounded = lax.optimization_barrier(values.astype(jnp.bfloat16))
    return rounded.astype(jnp.float32)


def token_layout(length_row, group_row, row_count):
    span_end = jnp.cumsum(length_row).astype(jnp.int32)
    starts = (span_end - length_row).astype(jnp.int32)
    row_ids = jnp.arange(row_count, dtype=jnp.int32)
    member = ((row_ids[:, None] >= starts[None, :]) & (row_ids[:, None] < span_end[None, :])).astype(jnp.int32)
    request = jnp.sum(member * jnp.arange(length_row.shape[0], dtype=jnp.int32)[None, :], axis=1).astype(jnp.int32)
    first_row = jnp.sum(member * starts[None, :], axis=1).astype(jnp.int32)
    tok_group = jnp.sum(member * group_row[None, :], axis=1).astype(jnp.int32)
    return row_ids, request, (row_ids - first_row).astype(jnp.int32), tok_group


def rotary(heads_in, positions):
    inverse = ROPE_BASE ** (-2.0 * jnp.arange(ROT // 2, dtype=jnp.float32) / ROT)
    angles = positions.astype(jnp.float32)[:, None] * inverse[None, :]
    sines = jnp.repeat(jnp.sin(angles), 2, axis=1)[:, None, :]
    cosines = jnp.repeat(jnp.cos(angles), 2, axis=1)[:, None, :]
    leading = heads_in[..., :ROT]
    even_part = leading[..., 0::2]
    odd_part = leading[..., 1::2]
    turned = jnp.stack((-odd_part, even_part), axis=-1).reshape(leading.shape)
    return jnp.concatenate((leading * cosines + turned * sines, heads_in[..., ROT:]), axis=-1)


def reference(suffix_heads, prefix_cache, lengths, groups, owners, out_weight):
    slot_count = GROUPS * OWNERS
    cached = prefix_cache.reshape(N_REQ, BLK, 2, HEADS * HD)
    shared = cached[owners.reshape(-1)].reshape(slot_count * BLK, 2, HEADS * HD)
    prefix_keys = shared[:, 0].reshape(slot_count * BLK, HEADS, HD).astype(jnp.float32)
    prefix_values = shared[:, 1].reshape(slot_count * BLK, HEADS, HD).astype(jnp.float32)
    key_group = (jnp.arange(slot_count * BLK, dtype=jnp.int32) // (OWNERS * BLK)).astype(jnp.int32)
    score_scale = HD ** -0.5
    buffers = suffix_heads.reshape(N_REQ, S_DEV, 3, HEADS, HD)

    def one_buffer(buffer_items):
        buffer, length_row, group_row = buffer_items
        row_ids, request, offsets, tok_group = token_layout(length_row, group_row, S_DEV)
        positions = (OWNERS * BLK + offsets).astype(jnp.int32)
        queries = stored(rotary(buffer[:, 0].astype(jnp.float32), positions))
        keys_new = stored(rotary(buffer[:, 1].astype(jnp.float32), positions))
        values_new = buffer[:, 2].astype(jnp.float32)
        causal = (request[:, None] == request[None, :]) & (row_ids[None, :] <= row_ids[:, None])
        visible = tok_group[:, None] == key_group[None, :]
        local_scores = jnp.where(causal[None], jnp.einsum("shd,uhd->hsu", queries, keys_new) * score_scale, NEG_FILL)
        prefix_scores = jnp.where(visible[None], jnp.einsum("shd,phd->hsp", queries, prefix_keys) * score_scale, NEG_FILL)
        peak = jnp.maximum(jnp.max(local_scores, axis=2, keepdims=True), jnp.max(prefix_scores, axis=2, keepdims=True))
        local_exp = jnp.exp(local_scores - peak)
        prefix_exp = jnp.exp(prefix_scores - peak)
        weight_sum = jnp.sum(local_exp, axis=2, keepdims=True) + jnp.sum(prefix_exp, axis=2, keepdims=True)
        weighted = jnp.einsum("hsu,uhd->shd", stored(local_exp), values_new)
        weighted = weighted + jnp.einsum("hsp,phd->shd", stored(prefix_exp), prefix_values)
        attended = weighted / jnp.transpose(weight_sum, (1, 0, 2))
        return attended.reshape(S_DEV, HEADS * HD).astype(jnp.bfloat16)

    attended_all = lax.map(one_buffer, (buffers, lengths, groups)).reshape(N_REQ * S_DEV, HEADS * HD)
    return jnp.dot(attended_all, out_weight, preferred_element_type=jnp.float32).astype(jnp.bfloat16)
```

```python
import functools
import jax
import jax.numpy as jnp
from jax import lax
from jax.experimental import pallas as pl
from jax.experimental.pallas import tpu as pltpu
from jax.sharding import PartitionSpec as P

HD = 256
ROT = 64
BLK = 512
OWNERS = 2
GROUPS = 4
SLOTS = GROUPS * OWNERS
MOST = 128

NEG_FILL = -1e30
ROPE_BASE = 10000.0
LOG2E = 1.4426950408889634
SCALE = HD ** (-0.5)

VMEM = pl.BlockSpec(memory_space=pltpu.VMEM)
SMEM = pl.BlockSpec(memory_space=pltpu.SMEM)
ANY = pl.BlockSpec(memory_space=pl.ANY)


def from_root(x, axis, root):
    mine = lax.axis_index(axis) == root
    return lax.psum(jnp.where(mine, x, jnp.zeros_like(x)), axis)


def token_layout(length_row, group_row, row_count):
    span_end = jnp.cumsum(length_row)
    starts = span_end - length_row
    row_ids = jnp.arange(row_count, dtype=jnp.int32)
    member = (
        (row_ids[:, None] >= starts[None, :]) & (row_ids[:, None] < span_end[None, :])
    ).astype(jnp.int32)
    first_row = jnp.sum(member * starts[None, :], axis=1)
    tok_group = jnp.sum(member * group_row[None, :], axis=1)
    return row_ids, first_row, tok_group


def rope_tables(positions):
    inverse = ROPE_BASE ** (-2.0 * jnp.arange(ROT // 2, dtype=jnp.float32) / ROT)
    inverse = jnp.concatenate([jnp.repeat(inverse, 2), jnp.zeros((128 - ROT,), jnp.float32)])
    angles = positions.astype(jnp.float32)[:, None] * inverse[None, :]
    sign = jnp.where(jnp.arange(128) % 2 == 0, -1.0, 1.0).astype(jnp.float32)
    return jnp.cos(angles), jnp.sin(angles) * sign[None, :]


def prep_kernel(x_ref, cos_ref, sin_ref, o_ref):
    rows = x_ref.shape[0]
    lane = lax.broadcasted_iota(jnp.int32, (rows, 128), 1)
    even = (lane % 2) == 0
    cos = cos_ref[...]
    sin = sin_ref[...]
    for i in range(x_ref.shape[1] // HD):
        x = x_ref[:, i * HD : i * HD + 128].astype(jnp.float32)
        swapped = jnp.where(even, pltpu.roll(x, 127, 1), pltpu.roll(x, 1, 1))
        o_ref[i, :, 0:128] = (x * cos + swapped * sin).astype(jnp.bfloat16)
        o_ref[i, :, 128:HD] = x_ref[:, i * HD + 128 : (i + 1) * HD]


def rotate(x, cos, sin):
    rows = x.shape[0]
    return pl.pallas_call(
        prep_kernel,
        out_shape=jax.ShapeDtypeStruct((x.shape[1] // HD, rows, HD), jnp.bfloat16),
        in_specs=[VMEM] * 3,
        out_specs=VMEM,
        name="rotate",
    )(x, cos, sin)


RB = 128


def attn_kernel(head, heads, pos_ref, qk_ref, v_ref, first_ref, grp_ref, *rest):
    pieces_k = rest[:SLOTS]
    pieces_v = rest[SLOTS : 2 * SLOTS]
    o_ref, ks, vs, sems = rest[2 * SLOTS :]
    rows = o_ref.shape[0]
    copies_k = []
    copies_v = []
    for d in range(SLOTS):
        copies_k.append(pltpu.make_async_copy(pieces_k[d], ks.at[pos_ref[d]], sems.at[0, d]))
        copies_v.append(pltpu.make_async_copy(pieces_v[d], vs.at[pos_ref[d]], sems.at[1, d]))
    for c in copies_k + copies_v:
        c.start()
    for c in copies_k:
        c.wait()
    for c in copies_v:
        c.wait()
    factor = SCALE * LOG2E
    half = 256
    nb = rows // RB
    for b in range(nb):
        r0 = b * RB
        q = qk_ref[head, r0 : r0 + RB, :]
        grp = jnp.broadcast_to(grp_ref[r0 : r0 + RB, :], (RB, half))
        scores = []
        for o in range(OWNERS):
            for j in range(BLK // half):
                acc = None
                for g in range(GROUPS):
                    s = lax.dot_general(
                        q,
                        ks[g * OWNERS + o, j * half : (j + 1) * half, :],
                        (((1,), (1,)), ((), ())),
                        preferred_element_type=jnp.float32,
                    )
                    acc = s if acc is None else jnp.where(grp == g, s, acc)
                scores.append(acc)
        lo = max(0, r0 - MOST)
        width = r0 + RB - lo
        local = lax.dot_general(
            q,
            qk_ref[heads + head, lo : r0 + RB, :],
            (((1,), (1,)), ((), ())),
            preferred_element_type=jnp.float32,
        )
        row = r0 + lax.broadcasted_iota(jnp.int32, (RB, width), 0)
        key = lo + lax.broadcasted_iota(jnp.int32, (RB, width), 1)
        seen = (key <= row) & (key >= jnp.broadcast_to(first_ref[r0 : r0 + RB, :], (RB, width)))
        local = jnp.where(seen, local, NEG_FILL)
        top = jnp.max(local, axis=1, keepdims=True)
        whole = scores[0]
        for s in scores[1:]:
            whole = jnp.maximum(whole, s)
        top = jnp.maximum(top, jnp.max(whole, axis=1, keepdims=True))
        e_local = jnp.exp2((local - top) * factor)
        den = jnp.sum(e_local, axis=1, keepdims=True)
        out = jnp.dot(
            e_local.astype(jnp.bfloat16), v_ref[lo : r0 + RB, :], preferred_element_type=jnp.float32
        )
        total = None
        i = 0
        for o in range(OWNERS):
            for j in range(BLK // half):
                e = jnp.exp2((scores[i] - top) * factor)
                i += 1
                total = e if total is None else total + e
                for g in range(GROUPS):
                    w = jnp.where(grp == g, e, 0.0).astype(jnp.bfloat16)
                    out = out + jnp.dot(
                        w,
                        vs[g * OWNERS + o, j * half : (j + 1) * half, :],
                        preferred_element_type=jnp.float32,
                    )
        den = den + jnp.sum(total, axis=1, keepdims=True)
        o_ref[r0 : r0 + RB, :] = (out / den).astype(jnp.bfloat16)


def attend(head, heads, place, qk, v, first, grp, keys, values):
    rows = qk.shape[1]
    return pl.pallas_call(
        functools.partial(attn_kernel, head, heads),
        out_shape=jax.ShapeDtypeStruct((rows, HD), jnp.bfloat16),
        in_specs=[SMEM, VMEM, VMEM, VMEM, VMEM] + [ANY] * (2 * SLOTS),
        out_specs=VMEM,
        scratch_shapes=[
            pltpu.VMEM((SLOTS, BLK, HD), jnp.bfloat16),
            pltpu.VMEM((SLOTS, BLK, HD), jnp.bfloat16),
            pltpu.SemaphoreType.DMA((2, SLOTS)),
        ],
        compiler_params=pltpu.CompilerParams(vmem_limit_bytes=32 << 20),
        name=f"attend{head}",
    )(place, qk, v, first, grp, *keys, *values)


def proj_kernel(parts, where_ref, *refs):
    n_att = 2 * parts
    att = refs[:n_att]
    w_ref = refs[n_att]
    pieces = refs[n_att + 1 : n_att + 1 + 16]
    o_ref, own, far, sems = refs[n_att + 17 :]
    cols = o_ref.shape[1]
    z = where_ref[0]
    chip = where_ref[1]
    core = where_ref[2]
    copies = [
        pltpu.make_async_copy(
            w_ref.at[:, pl.ds(pl.multiple_of(z * cols, cols), cols)], own, sems.at[16]
        )
    ]
    for d in range(8):
        head = lax.bitwise_xor(core, d & 1)
        block = lax.bitwise_xor(chip, d >> 1)
        for s in range(2):
            copies.append(
                pltpu.make_async_copy(
                    pieces[2 * d + s],
                    far.at[
                        :,
                        head,
                        s * 128 : (s + 1) * 128,
                        pl.ds(pl.multiple_of(block * HD, HD), HD),
                    ],
                    sems.at[2 * d + s],
                )
            )
    for c in copies:
        c.start()
    for c in copies:
        c.wait()
    rows = o_ref.shape[0]
    for n in range(cols // HD):
        c0 = n * HD
        acc = jnp.zeros((rows, HD), jnp.float32)
        for m in range(parts):
            for h in range(2):
                if m == 0:
                    w = own[h * HD : (h + 1) * HD, c0 : c0 + HD]
                else:
                    w = far[m - 1, h, :, c0 : c0 + HD]
                acc = acc + jnp.dot(att[2 * m + h][...], w, preferred_element_type=jnp.float32)
        o_ref[:, c0 : c0 + HD] = acc.astype(jnp.bfloat16)


def project(where, att, w, pieces, cols):
    rows = att[0].shape[0]
    parts = len(att) // 2
    return pl.pallas_call(
        functools.partial(proj_kernel, parts),
        out_shape=jax.ShapeDtypeStruct((rows, cols), jnp.bfloat16),
        in_specs=[SMEM] + [VMEM] * len(att) + [ANY] * (1 + len(pieces)),
        out_specs=VMEM,
        scratch_shapes=[
            pltpu.VMEM((w.shape[0], cols), jnp.bfloat16),
            pltpu.VMEM((parts - 1, 2, HD, cols), jnp.bfloat16),
            pltpu.SemaphoreType.DMA((17,)),
        ],
        compiler_params=pltpu.CompilerParams(vmem_limit_bytes=32 << 20),
        name="project",
    )(where, *att, w, *pieces)


def swap(x, axis, mask, size):
    return lax.ppermute(x, axis, [(i, i ^ mask) for i in range(size)])


def after(x, *deps):
    return lax.optimization_barrier((x,) + deps)[0]


def spread_pair(a, b):
    x = functools.partial(swap, axis="req", mask=2, size=8)
    y = functools.partial(swap, axis="req", mask=4, size=8)
    c = functools.partial(swap, axis="req", mask=1, size=8)
    ax = x(a)
    by = y(b)
    ay = y(a)
    bx = x(b)
    axy = y(ax)
    bxy = x(by)
    return (
        [a, c(a), ax, c(ax), ay, c(ay), axy, c(axy)],
        [b, c(b), bx, c(bx), by, c(by), bxy, c(bxy)],
    )


def per_device(req_size, tp_size, suffix_heads, prefix_cache, lengths, groups, owners, out_weight):
    row_count = suffix_heads.shape[0]
    local_feat = suffix_heads.shape[2]
    heads = local_feat // HD
    row_ids, first, tok_group = token_layout(lengths[0], groups[0], row_count)
    positions = OWNERS * BLK + row_ids - first
    cos, sin = rope_tables(positions)
    first = first[:, None]
    grp = tok_group[:, None]
    me = lax.axis_index("req")
    z = lax.axis_index("tp")
    split = req_size == 8 and tp_size == 4 and heads == 2
    flat_owner = owners.reshape(-1)

    if split:
        cols = out_weight.shape[1] // tp_size
        pieces = []
        for m in range(1, tp_size):
            piece = lax.dynamic_slice(
                out_weight,
                ((me % 2) * HD, (z ^ m) * cols + (me // 2) * HD),
                (HD, HD),
            )
            pieces.append(swap(piece, "tp", m, tp_size))
        place = jnp.sum(
            jnp.where(
                flat_owner[None, :] == (me ^ jnp.arange(SLOTS, dtype=jnp.int32))[:, None],
                jnp.arange(SLOTS, dtype=jnp.int32)[None, :],
                0,
            ),
            axis=1,
        ).astype(jnp.int32)
        keys = []
        values = []
        for h in range(heads):
            k = prefix_cache[:, 0, h * HD : (h + 1) * HD]
            v = prefix_cache[:, 1, h * HD : (h + 1) * HD]
            if h:
                k, v = lax.optimization_barrier((k, v, keys[-1][6], values[-1][6]))[:2]
            ks, vs = spread_pair(k, v)
            keys.append(ks)
            values.append(vs)
    else:
        place = jnp.arange(SLOTS, dtype=jnp.int32)
        received = [from_root(prefix_cache, "req", flat_owner[i]) for i in range(SLOTS)]
        keys = [[s[:, 0, h * HD : (h + 1) * HD] for s in received] for h in range(heads)]
        values = [[s[:, 1, h * HD : (h + 1) * HD] for s in received] for h in range(heads)]

    qk = rotate(
        jnp.concatenate([suffix_heads[:, 0], suffix_heads[:, 1]], axis=1), cos, sin
    )
    attended = []
    for h in range(heads):
        v = suffix_heads[:, 2, h * HD : (h + 1) * HD]
        attended.append(
            attend(h, heads, place, qk, v, first, grp, keys[h], values[h])
        )

    if split:
        last = (keys[-1][6], values[-1][6])
        stacked = jnp.stack(pieces)
        low, high = lax.optimization_barrier((stacked[:, :128], stacked[:, 128:]) + last)[:2]
        low, high = spread_pair(low, high)
        tiles = []
        for d in range(8):
            tiles += [low[d], high[d]]
        att = list(attended)
        for m in range(1, tp_size):
            for h in range(heads):
                att.append(swap(attended[h], "tp", m, tp_size))
        where = jnp.stack([z, me // 2, me % 2]).astype(jnp.int32)
        return project(where, att, out_weight, tiles, cols)
    partial_out = jnp.dot(
        jnp.concatenate(attended, axis=1), out_weight, preferred_element_type=jnp.float32
    )
    return lax.psum_scatter(partial_out.astype(jnp.bfloat16), "tp", scatter_dimension=1, tiled=True)


def solution(mesh):
    placed = (
        P("req", None, "tp"),
        P("req", None, "tp"),
        P("req", None),
        P("req", None),
        P(),
        P("tp", None),
    )
    return jax.shard_map(
        functools.partial(per_device, mesh.shape["req"], mesh.shape["tp"]),
        mesh=mesh,
        in_specs=placed,
        out_specs=P("req", "tp"),
        check_vma=False,
    )
```

```python
import functools
import jax
import jax.numpy as jnp
from jax import lax
from jax.experimental import pallas as pl
from jax.experimental.pallas import tpu as pltpu
from jax.sharding import PartitionSpec as P

HD = 256
ROT = 64
BLK = 512
OWNERS = 2
GROUPS = 4
SLOTS = GROUPS * OWNERS
MOST = 128
SEEN = OWNERS * BLK

NEG_FILL = -1e30
ROPE_BASE = 10000.0
FACTOR = HD ** (-0.5) * 1.4426950408889634

RB = 128
VCHUNKS = 2

VMEM = pl.BlockSpec(memory_space=pltpu.VMEM)
SMEM = pl.BlockSpec(memory_space=pltpu.SMEM)
HBM = pl.BlockSpec(memory_space=pltpu.HBM)


def from_root(x, axis, root):
    mine = lax.axis_index(axis) == root
    return lax.psum(jnp.where(mine, x, jnp.zeros_like(x)), axis)


def token_layout(length_row, group_row, row_count):
    span_end = jnp.cumsum(length_row)
    starts = span_end - length_row
    row_ids = jnp.arange(row_count, dtype=jnp.int32)
    member = (
        (row_ids[:, None] >= starts[None, :]) & (row_ids[:, None] < span_end[None, :])
    ).astype(jnp.int32)
    first_row = jnp.sum(member * starts[None, :], axis=1)
    tok_group = jnp.sum(member * group_row[None, :], axis=1)
    return row_ids, first_row, tok_group


def rope_tables(positions):
    inverse = ROPE_BASE ** (-2.0 * jnp.arange(ROT // 2, dtype=jnp.float32) / ROT)
    inverse = jnp.concatenate([jnp.repeat(inverse, 2), jnp.zeros((128 - ROT,), jnp.float32)])
    angles = positions.astype(jnp.float32)[:, None] * inverse[None, :]
    sign = jnp.where(jnp.arange(128) % 2 == 0, -1.0, 1.0).astype(jnp.float32)
    return jnp.cos(angles), jnp.sin(angles) * sign[None, :]


def prep_kernel(flip_ref, q_ref, k_ref, v_ref, cos_ref, sin_ref, *o_refs):
    rows = q_ref.shape[0]
    lane = lax.broadcasted_iota(jnp.int32, (rows, 128), 1)
    even = (lane % 2) == 0
    cos = cos_ref[...]
    sin = sin_ref[...]
    heads = len(o_refs)
    for i, o_ref in enumerate(o_refs):
        for flip in range(heads):

            @pl.when(flip_ref[0] == flip)
            def _():
                c0 = (i ^ flip) * HD
                for n, ref in enumerate((q_ref, k_ref)):
                    x = ref[:, c0 : c0 + 128].astype(jnp.float32)
                    swapped = jnp.where(even, pltpu.roll(x, 127, 1), pltpu.roll(x, 1, 1))
                    o_ref[n, :, 0:128] = (x * cos + swapped * sin).astype(jnp.bfloat16)
                    o_ref[n, :, 128:HD] = ref[:, c0 + 128 : c0 + HD]
                o_ref[2] = v_ref[:, c0 : c0 + HD]


def prepare(flip, q, k, v, cos, sin):
    rows, feat = q.shape
    heads = feat // HD
    return pl.pallas_call(
        prep_kernel,
        out_shape=[jax.ShapeDtypeStruct((3, rows, HD), jnp.bfloat16)] * heads,
        in_specs=[SMEM] + [VMEM] * 5,
        out_specs=[VMEM] * heads,
        compiler_params=pltpu.CompilerParams(vmem_limit_bytes=3 << 20),
        name="prepare",
    )(flip, q, k, v, cos, sin)


def fetch(pieces, members, place_ref, store, sems):
    copies = []
    for piece, member in zip(pieces, members):
        for j, d in enumerate(member):
            copies.append(
                pltpu.make_async_copy(piece.at[j], store.at[place_ref[d]], sems.at[d])
            )
    for c in copies:
        c.start()
    return copies


def score_kernel(nb, members, place_ref, here_ref, first_ref, grp_ref, *rest):
    sufs = rest[:nb]
    pieces = rest[nb : nb + len(members)]
    p_ref, near_ref, den_ref, ks, sc, sems = rest[nb + len(members) :]
    copies = fetch(pieces, members, place_ref, ks, sems)
    for c in copies:
        c.wait()
    half = 256
    for n in range(nb):
        rows = sufs[n].shape[1]
        for b in range(rows // RB):
            r0 = b * RB
            t0 = n * rows + r0
            blk = t0 // RB
            buf = blk % 2
            q = sufs[n][0, r0 : r0 + RB, :]
            grp = jnp.broadcast_to(grp_ref[t0 : t0 + RB, :], (RB, half))
            for g in range(GROUPS):

                @pl.when(here_ref[blk * GROUPS + g] > 0)
                def _():
                    for o in range(OWNERS):
                        for j in range(BLK // half):
                            s = lax.dot_general(
                                q,
                                ks[g * OWNERS + o, j * half : (j + 1) * half, :],
                                (((1,), (1,)), ((), ())),
                                preferred_element_type=jnp.float32,
                            )
                            c0 = o * BLK + j * half
                            sc[buf, :, c0 : c0 + half] = jnp.where(
                                grp == g, s, sc[buf, :, c0 : c0 + half]
                            )

            lo = max(0, r0 - MOST)
            width = r0 + RB - lo
            local = lax.dot_general(
                q,
                sufs[n][1, lo : r0 + RB, :],
                (((1,), (1,)), ((), ())),
                preferred_element_type=jnp.float32,
            )
            row = r0 + lax.broadcasted_iota(jnp.int32, (RB, width), 0)
            key = lo + lax.broadcasted_iota(jnp.int32, (RB, width), 1)
            start = jnp.broadcast_to(first_ref[t0 : t0 + RB, :], (RB, width))
            local = jnp.where((key <= row) & (key >= start), local, NEG_FILL)
            top = jnp.max(local, axis=1, keepdims=True)
            whole = sc[buf, :, 0:half]
            for c0 in range(half, SEEN, half):
                whole = jnp.maximum(whole, sc[buf, :, c0 : c0 + half])
            top = jnp.maximum(top, jnp.max(whole, axis=1, keepdims=True))
            e = jnp.exp2((local - top) * FACTOR)
            den = jnp.sum(e, axis=1, keepdims=True)
            near_ref[t0 : t0 + RB, 0:width] = e.astype(jnp.bfloat16)
            total = None
            for c0 in range(0, SEEN, half):
                e = jnp.exp2((sc[buf, :, c0 : c0 + half] - top) * FACTOR)
                p_ref[t0 : t0 + RB, c0 : c0 + half] = e.astype(jnp.bfloat16)
                total = e if total is None else total + e
            den = den + jnp.sum(total, axis=1, keepdims=True)
            den_ref[t0 : t0 + RB, :] = jnp.broadcast_to(den, (RB, 128))


def score(place, here, first, grp, sufs, pieces, members):
    rows = sum(s.shape[1] for s in sufs)
    return pl.pallas_call(
        functools.partial(score_kernel, len(sufs), members),
        out_shape=[
            jax.ShapeDtypeStruct((rows, SEEN), jnp.bfloat16),
            jax.ShapeDtypeStruct((rows, RB + MOST), jnp.bfloat16),
            jax.ShapeDtypeStruct((rows, 128), jnp.float32),
        ],
        in_specs=[SMEM, SMEM] + [VMEM] * (2 + len(sufs)) + [HBM] * len(pieces),
        out_specs=[VMEM] * 3,
        scratch_shapes=[
            pltpu.VMEM((SLOTS, BLK, HD), jnp.bfloat16),
            pltpu.VMEM((2, RB, SEEN), jnp.float32),
            pltpu.SemaphoreType.DMA((SLOTS,)),
        ],
        compiler_params=pltpu.CompilerParams(vmem_limit_bytes=5 << 20),
        name="score",
    )(place, here, first, grp, *sufs, *pieces)


def mix_kernel(nb, members, col, place_ref, here_ref, grp_ref, p_ref, near_ref, den_ref, *rest):
    sufs = rest[:nb]
    pieces = rest[nb : nb + len(members)]
    outs = rest[nb + len(members) : nb + len(members) + nb]
    vs, acc, sems = rest[nb + len(members) + nb :]
    width = outs[0].shape[1]
    copies = fetch(pieces, members, place_ref, vs, sems)
    for c in copies:
        c.wait()
    for n in range(nb):
        rows = outs[n].shape[0]
        for b in range(rows // RB):
            r0 = b * RB
            t0 = n * rows + r0
            blk = t0 // RB
            buf = blk % 2
            grp = jnp.broadcast_to(grp_ref[t0 : t0 + RB, :], (RB, width))
            for g in range(GROUPS):

                @pl.when(here_ref[blk * GROUPS + g] > 0)
                def _():
                    part = jnp.zeros((RB, width), jnp.float32)
                    for o in range(OWNERS):
                        part = part + jnp.dot(
                            p_ref[t0 : t0 + RB, o * BLK : (o + 1) * BLK],
                            vs[g * OWNERS + o],
                            preferred_element_type=jnp.float32,
                        )
                    acc[buf] = jnp.where(grp == g, part, acc[buf])

            lo = max(0, r0 - MOST)
            near = jnp.dot(
                near_ref[t0 : t0 + RB, 0 : r0 + RB - lo],
                sufs[n][2, lo : r0 + RB, col : col + width],
                preferred_element_type=jnp.float32,
            )
            den = den_ref[t0 : t0 + RB, :]
            if width > 128:
                den = jnp.concatenate([den] * (width // 128), axis=1)
            outs[n][r0 : r0 + RB, :] = ((near + acc[buf]) / den).astype(jnp.bfloat16)


def mix(col, width, place, here, grp, scored, sufs, pieces, members):
    rows = sufs[0].shape[1]
    nb = len(sufs)
    return pl.pallas_call(
        functools.partial(mix_kernel, nb, members, col),
        out_shape=[jax.ShapeDtypeStruct((rows, width), jnp.bfloat16)] * nb,
        in_specs=[SMEM, SMEM] + [VMEM] * (4 + nb) + [HBM] * len(pieces),
        out_specs=[VMEM] * nb,
        scratch_shapes=[
            pltpu.VMEM((SLOTS, BLK, width), jnp.bfloat16),
            pltpu.VMEM((2, RB, width), jnp.float32),
            pltpu.SemaphoreType.DMA((SLOTS,)),
        ],
        compiler_params=pltpu.CompilerParams(vmem_limit_bytes=3 << 20),
        name="mix",
    )(place, here, grp, *scored, *sufs, *pieces)


def proj_kernel(where_ref, *refs):
    n_att = VCHUNKS * 2 * 5
    att = refs[:n_att]
    w_ref, gathered, o_ref, own, far, sems = refs[n_att:]
    cols = o_ref.shape[1]
    rows = o_ref.shape[0]
    z = where_ref[0]
    core = where_ref[1]
    copies = []
    for h in range(2):
        copies.append(
            pltpu.make_async_copy(
                w_ref.at[
                    h * HD : (h + 1) * HD, pl.ds(pl.multiple_of(z * cols, cols), cols)
                ],
                own.at[h],
                sems.at[h],
            )
        )
    for r in range(8):
        copies.append(
            pltpu.make_async_copy(
                gathered.at[r],
                far.at[:, r & 1, :, (r >> 1) * HD : (r >> 1) * HD + HD],
                sems.at[2 + r],
            )
        )
    for c in copies:
        c.start()
    for c in copies:
        c.wait()
    for n in range(cols // HD):
        c0 = n * HD
        acc = jnp.zeros((rows, HD), jnp.float32)
        for h in range(2):
            head = lax.bitwise_xor(core, h)
            for m in range(4):
                part = []
                for i in range(VCHUNKS):
                    at = (i * 2 + h) * 5 + m
                    a = att[at][...]
                    if m == 3:
                        a = a + att[at + 1][...]
                    part.append(a)
                a = jnp.concatenate(part, axis=1)
                if m == 0:
                    w = own[head, :, c0 : c0 + HD]
                else:
                    w = far[m - 1, head, :, c0 : c0 + HD]
                acc = acc + jnp.dot(a, w, preferred_element_type=jnp.float32)
        o_ref[:, c0 : c0 + HD] = acc.astype(jnp.bfloat16)


def project(where, att, w, gathered, cols):
    rows = att[0].shape[0]
    return pl.pallas_call(
        proj_kernel,
        out_shape=jax.ShapeDtypeStruct((rows, cols), jnp.bfloat16),
        in_specs=[SMEM] + [VMEM] * len(att) + [HBM] * 2,
        out_specs=VMEM,
        scratch_shapes=[
            pltpu.VMEM((2, HD, cols), jnp.bfloat16),
            pltpu.VMEM((3, 2, HD, cols), jnp.bfloat16),
            pltpu.SemaphoreType.DMA((10,)),
        ],
        compiler_params=pltpu.CompilerParams(vmem_limit_bytes=7 << 20),
        name="project",
    )(where, *att, w, gathered)


def swap(x, axis, mask, size):
    return lax.ppermute(x, axis, [(i, i ^ mask) for i in range(size)])


def after(x, *deps):
    return lax.optimization_barrier((x,) + deps)[0]


over_x = functools.partial(swap, axis="req", mask=2, size=8)
over_y = functools.partial(swap, axis="req", mask=4, size=8)
over_core = functools.partial(swap, axis="req", mask=1, size=8)


def blocks_here(grp):
    blocks = grp.reshape(-1, RB)
    kinds = jnp.arange(GROUPS, dtype=jnp.int32)
    return jnp.any(blocks[:, None, :] == kinds[None, :, None], axis=2).astype(jnp.int32).reshape(-1)


def split_heads(suffix_heads, prefix_cache, lengths, groups, owners, out_weight):
    rows = suffix_heads.shape[0]
    me = lax.axis_index("req")
    z = lax.axis_index("tp")
    core = me % 2
    tp_size = 4
    first_head = core == 0

    k = prefix_cache[:, 0]
    v = prefix_cache[:, 1]
    k_own = jnp.where(first_head, k[:, :HD], k[:, HD:])
    k_other = jnp.where(first_head, k[:, HD:], k[:, :HD])
    ax = over_x(k_own)
    ay = over_y(k_own)
    k_pair = over_core(k_other)
    bx = over_x(k_pair)
    by = over_y(k_pair)
    axy = over_y(ax)
    bxy = over_x(by)
    k_pieces = [p[None] for p in (k_own, k_pair, ax, bx, ay, by, axy, bxy)]
    k_members = tuple((d,) for d in range(SLOTS))

    v_own = jnp.where(first_head, v[:, :HD], v[:, HD:])
    v_other = jnp.where(first_head, v[:, HD:], v[:, :HD])
    v_pair = over_core(after(v_other, ax, ay))
    width = HD // VCHUNKS
    v_pieces = []
    gate = (axy, bxy)
    for i in range(VCHUNKS):
        c0 = i * width
        both = jnp.stack([v_own[:, c0 : c0 + width], v_pair[:, c0 : c0 + width]])
        both = after(both, *gate)
        vx = over_x(both)
        vy = over_y(both)
        vxy0 = over_y(vx[0:1])
        vxy1 = over_x(vy[1:2])
        v_pieces.append((both, vx, vy, vxy0, vxy1))
        gate = (vx, vy)
    v_members = ((0, 1), (2, 3), (4, 5), (6,), (7,))

    cols = out_weight.shape[1] // tp_size
    pieces = [None] * 3
    gates = ((axy, bxy), (bx, by), (ax, ay))
    last = ()
    for m in (3, 2, 1):
        piece = lax.dynamic_slice(
            out_weight, (core * HD, (z ^ m) * cols + (me // 2) * HD), (HD, HD)
        )
        piece = after(piece, *gates[m - 1], *last)
        pieces[m - 1] = swap(piece, "tp", m, tp_size)
        last = (pieces[m - 1],)
    gathered = lax.all_gather(after(jnp.stack(pieces), v_pieces[0][1], v_pieces[0][2]), "req")

    flat_owner = owners.reshape(-1)
    place = jnp.sum(
        jnp.where(
            flat_owner[None, :] == (me ^ jnp.arange(SLOTS, dtype=jnp.int32))[:, None],
            jnp.arange(SLOTS, dtype=jnp.int32)[None, :],
            0,
        ),
        axis=1,
    ).astype(jnp.int32)

    table = jnp.concatenate([lengths, groups], axis=0)
    table_pair = over_core(table)
    row_ids, first, grp = token_layout(table[0], table[1], rows)
    _, first_pair, grp_pair = token_layout(table_pair[0], table_pair[1], rows)
    cos, sin = rope_tables(OWNERS * BLK + row_ids - first)
    first = jnp.concatenate([first, first_pair])
    grp = jnp.concatenate([grp, grp_pair])
    here = blocks_here(grp)
    first = first[:, None]
    grp = grp[:, None]
    mine, other = prepare(
        core[None].astype(jnp.int32),
        suffix_heads[:, 0],
        suffix_heads[:, 1],
        suffix_heads[:, 2],
        cos,
        sin,
    )
    sufs = [mine, over_core(other)]

    scored = score(place, here, first, grp, sufs, k_pieces, k_members)
    att = []
    for i in range(VCHUNKS):
        own, pair = mix(i * width, width, place, here, grp, scored, sufs, v_pieces[i], v_members)
        back = over_core(pair)
        for a in (own, back):
            one = swap(a, "tp", 1, tp_size)
            two = swap(a, "tp", 2, tp_size)
            three = lax.ppermute(a, "tp", [(1, 2), (2, 1)])
            forward = lax.ppermute(two, "tp", [(2, 3), (1, 0)])
            att += [a, one, two, three, forward]
    where = jnp.stack([z, core]).astype(jnp.int32)
    return project(where, att, out_weight, gathered, cols)


def whole_heads(suffix_heads, prefix_cache, lengths, groups, owners, out_weight):
    rows = suffix_heads.shape[0]
    heads = suffix_heads.shape[2] // HD
    flat_owner = owners.reshape(-1)
    received = [from_root(prefix_cache, "req", flat_owner[i]) for i in range(SLOTS)]
    row_ids, first, grp = token_layout(lengths[0], groups[0], rows)
    cos, sin = rope_tables(OWNERS * BLK + row_ids - first)
    place = jnp.arange(SLOTS, dtype=jnp.int32)
    here = blocks_here(grp)
    first = first[:, None]
    grp = grp[:, None]
    sufs = prepare(
        jnp.zeros((1,), jnp.int32),
        suffix_heads[:, 0],
        suffix_heads[:, 1],
        suffix_heads[:, 2],
        cos,
        sin,
    )
    members = tuple((d,) for d in range(SLOTS))
    attended = []
    for h in range(heads):
        keys = [s[None, :, 0, h * HD : (h + 1) * HD] for s in received]
        values = [s[None, :, 1, h * HD : (h + 1) * HD] for s in received]
        scored = score(place, here, first, grp, [sufs[h]], keys, members)
        attended += mix(0, HD, place, here, grp, scored, [sufs[h]], values, members)
    partial_out = jnp.dot(
        jnp.concatenate(attended, axis=1), out_weight, preferred_element_type=jnp.float32
    )
    return lax.psum_scatter(partial_out.astype(jnp.bfloat16), "tp", scatter_dimension=1, tiled=True)


def per_device(req_size, tp_size, *args):
    if req_size == 8 and tp_size == 4 and args[0].shape[2] == 2 * HD:
        return split_heads(*args)
    return whole_heads(*args)


def solution(mesh):
    placed = (
        P("req", None, "tp"),
        P("req", None, "tp"),
        P("req", None),
        P("req", None),
        P(),
        P("tp", None),
    )
    return jax.shard_map(
        functools.partial(per_device, mesh.shape["req"], mesh.shape["tp"]),
        mesh=mesh,
        in_specs=placed,
        out_specs=P("req", "tp"),
        check_vma=False,
    )
```

```python
import functools
import jax
import jax.numpy as jnp
import numpy as np
from jax import lax
from jax.experimental import pallas as pl
from jax.experimental.pallas import tpu as pltpu
from jax.sharding import PartitionSpec as P

HD = 256
ROT = 64
BLK = 512
OWNERS = 2
GROUPS = 4
SLOTS = GROUPS * OWNERS
MOST = 128
SEEN = OWNERS * BLK

NEG_FILL = -1e30
ROPE_BASE = 10000.0
FACTOR = HD ** (-0.5) * 1.4426950408889634

RB = 128

VMEM = pl.BlockSpec(memory_space=pltpu.VMEM)
SMEM = pl.BlockSpec(memory_space=pltpu.SMEM)


def from_root(x, axis, root):
    mine = lax.axis_index(axis) == root
    return lax.psum(jnp.where(mine, x, jnp.zeros_like(x)), axis)


def rope_table():
    inverse = np.float32(ROPE_BASE) ** (-2.0 * np.arange(ROT // 2, dtype=np.float32) / ROT)
    inverse = np.concatenate([np.repeat(inverse, 2), np.zeros(128 - ROT)]).astype(np.float32)
    angles = np.arange(SEEN, SEEN + MOST, dtype=np.float32)[:, None] * inverse[None, :]
    angles = angles.astype(np.float64)
    sign = np.where(np.arange(128) % 2 == 0, -1.0, 1.0)
    table = np.concatenate([np.cos(angles), np.sin(angles) * sign[None, :]], axis=1)
    return jnp.asarray(table.astype(np.float32))


def prep_kernel(spans, where_ref, *refs):
    tables = refs[:spans]
    q_ref, k_ref, v_ref, rope_ref = refs[spans : spans + 4]
    first_ref, grp_ref = refs[spans + 4 : spans + 6]
    o_refs = refs[spans + 6 :]
    rows = q_ref.shape[0]
    heads = len(o_refs)
    lane = lax.broadcasted_iota(jnp.int32, (RB, 128), 1)
    even = (lane % 2) == 0
    for n in range(spans):
        requests = tables[n].shape[1]
        for r0 in range(0, rows, RB):
            row = r0 + lax.broadcasted_iota(jnp.int32, (RB, 128), 0)
            start = jnp.int32(0)
            first = jnp.zeros((RB, 128), jnp.int32)
            grp = jnp.zeros((RB, 128), jnp.int32) + tables[n][1, 0]
            for r in range(1, requests):
                start = start + tables[n][0, r - 1]
                later = row >= start
                first = jnp.where(later, start, first)
                grp = jnp.where(later, tables[n][1, r], grp)
            first_ref[n * rows + r0 : n * rows + r0 + RB, :] = first
            grp_ref[n * rows + r0 : n * rows + r0 + RB, :] = grp
    for r0 in range(0, rows, RB):
        at = slice(r0, r0 + RB)
        row = r0 + lax.broadcasted_iota(jnp.int32, (RB, 128), 0)
        chosen = jnp.where(row - first_ref[at, :] == lane, 1.0, 0.0)
        turn = lax.dot_general(
            chosen,
            rope_ref[...],
            (((1,), (0,)), ((), ())),
            precision=lax.Precision.HIGHEST,
            preferred_element_type=jnp.float32,
        )
        cos = turn[:, :128]
        sin = turn[:, 128:]
        for i, o_ref in enumerate(o_refs):
            flip = where_ref[1] > 0
            for n, ref in enumerate((q_ref, k_ref)):
                x = ref[at, i * HD : (i + 1) * HD]
                if heads == 2:
                    x = jnp.where(flip, ref[at, (1 - i) * HD : (2 - i) * HD], x)
                y = x[:, :128].astype(jnp.float32)
                swapped = jnp.where(even, pltpu.roll(y, 127, 1), pltpu.roll(y, 1, 1))
                o_ref[n, at, 0:128] = (y * cos + swapped * sin).astype(jnp.bfloat16)
                o_ref[n, at, 128:HD] = x[:, 128:]
            v = v_ref[at, i * HD : (i + 1) * HD]
            if heads == 2:
                v = jnp.where(flip, v_ref[at, (1 - i) * HD : (2 - i) * HD], v)
            o_ref[2, at, :] = v


def prepare(where, tables, q, k, v):
    rows, feat = q.shape
    heads = feat // HD
    spans = len(tables)
    column = jax.ShapeDtypeStruct((spans * rows, 128), jnp.int32)
    return pl.pallas_call(
        functools.partial(prep_kernel, spans),
        out_shape=[column] * 2 + [jax.ShapeDtypeStruct((3, rows, HD), jnp.bfloat16)] * heads,
        in_specs=[SMEM] * (1 + spans) + [VMEM] * 4,
        out_specs=[VMEM] * (2 + heads),
        compiler_params=pltpu.CompilerParams(vmem_limit_bytes=4 << 20),
        name="prepare",
    )(where, *tables, q, k, v, rope_table())


def cut_kernel(where_ref, w_ref, own_ref, *rest):
    sends = rest[:-1]
    sems = rest[-1]
    z = where_ref[0]
    core = where_ref[1]
    side = where_ref[2]
    cols = own_ref.shape[1]
    high, width = sends[0].shape
    copies = []
    for m in range(1, 1 + len(sends)):
        at = lax.bitwise_xor(z, m) * cols + side * width
        copies.append(
            pltpu.make_async_copy(
                w_ref.at[
                    pl.ds(pl.multiple_of(core * high, high), high),
                    pl.ds(pl.multiple_of(at, width), width),
                ],
                sends[m - 1],
                sems.at[m],
            )
        )
    copies.append(
        pltpu.make_async_copy(
            w_ref.at[:, pl.ds(pl.multiple_of(z * cols, cols), cols)], own_ref, sems.at[0]
        )
    )
    for c in copies:
        c.start()
    for c in copies:
        c.wait()


def cut(where, w, tp_size):
    rows, cols = w.shape[0], w.shape[1] // tp_size
    return pl.pallas_call(
        cut_kernel,
        out_shape=[jax.ShapeDtypeStruct((rows, cols), w.dtype)]
        + [jax.ShapeDtypeStruct((rows // 2, cols // 2), w.dtype)] * (tp_size - 1),
        in_specs=[SMEM, pl.BlockSpec(memory_space=pl.ANY)],
        out_specs=[VMEM] * tp_size,
        scratch_shapes=[pltpu.SemaphoreType.DMA((tp_size,))],
        compiler_params=pltpu.CompilerParams(vmem_limit_bytes=1 << 20),
        name="cut",
    )(where, w)


def wide(x, width):
    return x if width == 128 else jnp.concatenate([x] * (width // 128), axis=1)


def score_kernel(nb, place_ref, first_ref, grp_ref, *rest):
    sufs = rest[:nb]
    pieces = rest[nb : nb + SLOTS]
    p_ref, near_ref, den_ref, sc = rest[nb + SLOTS :]
    half = 256
    for n in range(nb):
        rows = sufs[n].shape[1]
        for b in range(rows // RB):
            r0 = b * RB
            t0 = n * rows + r0
            buf = (t0 // RB) % 2
            q = sufs[n][0, r0 : r0 + RB, :]
            grp = wide(grp_ref[t0 : t0 + RB, :], half)
            for d in range(SLOTS):
                g = place_ref[d] // OWNERS
                o = place_ref[d] % OWNERS
                for j in range(BLK // half):
                    s = lax.dot_general(
                        q,
                        pieces[d][j * half : (j + 1) * half, :],
                        (((1,), (1,)), ((), ())),
                        preferred_element_type=jnp.float32,
                    )
                    at = pl.ds(pl.multiple_of(o * BLK + j * half, half), half)
                    sc[buf, :, at] = jnp.where(grp == g, s, sc[buf, :, at])
            lo = max(0, r0 - MOST)
            width = r0 + RB - lo
            local = lax.dot_general(
                q,
                sufs[n][1, lo : r0 + RB, :],
                (((1,), (1,)), ((), ())),
                preferred_element_type=jnp.float32,
            )
            row = r0 + lax.broadcasted_iota(jnp.int32, (RB, width), 0)
            key = lo + lax.broadcasted_iota(jnp.int32, (RB, width), 1)
            start = wide(first_ref[t0 : t0 + RB, :], width)
            local = jnp.where((key <= row) & (key >= start), local, NEG_FILL)
            top = jnp.max(local, axis=1, keepdims=True)
            whole = sc[buf, :, 0:half]
            for c0 in range(half, SEEN, half):
                whole = jnp.maximum(whole, sc[buf, :, c0 : c0 + half])
            top = jnp.maximum(top, jnp.max(whole, axis=1, keepdims=True))
            e = jnp.exp2((local - top) * FACTOR)
            den = jnp.sum(e, axis=1, keepdims=True)
            near_ref[t0 : t0 + RB, 0:width] = e.astype(jnp.bfloat16)
            total = None
            for c0 in range(0, SEEN, half):
                e = jnp.exp2((sc[buf, :, c0 : c0 + half] - top) * FACTOR)
                p_ref[t0 : t0 + RB, c0 : c0 + half] = e.astype(jnp.bfloat16)
                total = e if total is None else total + e
            den = den + jnp.sum(total, axis=1, keepdims=True)
            den_ref[t0 : t0 + RB, :] = jnp.broadcast_to(den, (RB, 128))


def score(place, first, grp, sufs, pieces):
    rows = sum(s.shape[1] for s in sufs)
    return pl.pallas_call(
        functools.partial(score_kernel, len(sufs)),
        out_shape=[
            jax.ShapeDtypeStruct((rows, SEEN), jnp.bfloat16),
            jax.ShapeDtypeStruct((rows, RB + MOST), jnp.bfloat16),
            jax.ShapeDtypeStruct((rows, 128), jnp.float32),
        ],
        in_specs=[SMEM] + [VMEM] * (2 + len(sufs) + SLOTS),
        out_specs=[VMEM] * 3,
        scratch_shapes=[pltpu.VMEM((2, RB, SEEN), jnp.float32)],
        compiler_params=pltpu.CompilerParams(vmem_limit_bytes=4 << 20),
        name="score",
    )(place, first, grp, *sufs, *pieces)


def mix_kernel(nb, col, place_ref, grp_ref, p_ref, near_ref, den_ref, *rest):
    sufs = rest[:nb]
    pieces = rest[nb : nb + SLOTS]
    outs = rest[nb + SLOTS :]
    width = outs[0].shape[1]
    for n in reversed(range(nb)):
        rows = outs[n].shape[0]
        for b in range(rows // RB):
            r0 = b * RB
            t0 = n * rows + r0
            grp = wide(grp_ref[t0 : t0 + RB, :], width)
            lo = max(0, r0 - MOST)
            acc = jnp.dot(
                near_ref[t0 : t0 + RB, 0 : r0 + RB - lo],
                sufs[n][2, lo : r0 + RB, col : col + width],
                preferred_element_type=jnp.float32,
            )
            for d in range(SLOTS):
                g = place_ref[d] // OWNERS
                o = place_ref[d] % OWNERS
                part = jnp.dot(
                    p_ref[t0 : t0 + RB, pl.ds(pl.multiple_of(o * BLK, BLK), BLK)],
                    pieces[d][...],
                    preferred_element_type=jnp.float32,
                )
                acc = acc + jnp.where(grp == g, part, 0.0)
            den = wide(den_ref[t0 : t0 + RB, :], width)
            outs[n][r0 : r0 + RB, :] = (acc / den).astype(jnp.bfloat16)


def mix(col, width, place, grp, scored, sufs, pieces):
    rows = sufs[0].shape[1]
    nb = len(sufs)
    return pl.pallas_call(
        functools.partial(mix_kernel, nb, col),
        out_shape=[jax.ShapeDtypeStruct((rows, width), jnp.bfloat16)] * nb,
        in_specs=[SMEM] + [VMEM] * (4 + nb + SLOTS),
        out_specs=[VMEM] * nb,
        compiler_params=pltpu.CompilerParams(vmem_limit_bytes=4 << 20),
        name="mix",
    )(place, grp, *scored, *sufs, *pieces)


def proj_kernel(where_ref, *refs):
    att = refs[:10]
    own = refs[10]
    far = refs[11:15]
    o_ref = refs[15]
    cols = o_ref.shape[1] // 2
    rows = o_ref.shape[0]
    core = where_ref[1]
    side = where_ref[2]
    tall = 256
    for r0 in range(0, rows, tall):
        for x in range(2):
            c0 = pl.multiple_of(lax.bitwise_xor(side, x) * cols, cols)
            acc = jnp.zeros((tall, cols), jnp.float32)
            for h in range(2):
                head = lax.bitwise_xor(core, h)
                for m in range(4):
                    a = att[h * 5 + m][r0 : r0 + tall, :]
                    if m == 3:
                        a = a + att[h * 5 + 4][r0 : r0 + tall, :]
                    if m == 0:
                        w = own[pl.ds(pl.multiple_of(head * HD, HD), HD), pl.ds(c0, cols)]
                    else:
                        w = far[2 * h + x][m - 1]
                    acc = acc + jnp.dot(a, w, preferred_element_type=jnp.float32)
            o_ref[r0 : r0 + tall, pl.ds(c0, cols)] = acc.astype(jnp.bfloat16)


def project(where, att, own, far):
    rows = att[0].shape[0]
    cols = own.shape[1]
    return pl.pallas_call(
        proj_kernel,
        out_shape=jax.ShapeDtypeStruct((rows, cols), jnp.bfloat16),
        in_specs=[SMEM] + [VMEM] * (len(att) + 1 + len(far)),
        out_specs=VMEM,
        compiler_params=pltpu.CompilerParams(vmem_limit_bytes=6 << 20),
        name="project",
    )(where, *att, own, *far)


def swap(x, axis, mask, size):
    return lax.ppermute(x, axis, [(i, i ^ mask) for i in range(size)])


def after(x, *deps):
    return lax.optimization_barrier((x,) + deps)[0]


over_x = functools.partial(swap, axis="req", mask=2, size=8)
over_y = functools.partial(swap, axis="req", mask=4, size=8)
over_core = functools.partial(swap, axis="req", mask=1, size=8)


def split_heads(suffix_heads, prefix_cache, lengths, groups, owners, out_weight):
    me = lax.axis_index("req")
    z = lax.axis_index("tp")
    core = me & 1
    side = (me >> 1) & 1
    where = jnp.stack([z, core, side]).astype(jnp.int32)
    place = jnp.sum(
        jnp.where(
            owners[None] == (me ^ jnp.arange(SLOTS, dtype=jnp.int32))[:, None, None],
            jnp.arange(SLOTS, dtype=jnp.int32).reshape(1, GROUPS, OWNERS),
            0,
        ),
        axis=(1, 2),
    ).astype(jnp.int32)
    tp_size = 4
    first_head = core == 0

    k = prefix_cache[:, 0]
    k_own = jnp.where(first_head, k[:, :HD], k[:, HD:])
    k_other = jnp.where(first_head, k[:, HD:], k[:, :HD])
    k_pair = over_core(k_other)
    ax = over_x(k_own)
    ay = over_y(k_own)
    bx = over_x(k_pair)
    by = over_y(k_pair)

    table = jnp.concatenate([lengths, groups], axis=0)
    table_pair = over_core(table)
    first, grp, mine, other = prepare(
        where, (table, table_pair), suffix_heads[:, 0], suffix_heads[:, 1], suffix_heads[:, 2]
    )
    axy = over_y(after(ax, mine))
    bxy = over_x(after(by, mine))
    sufs = [mine, over_core(other)]
    k_pieces = [k_own, k_pair, ax, bx, ay, by, axy, bxy]

    v = after(prefix_cache, k_own)[:, 1]
    v_own = jnp.where(first_head, v[:, :HD], v[:, HD:])
    v_other = jnp.where(first_head, v[:, HD:], v[:, :HD])
    v_pair = over_core(v_other)
    v_own, v_pair = lax.optimization_barrier((v_own, v_pair, ay, bx, axy, bxy))[:2]
    vax = over_x(v_own)
    vay = over_y(v_own)
    vbx = over_x(v_pair)
    vby = over_y(v_pair)

    w_own, *sends = cut(where, out_weight, tp_size)
    w_far = jnp.stack([swap(sends[m - 1], "tp", m, tp_size) for m in range(1, tp_size)])

    vaxy = over_y(after(vax, w_far))
    vbxy = over_x(after(vby, w_far))
    v_pieces = [v_own, v_pair, vax, vbx, vay, vby, vaxy, vbxy]

    w_x = over_x(after(w_far, vay, vbx, vaxy, vbxy))
    w_core = over_core(after(w_far, vay, vbx, vaxy, vbxy))
    w_core_x = over_core(w_x)

    scored = score(place, first, grp, sufs, k_pieces)
    own, pair = mix(0, HD, place, grp, scored, sufs, v_pieces)
    back = over_core(pair)
    att = []
    for a in (own, back):
        two = swap(a, "tp", 2, tp_size)
        three = lax.ppermute(a, "tp", [(1, 2), (2, 1)])
        one = swap(a, "tp", 1, tp_size)
        forward = lax.ppermute(two, "tp", [(2, 3), (1, 0)])
        att += [a, one, two, three, forward]
    return project(where, att, w_own, [w_far, w_x, w_core, w_core_x])


def whole_heads(suffix_heads, prefix_cache, lengths, groups, owners, out_weight):
    heads = suffix_heads.shape[2] // HD
    received = [
        from_root(prefix_cache, "req", owners[i // OWNERS, i % OWNERS]) for i in range(SLOTS)
    ]
    place = jnp.arange(SLOTS, dtype=jnp.int32)
    first, grp, *sufs = prepare(
        jnp.zeros((3,), jnp.int32),
        (jnp.concatenate([lengths, groups], axis=0),),
        suffix_heads[:, 0],
        suffix_heads[:, 1],
        suffix_heads[:, 2],
    )
    attended = []
    for h in range(heads):
        keys = [s[:, 0, h * HD : (h + 1) * HD] for s in received]
        values = [s[:, 1, h * HD : (h + 1) * HD] for s in received]
        scored = score(place, first, grp, [sufs[h]], keys)
        attended += mix(0, HD, place, grp, scored, [sufs[h]], values)
    partial_out = jnp.dot(
        jnp.concatenate(attended, axis=1), out_weight, preferred_element_type=jnp.float32
    )
    return lax.psum_scatter(partial_out.astype(jnp.bfloat16), "tp", scatter_dimension=1, tiled=True)


def per_device(req_size, tp_size, *args):
    if req_size == 8 and tp_size == 4 and args[0].shape[2] == 2 * HD:
        return split_heads(*args)
    return whole_heads(*args)


def solution(mesh):
    placed = (
        P("req", None, "tp"),
        P("req", None, "tp"),
        P("req", None),
        P("req", None),
        P(),
        P("tp", None),
    )
    return jax.shard_map(
        functools.partial(per_device, mesh.shape["req"], mesh.shape["tp"]),
        mesh=mesh,
        in_specs=placed,
        out_specs=P("req", "tp"),
        check_vma=False,
    )
```

```python
import functools
import jax
import jax.numpy as jnp
import numpy as np
from jax import lax
from jax.experimental import pallas as pl
from jax.experimental.pallas import tpu as pltpu
from jax.sharding import PartitionSpec as P

HD = 256
ROT = 64
BLK = 512
OWNERS = 2
GROUPS = 4
SLOTS = GROUPS * OWNERS
MOST = 128
SEEN = OWNERS * BLK

NEG_FILL = -1e30
ROPE_BASE = 10000.0
FACTOR = HD ** (-0.5) * 1.4426950408889634

RB = 128

VMEM = pl.BlockSpec(memory_space=pltpu.VMEM)
SMEM = pl.BlockSpec(memory_space=pltpu.SMEM)


def from_root(x, axis, root):
    mine = lax.axis_index(axis) == root
    return lax.psum(jnp.where(mine, x, jnp.zeros_like(x)), axis)


def rope_table():
    inverse = np.float32(ROPE_BASE) ** (-2.0 * np.arange(ROT // 2, dtype=np.float32) / ROT)
    inverse = np.concatenate([np.repeat(inverse, 2), np.zeros(128 - ROT)]).astype(np.float32)
    angles = np.arange(SEEN, SEEN + MOST, dtype=np.float32)[:, None] * inverse[None, :]
    angles = angles.astype(np.float64)
    sign = np.where(np.arange(128) % 2 == 0, -1.0, 1.0)
    table = np.concatenate([np.cos(angles), np.sin(angles) * sign[None, :]], axis=1)
    return jnp.asarray(table.astype(np.float32))


def prep_kernel(spans, where_ref, *refs):
    tables = refs[:spans]
    q_ref, k_ref, v_ref, rope_ref = refs[spans : spans + 4]
    first_ref, grp_ref = refs[spans + 4 : spans + 6]
    o_refs = refs[spans + 6 :]
    rows = q_ref.shape[0]
    heads = len(o_refs)
    lane = lax.broadcasted_iota(jnp.int32, (RB, 128), 1)
    even = (lane % 2) == 0
    for n in range(spans):
        requests = tables[n].shape[1]
        for r0 in range(0, rows, RB):
            row = r0 + lax.broadcasted_iota(jnp.int32, (RB, 128), 0)
            start = jnp.int32(0)
            first = jnp.zeros((RB, 128), jnp.int32)
            grp = jnp.zeros((RB, 128), jnp.int32) + tables[n][1, 0]
            for r in range(1, requests):
                start = start + tables[n][0, r - 1]
                later = row >= start
                first = jnp.where(later, start, first)
                grp = jnp.where(later, tables[n][1, r], grp)
            first_ref[n * rows + r0 : n * rows + r0 + RB, :] = first
            grp_ref[n * rows + r0 : n * rows + r0 + RB, :] = grp
    for r0 in range(0, rows, RB):
        at = slice(r0, r0 + RB)
        row = r0 + lax.broadcasted_iota(jnp.int32, (RB, 128), 0)
        chosen = jnp.where(row - first_ref[at, :] == lane, 1.0, 0.0)
        turn = lax.dot_general(
            chosen,
            rope_ref[...],
            (((1,), (0,)), ((), ())),
            precision=lax.Precision.HIGHEST,
            preferred_element_type=jnp.float32,
        )
        cos = turn[:, :128]
        sin = turn[:, 128:]
        for i, o_ref in enumerate(o_refs):
            flip = where_ref[1] > 0
            for n, ref in enumerate((q_ref, k_ref)):
                x = ref[at, i * HD : (i + 1) * HD]
                if heads == 2:
                    x = jnp.where(flip, ref[at, (1 - i) * HD : (2 - i) * HD], x)
                y = x[:, :128].astype(jnp.float32)
                swapped = jnp.where(even, pltpu.roll(y, 127, 1), pltpu.roll(y, 1, 1))
                o_ref[n, at, 0:128] = (y * cos + swapped * sin).astype(jnp.bfloat16)
                o_ref[n, at, 128:HD] = x[:, 128:]
            v = v_ref[at, i * HD : (i + 1) * HD]
            if heads == 2:
                v = jnp.where(flip, v_ref[at, (1 - i) * HD : (2 - i) * HD], v)
            o_ref[2, at, :] = v


def prepare(where, tables, q, k, v):
    rows, feat = q.shape
    heads = feat // HD
    spans = len(tables)
    column = jax.ShapeDtypeStruct((spans * rows, 128), jnp.int32)
    return pl.pallas_call(
        functools.partial(prep_kernel, spans),
        out_shape=[column] * 2 + [jax.ShapeDtypeStruct((3, rows, HD), jnp.bfloat16)] * heads,
        in_specs=[SMEM] * (1 + spans) + [VMEM] * 4,
        out_specs=[VMEM] * (2 + heads),
        compiler_params=pltpu.CompilerParams(vmem_limit_bytes=4 << 20),
        name="prepare",
    )(where, *tables, q, k, v, rope_table())


def wide(x, width):
    return x if width == 128 else jnp.concatenate([x] * (width // 128), axis=1)


def flatten(refs, counts):
    return [ref.at[j] for ref, count in zip(refs, counts) for j in range(count)]


def score_kernel(nb, counts, place_ref, first_ref, grp_ref, *rest):
    sufs = rest[:nb]
    n_pieces = len(counts)
    pieces = flatten(rest[nb : nb + n_pieces], counts)
    p_ref, near_ref, den_ref, sc = rest[nb + n_pieces :]
    half = 256
    for n in range(nb):
        rows = sufs[n].shape[1]
        for b in range(rows // RB):
            r0 = b * RB
            t0 = n * rows + r0
            buf = (t0 // RB) % 2
            q = sufs[n][0, r0 : r0 + RB, :]
            grp = wide(grp_ref[t0 : t0 + RB, :], half)
            for d in range(SLOTS):
                g = place_ref[d] // OWNERS
                o = place_ref[d] % OWNERS
                for j in range(BLK // half):
                    s = lax.dot_general(
                        q,
                        pieces[d][j * half : (j + 1) * half, :],
                        (((1,), (1,)), ((), ())),
                        preferred_element_type=jnp.float32,
                    )
                    at = pl.ds(pl.multiple_of(o * BLK + j * half, half), half)
                    sc[buf, :, at] = jnp.where(grp == g, s, sc[buf, :, at])
            lo = max(0, r0 - MOST)
            width = r0 + RB - lo
            local = lax.dot_general(
                q,
                sufs[n][1, lo : r0 + RB, :],
                (((1,), (1,)), ((), ())),
                preferred_element_type=jnp.float32,
            )
            row = r0 + lax.broadcasted_iota(jnp.int32, (RB, width), 0)
            key = lo + lax.broadcasted_iota(jnp.int32, (RB, width), 1)
            start = wide(first_ref[t0 : t0 + RB, :], width)
            local = jnp.where((key <= row) & (key >= start), local, NEG_FILL)
            top = jnp.max(local, axis=1, keepdims=True)
            whole = sc[buf, :, 0:half]
            for c0 in range(half, SEEN, half):
                whole = jnp.maximum(whole, sc[buf, :, c0 : c0 + half])
            top = jnp.maximum(top, jnp.max(whole, axis=1, keepdims=True))
            e = jnp.exp2((local - top) * FACTOR)
            den = jnp.sum(e, axis=1, keepdims=True)
            near_ref[t0 : t0 + RB, 0:width] = e.astype(jnp.bfloat16)
            total = None
            for c0 in range(0, SEEN, half):
                e = jnp.exp2((sc[buf, :, c0 : c0 + half] - top) * FACTOR)
                p_ref[t0 : t0 + RB, c0 : c0 + half] = e.astype(jnp.bfloat16)
                total = e if total is None else total + e
            den = den + jnp.sum(total, axis=1, keepdims=True)
            den_ref[t0 : t0 + RB, :] = jnp.broadcast_to(den, (RB, 128))


def score(place, first, grp, sufs, pieces):
    rows = sum(s.shape[1] for s in sufs)
    return pl.pallas_call(
        functools.partial(score_kernel, len(sufs), tuple(p.shape[0] for p in pieces)),
        out_shape=[
            jax.ShapeDtypeStruct((rows, SEEN), jnp.bfloat16),
            jax.ShapeDtypeStruct((rows, RB + MOST), jnp.bfloat16),
            jax.ShapeDtypeStruct((rows, 128), jnp.float32),
        ],
        in_specs=[SMEM] + [VMEM] * (2 + len(sufs) + len(pieces)),
        out_specs=[VMEM] * 3,
        scratch_shapes=[pltpu.VMEM((2, RB, SEEN), jnp.float32)],
        compiler_params=pltpu.CompilerParams(vmem_limit_bytes=4 << 20),
        name="score",
    )(place, first, grp, *sufs, *pieces)


def mix_kernel(nb, counts, col, place_ref, grp_ref, p_ref, near_ref, den_ref, *rest):
    sufs = rest[:nb]
    n_pieces = len(counts)
    pieces = flatten(rest[nb : nb + n_pieces], counts)
    outs = rest[nb + n_pieces :]
    width = outs[0].shape[1]
    for n in reversed(range(nb)):
        rows = outs[n].shape[0]
        for b in range(rows // RB):
            r0 = b * RB
            t0 = n * rows + r0
            grp = wide(grp_ref[t0 : t0 + RB, :], width)
            lo = max(0, r0 - MOST)
            acc = jnp.dot(
                near_ref[t0 : t0 + RB, 0 : r0 + RB - lo],
                sufs[n][2, lo : r0 + RB, col : col + width],
                preferred_element_type=jnp.float32,
            )
            for d in range(SLOTS):
                g = place_ref[d] // OWNERS
                o = place_ref[d] % OWNERS
                part = jnp.dot(
                    p_ref[t0 : t0 + RB, pl.ds(pl.multiple_of(o * BLK, BLK), BLK)],
                    pieces[d][...],
                    preferred_element_type=jnp.float32,
                )
                acc = acc + jnp.where(grp == g, part, 0.0)
            den = wide(den_ref[t0 : t0 + RB, :], width)
            outs[n][r0 : r0 + RB, :] = (acc / den).astype(jnp.bfloat16)


def mix(col, width, place, grp, scored, sufs, pieces):
    rows = sufs[0].shape[1]
    nb = len(sufs)
    return pl.pallas_call(
        functools.partial(mix_kernel, nb, tuple(p.shape[0] for p in pieces), col),
        out_shape=[jax.ShapeDtypeStruct((rows, width), jnp.bfloat16)] * nb,
        in_specs=[SMEM] + [VMEM] * (4 + nb + len(pieces)),
        out_specs=[VMEM] * nb,
        compiler_params=pltpu.CompilerParams(vmem_limit_bytes=4 << 20),
        name="mix",
    )(place, grp, *scored, *sufs, *pieces)


def proj_kernel(where_ref, *refs):
    att = refs[:10]
    own = refs[10]
    far = refs[11:15]
    o_ref = refs[15]
    cols = o_ref.shape[1] // 2
    rows = o_ref.shape[0]
    core = where_ref[1]
    side = where_ref[2]
    tall = 256
    for r0 in range(0, rows, tall):
        for x in range(2):
            c0 = pl.multiple_of(lax.bitwise_xor(side, x) * cols, cols)
            acc = jnp.zeros((tall, cols), jnp.float32)
            for h in range(2):
                head = lax.bitwise_xor(core, h)
                for m in range(4):
                    a = att[h * 5 + m][r0 : r0 + tall, :]
                    if m == 3:
                        a = a + att[h * 5 + 4][r0 : r0 + tall, :]
                    if m == 0:
                        w = own[pl.ds(pl.multiple_of(head * HD, HD), HD), pl.ds(c0, cols)]
                    else:
                        w = far[2 * h + x][m - 1]
                    acc = acc + jnp.dot(a, w, preferred_element_type=jnp.float32)
            o_ref[r0 : r0 + tall, pl.ds(c0, cols)] = acc.astype(jnp.bfloat16)


def project(where, att, own, far):
    rows = att[0].shape[0]
    cols = own.shape[1]
    return pl.pallas_call(
        proj_kernel,
        out_shape=jax.ShapeDtypeStruct((rows, cols), jnp.bfloat16),
        in_specs=[SMEM] + [VMEM] * (len(att) + 1 + len(far)),
        out_specs=VMEM,
        compiler_params=pltpu.CompilerParams(vmem_limit_bytes=6 << 20),
        name="project",
    )(where, *att, own, *far)


def swap(x, axis, mask, size):
    return lax.ppermute(x, axis, [(i, i ^ mask) for i in range(size)])


def after(x, *deps):
    return lax.optimization_barrier((x,) + deps)[0]


over_x = functools.partial(swap, axis="req", mask=2, size=8)
over_y = functools.partial(swap, axis="req", mask=4, size=8)
over_core = functools.partial(swap, axis="req", mask=1, size=8)


def split_heads(suffix_heads, prefix_cache, lengths, groups, owners, out_weight):
    me = lax.axis_index("req")
    z = lax.axis_index("tp")
    core = me & 1
    side = (me >> 1) & 1
    where = jnp.stack([z, core, side]).astype(jnp.int32)
    place = jnp.sum(
        jnp.where(
            owners[None] == (me ^ jnp.arange(SLOTS, dtype=jnp.int32))[:, None, None],
            jnp.arange(SLOTS, dtype=jnp.int32).reshape(1, GROUPS, OWNERS),
            0,
        ),
        axis=(1, 2),
    ).astype(jnp.int32)
    tp_size = 4
    first_head = core == 0

    cols = out_weight.shape[1] // tp_size
    z_u, core_u, side_u = (i.astype(jnp.uint32) for i in (z, core, side))
    starts = [core_u * HD, z_u * cols]
    starts += [(z_u ^ m) * cols + side_u * (cols // 2) for m in range(1, tp_size)]
    first_head, *starts = lax.optimization_barrier((first_head, *starts))
    sends = [
        lax.dynamic_slice(out_weight, (starts[0], starts[1 + m]), (HD, cols // 2))
        for m in range(1, tp_size)
    ]
    w_own = lax.dynamic_slice(
        out_weight, (jnp.zeros_like(starts[0]), starts[1]), (out_weight.shape[0], cols)
    )

    k = prefix_cache[:, 0]
    k_own = jnp.where(first_head, k[:, :HD], k[:, HD:])
    k_other = jnp.where(first_head, k[:, HD:], k[:, :HD])
    k_both = jnp.stack([k_own, over_core(k_other)])
    kx = over_x(k_both)
    ky = over_y(k_both)
    w_one, w_two = (swap(sends[m - 1], "tp", m, tp_size) for m in (1, 2))

    table = jnp.concatenate([lengths, groups], axis=0)
    table_pair = over_core(table)
    first, grp, mine, other = prepare(
        after(where, k_both), (table, table_pair), suffix_heads[:, 0], suffix_heads[:, 1], suffix_heads[:, 2]
    )
    sufs = [mine, over_core(other)]
    v = after(prefix_cache, k_both)[:, 1]
    v_own = jnp.where(first_head, v[:, :HD], v[:, HD:])
    v_other = jnp.where(first_head, v[:, HD:], v[:, :HD])
    v_both = jnp.stack([v_own, over_core(v_other)])

    kxy = over_y(after(kx[0:1], mine, v_both, w_own))
    kyx = over_x(after(ky[1:2], mine, v_both, w_own))
    v_both = after(v_both, kxy, kyx, w_one, w_two, sufs[1])
    vx = over_x(v_both)
    vy = over_y(v_both)
    w_three = swap(after(sends[2], w_two), "tp", 3, tp_size)
    scored = score(place, first, grp, sufs, (k_both, kx, ky, kxy, kyx))
    w_far = jnp.stack([after(w_one, scored[0]), w_two, w_three])
    w_core = over_core(w_far)
    vxy = over_y(after(vx[0:1], scored[0], w_far))
    vyx = over_x(after(vy[1:2], scored[0], w_far))
    own, pair = mix(0, HD, place, grp, scored, sufs, (v_both, vx, vy, vxy, vyx))
    w_x = over_x(after(w_far, vxy, vyx))
    w_core_x = over_core(w_x)

    back = over_core(pair)
    two_own = swap(own, "tp", 2, tp_size)
    two_back = swap(back, "tp", 2, tp_size)
    att = []
    for a, two in ((own, two_own), (back, two_back)):
        one = swap(a, "tp", 1, tp_size)
        three = lax.ppermute(after(a, two), "tp", [(1, 2), (2, 1)])
        forward = lax.ppermute(two, "tp", [(2, 3), (1, 0)])
        att += [a, one, two, three, forward]
    return project(where, att, w_own, [w_far, w_x, w_core, w_core_x])


def whole_heads(suffix_heads, prefix_cache, lengths, groups, owners, out_weight):
    heads = suffix_heads.shape[2] // HD
    received = [
        from_root(prefix_cache, "req", owners[i // OWNERS, i % OWNERS]) for i in range(SLOTS)
    ]
    place = jnp.arange(SLOTS, dtype=jnp.int32)
    first, grp, *sufs = prepare(
        jnp.zeros((3,), jnp.int32),
        (jnp.concatenate([lengths, groups], axis=0),),
        suffix_heads[:, 0],
        suffix_heads[:, 1],
        suffix_heads[:, 2],
    )
    attended = []
    for h in range(heads):
        keys = [s[None, :, 0, h * HD : (h + 1) * HD] for s in received]
        values = [s[None, :, 1, h * HD : (h + 1) * HD] for s in received]
        scored = score(place, first, grp, [sufs[h]], keys)
        attended += mix(0, HD, place, grp, scored, [sufs[h]], values)
    partial_out = jnp.dot(
        jnp.concatenate(attended, axis=1), out_weight, preferred_element_type=jnp.float32
    )
    return lax.psum_scatter(partial_out.astype(jnp.bfloat16), "tp", scatter_dimension=1, tiled=True)


def per_device(req_size, tp_size, *args):
    if req_size == 8 and tp_size == 4 and args[0].shape[2] == 2 * HD:
        return split_heads(*args)
    return whole_heads(*args)


def solution(mesh):
    placed = (
        P("req", None, "tp"),
        P("req", None, "tp"),
        P("req", None),
        P("req", None),
        P(),
        P("tp", None),
    )
    return jax.shard_map(
        functools.partial(per_device, mesh.shape["req"], mesh.shape["tp"]),
        mesh=mesh,
        in_specs=placed,
        out_specs=P("req", "tp"),
        check_vma=False,
    )
```

```python
import functools
import jax
import jax.numpy as jnp
import numpy as np
from jax import lax
from jax.experimental import pallas as pl
from jax.experimental.pallas import tpu as pltpu
from jax.sharding import PartitionSpec as P

HD = 256
ROT = 64
BLK = 512
OWNERS = 2
GROUPS = 4
SLOTS = GROUPS * OWNERS
MOST = 128
SEEN = OWNERS * BLK

NEG_FILL = -1e30
ROPE_BASE = 10000.0
FACTOR = HD ** (-0.5) * 1.4426950408889634

RB = 128

VMEM = pl.BlockSpec(memory_space=pltpu.VMEM)
SMEM = pl.BlockSpec(memory_space=pltpu.SMEM)


def from_root(x, axis, root):
    mine = lax.axis_index(axis) == root
    return lax.psum(jnp.where(mine, x, jnp.zeros_like(x)), axis)


def rope_table():
    inverse = np.float32(ROPE_BASE) ** (-2.0 * np.arange(ROT // 2, dtype=np.float32) / ROT)
    inverse = np.concatenate([np.repeat(inverse, 2), np.zeros(128 - ROT)]).astype(np.float32)
    angles = np.arange(SEEN, SEEN + MOST, dtype=np.float32)[:, None] * inverse[None, :]
    angles = angles.astype(np.float64)
    sign = np.where(np.arange(128) % 2 == 0, -1.0, 1.0)
    table = np.concatenate([np.cos(angles), np.sin(angles) * sign[None, :]], axis=1)
    return jnp.asarray(table.astype(np.float32))


def prep_kernel(table_ref, q_ref, k_ref, v_ref, rope_ref, first_ref, grp_ref, *o_refs):
    rows = q_ref.shape[0]
    requests = table_ref.shape[1]
    lane = lax.broadcasted_iota(jnp.int32, (RB, 128), 1)
    even = (lane % 2) == 0
    for r0 in range(0, rows, RB):
        at = slice(r0, r0 + RB)
        row = r0 + lax.broadcasted_iota(jnp.int32, (RB, 128), 0)
        start = jnp.int32(0)
        first = jnp.zeros((RB, 128), jnp.int32)
        grp = jnp.zeros((RB, 128), jnp.int32) + table_ref[1, 0]
        for r in range(1, requests):
            start = start + table_ref[0, r - 1]
            later = row >= start
            first = jnp.where(later, start, first)
            grp = jnp.where(later, table_ref[1, r], grp)
        first_ref[at, :] = first
        grp_ref[at, :] = grp
        chosen = jnp.where(row - first == lane, 1.0, 0.0)
        turn = lax.dot_general(
            chosen,
            rope_ref[...],
            (((1,), (0,)), ((), ())),
            precision=lax.Precision.HIGHEST,
            preferred_element_type=jnp.float32,
        )
        cos = turn[:, :128]
        sin = turn[:, 128:]
        for i, o_ref in enumerate(o_refs):
            c0 = i * HD
            for n, ref in enumerate((q_ref, k_ref)):
                y = ref[at, c0 : c0 + 128].astype(jnp.float32)
                swapped = jnp.where(even, pltpu.roll(y, 127, 1), pltpu.roll(y, 1, 1))
                o_ref[n, at, 0:128] = (y * cos + swapped * sin).astype(jnp.bfloat16)
                o_ref[n, at, 128:HD] = ref[at, c0 + 128 : c0 + HD]
            o_ref[2, at, :] = v_ref[at, c0 : c0 + HD]


def prepare(table, q, k, v):
    rows, feat = q.shape
    heads = feat // HD
    column = jax.ShapeDtypeStruct((rows, 128), jnp.int32)
    return pl.pallas_call(
        prep_kernel,
        out_shape=[column] * 2 + [jax.ShapeDtypeStruct((3, rows, HD), jnp.bfloat16)] * heads,
        in_specs=[SMEM] + [VMEM] * 4,
        out_specs=[VMEM] * (2 + heads),
        compiler_params=pltpu.CompilerParams(vmem_limit_bytes=4 << 20),
        name="prepare",
    )(table, q, k, v, rope_table())


def wide(x, width):
    return x if width == 128 else jnp.concatenate([x] * (width // 128), axis=1)


def attend_kernel(where_k, where_v, place_ref, first_ref, grp_ref, suf, *rest):
    o_ref, sc, p = rest[-3:]
    keys = [rest[i].at[j] for i, j in where_k]
    values = [rest[i].at[j] for i, j in where_v]
    half = 256
    for b in range(o_ref.shape[0] // RB):
        r0 = b * RB
        buf = b % 2
        at = slice(r0, r0 + RB)
        q = suf[0, at, :]
        grp = wide(grp_ref[at, :], half)
        for d in range(SLOTS):
            g = place_ref[d] // OWNERS
            o = place_ref[d] % OWNERS
            for j in range(BLK // half):
                s = lax.dot_general(
                    q,
                    keys[d][j * half : (j + 1) * half, :],
                    (((1,), (1,)), ((), ())),
                    preferred_element_type=jnp.float32,
                )
                c = pl.ds(pl.multiple_of(o * BLK + j * half, half), half)
                sc[buf, :, c] = jnp.where(grp == g, s, sc[buf, :, c])
        lo = max(0, r0 - MOST)
        width = r0 + RB - lo
        local = lax.dot_general(
            q,
            suf[1, lo : r0 + RB, :],
            (((1,), (1,)), ((), ())),
            preferred_element_type=jnp.float32,
        )
        row = r0 + lax.broadcasted_iota(jnp.int32, (RB, width), 0)
        key = lo + lax.broadcasted_iota(jnp.int32, (RB, width), 1)
        start = wide(first_ref[at, :], width)
        local = jnp.where((key <= row) & (key >= start), local, NEG_FILL)
        top = jnp.max(local, axis=1, keepdims=True)
        whole = sc[buf, :, 0:half]
        for c0 in range(half, SEEN, half):
            whole = jnp.maximum(whole, sc[buf, :, c0 : c0 + half])
        top = jnp.maximum(top, jnp.max(whole, axis=1, keepdims=True))
        e = jnp.exp2((local - top) * FACTOR)
        den = jnp.sum(e, axis=1, keepdims=True)
        acc = jnp.dot(
            e.astype(jnp.bfloat16), suf[2, lo : r0 + RB, :], preferred_element_type=jnp.float32
        )
        total = None
        for c0 in range(0, SEEN, half):
            e = jnp.exp2((sc[buf, :, c0 : c0 + half] - top) * FACTOR)
            p[buf, :, c0 : c0 + half] = e.astype(jnp.bfloat16)
            total = e if total is None else total + e
        den = den + jnp.sum(total, axis=1, keepdims=True)
        for d in range(SLOTS):
            g = place_ref[d] // OWNERS
            o = place_ref[d] % OWNERS
            part = jnp.dot(
                p[buf, :, pl.ds(pl.multiple_of(o * BLK, BLK), BLK)],
                values[d][...],
                preferred_element_type=jnp.float32,
            )
            acc = acc + jnp.where(grp == g, part, 0.0)
        o_ref[at, :] = (acc / den).astype(jnp.bfloat16)


def attend(place, first, grp, suf, pieces, where_k, where_v):
    rows = suf.shape[1]
    return pl.pallas_call(
        functools.partial(attend_kernel, where_k, where_v),
        out_shape=jax.ShapeDtypeStruct((rows, HD), jnp.bfloat16),
        in_specs=[SMEM] + [VMEM] * (3 + len(pieces)),
        out_specs=VMEM,
        scratch_shapes=[
            pltpu.VMEM((2, RB, SEEN), jnp.float32),
            pltpu.VMEM((2, RB, SEEN), jnp.bfloat16),
        ],
        compiler_params=pltpu.CompilerParams(vmem_limit_bytes=8 << 20),
        name="attend",
    )(place, first, grp, suf, *pieces)


def proj_kernel(head, where_ref, *refs):
    att = refs[:5]
    own = refs[5]
    far = refs[6:10]
    add_ref = refs[10] if len(refs) == 12 else None
    o_ref = refs[-1]
    cols = o_ref.shape[1] // 2
    rows = o_ref.shape[0]
    mine = where_ref[1] == head
    side = where_ref[2]
    tall = 256
    for x in range(2):
        c0 = pl.multiple_of(lax.bitwise_xor(side, x) * cols, cols)
        w = [own[head * HD : (head + 1) * HD, pl.ds(c0, cols)]]
        w += [jnp.where(mine, far[x][m], far[2 + x][m]) for m in range(3)]
        for r0 in range(0, rows, tall):
            at = slice(r0, r0 + tall)
            acc = jnp.dot(att[0][at, :], w[0], preferred_element_type=jnp.float32)
            for m in range(1, 4):
                a = att[m][at, :]
                if m == 3:
                    a = a + att[4][at, :]
                acc = acc + jnp.dot(a, w[m], preferred_element_type=jnp.float32)
            if add_ref is not None:
                acc = acc + add_ref[at, pl.ds(c0, cols)]
            o_ref[at, pl.ds(c0, cols)] = acc.astype(o_ref.dtype)


def project(head, where, att, own, far, add=None):
    rows = att[0].shape[0]
    cols = own.shape[1]
    extra = [] if add is None else [add]
    return pl.pallas_call(
        functools.partial(proj_kernel, head),
        out_shape=jax.ShapeDtypeStruct((rows, cols), jnp.float32 if add is None else jnp.bfloat16),
        in_specs=[SMEM] + [VMEM] * (len(att) + 1 + len(far) + len(extra)),
        out_specs=VMEM,
        compiler_params=pltpu.CompilerParams(vmem_limit_bytes=6 << 20),
        name="project",
    )(where, *att, own, *far, *extra)


def swap(x, axis, mask, size):
    return lax.ppermute(x, axis, [(i, i ^ mask) for i in range(size)])


def after(x, *deps):
    return lax.optimization_barrier((x,) + deps)[0]


over_x = functools.partial(swap, axis="req", mask=2, size=8)
over_y = functools.partial(swap, axis="req", mask=4, size=8)
over_core = functools.partial(swap, axis="req", mask=1, size=8)


def over_tp(a):
    two = swap(a, "tp", 2, 4)
    one = swap(a, "tp", 1, 4)
    three = lax.ppermute(after(a, two), "tp", [(1, 2), (2, 1)])
    forward = lax.ppermute(two, "tp", [(2, 3), (1, 0)])
    return [a, one, two, three, forward]


WHERE_K = ((0, 0), (5, 0), (1, 0), (6, 0), (2, 0), (7, 0), (3, 0), (8, 0))
WHERE_V = ((0, 1), (5, 1), (1, 1), (6, 1), (2, 1), (7, 1), (4, 0), (9, 0))


def split_heads(suffix_heads, prefix_cache, lengths, groups, owners, out_weight):
    me = lax.axis_index("req")
    z = lax.axis_index("tp")
    core = me & 1
    side = (me >> 1) & 1
    where = jnp.stack([z, core, side]).astype(jnp.int32)
    place = jnp.sum(
        jnp.where(
            owners[None] == (me ^ jnp.arange(SLOTS, dtype=jnp.int32))[:, None, None],
            jnp.arange(SLOTS, dtype=jnp.int32).reshape(1, GROUPS, OWNERS),
            0,
        ),
        axis=(1, 2),
    ).astype(jnp.int32)
    tp_size = 4

    cols = out_weight.shape[1] // tp_size
    z_u, core_u, side_u = (i.astype(jnp.uint32) for i in (z, core, side))
    starts = [core_u * HD, z_u * cols]
    starts += [(z_u ^ m) * cols + side_u * (cols // 2) for m in range(1, tp_size)]
    prefix = jnp.swapaxes(prefix_cache, 0, 1)
    sends = [
        lax.dynamic_slice(out_weight, (starts[0], starts[1 + m]), (HD, cols // 2))
        for m in range(1, tp_size)
    ]
    w_own = lax.dynamic_slice(
        out_weight, (jnp.zeros_like(starts[0]), starts[1]), (out_weight.shape[0], cols)
    )

    kv0 = prefix[:, :, :HD]
    kvx0 = over_x(kv0)
    kvy0 = over_y(kv0)
    w_one, w_two = (swap(sends[m - 1], "tp", m, tp_size) for m in (1, 2))
    table = jnp.concatenate([lengths, groups], axis=0)
    first, grp, suf0, suf1 = prepare(
        after(table, kv0), suffix_heads[:, 0], suffix_heads[:, 1], suffix_heads[:, 2]
    )
    kxy0 = over_y(after(kvx0[0:1], suf0, w_own))
    vyx0 = over_x(after(kvy0[1:2], suf0, w_own))
    kv1 = after(prefix[:, :, HD:], kvx0, kvy0)
    kvx1 = over_x(kv1)
    kvy1 = over_y(kv1)
    pieces0 = [kv0, kvx0, kvy0, kxy0, vyx0]
    pieces0 += [over_core(p) for p in pieces0]
    att0 = attend(after(place, w_one, w_two), first, grp, suf0, pieces0, WHERE_K, WHERE_V)

    w_three = swap(after(sends[2], w_two), "tp", 3, tp_size)
    kxy1 = over_y(after(kvx1[0:1], att0, w_three))
    vyx1 = over_x(after(kvy1[1:2], att0, w_three))
    pieces1 = [kv1, kvx1, kvy1, kxy1, vyx1]
    pieces1 += [over_core(p) for p in pieces1]
    spread0 = over_tp(att0)
    att1 = attend(after(place, spread0[2]), first, grp, suf1, pieces1, WHERE_K, WHERE_V)

    w_far = jnp.stack([after(w_one, att0), w_two, w_three])
    w_core = over_core(w_far)
    w_x = over_x(after(w_far, kxy1, vyx1))
    spread1 = over_tp(after(att1, *spread0[1:]))
    w_core_x = over_core(after(w_x, att1))
    far = [w_far, w_x, w_core, w_core_x]
    half = project(0, where, spread0, w_own, far)
    return project(1, where, spread1, w_own, far, half)


def whole_heads(suffix_heads, prefix_cache, lengths, groups, owners, out_weight):
    heads = suffix_heads.shape[2] // HD
    received = [
        from_root(prefix_cache, "req", owners[i // OWNERS, i % OWNERS]) for i in range(SLOTS)
    ]
    place = jnp.arange(SLOTS, dtype=jnp.int32)
    first, grp, *sufs = prepare(
        jnp.concatenate([lengths, groups], axis=0),
        suffix_heads[:, 0],
        suffix_heads[:, 1],
        suffix_heads[:, 2],
    )
    where_k = tuple((d, 0) for d in range(SLOTS))
    where_v = tuple((d, 1) for d in range(SLOTS))
    attended = []
    for h in range(heads):
        pieces = [jnp.swapaxes(s[:, :, h * HD : (h + 1) * HD], 0, 1) for s in received]
        attended.append(attend(place, first, grp, sufs[h], pieces, where_k, where_v))
    partial_out = jnp.dot(
        jnp.concatenate(attended, axis=1), out_weight, preferred_element_type=jnp.float32
    )
    return lax.psum_scatter(partial_out.astype(jnp.bfloat16), "tp", scatter_dimension=1, tiled=True)


def per_device(req_size, tp_size, *args):
    if req_size == 8 and tp_size == 4 and args[0].shape[2] == 2 * HD:
        return split_heads(*args)
    return whole_heads(*args)


def solution(mesh):
    placed = (
        P("req", None, "tp"),
        P("req", None, "tp"),
        P("req", None),
        P("req", None),
        P(),
        P("tp", None),
    )
    return jax.shard_map(
        functools.partial(per_device, mesh.shape["req"], mesh.shape["tp"]),
        mesh=mesh,
        in_specs=placed,
        out_specs=P("req", "tp"),
        check_vma=False,
    )
```

```python
import functools
import jax
import jax.numpy as jnp
import numpy as np
from jax import lax
from jax.experimental import pallas as pl
from jax.experimental.pallas import tpu as pltpu
from jax.sharding import PartitionSpec as P

HD = 256
ROT = 64
BLK = 512
OWNERS = 2
GROUPS = 4
SLOTS = GROUPS * OWNERS
MOST = 128
SEEN = OWNERS * BLK

NEG_FILL = -1e30
ROPE_BASE = 10000.0
FACTOR = HD ** (-0.5) * 1.4426950408889634

RB = 128

VMEM = pl.BlockSpec(memory_space=pltpu.VMEM)
SMEM = pl.BlockSpec(memory_space=pltpu.SMEM)


def from_root(x, axis, root):
    mine = lax.axis_index(axis) == root
    return lax.psum(jnp.where(mine, x, jnp.zeros_like(x)), axis)


def rope_table():
    inverse = np.float32(ROPE_BASE) ** (-2.0 * np.arange(ROT // 2, dtype=np.float32) / ROT)
    inverse = np.concatenate([np.repeat(inverse, 2), np.zeros(128 - ROT)]).astype(np.float32)
    angles = np.arange(SEEN, SEEN + MOST, dtype=np.float32)[:, None] * inverse[None, :]
    angles = angles.astype(np.float64)
    sign = np.where(np.arange(128) % 2 == 0, -1.0, 1.0)
    table = np.concatenate([np.cos(angles), np.sin(angles) * sign[None, :]], axis=1)
    return jnp.asarray(table.astype(np.float32))


def prep_kernel(table_ref, q_ref, k_ref, v_ref, rope_ref, first_ref, grp_ref, *o_refs):
    rows = q_ref.shape[0]
    requests = table_ref.shape[1]
    lane = lax.broadcasted_iota(jnp.int32, (RB, 128), 1)
    even = (lane % 2) == 0
    for r0 in range(0, rows, RB):
        at = slice(r0, r0 + RB)
        row = r0 + lax.broadcasted_iota(jnp.int32, (RB, 128), 0)
        start = jnp.int32(0)
        first = jnp.zeros((RB, 128), jnp.int32)
        grp = jnp.zeros((RB, 128), jnp.int32) + table_ref[1, 0]
        for r in range(1, requests):
            start = start + table_ref[0, r - 1]
            later = row >= start
            first = jnp.where(later, start, first)
            grp = jnp.where(later, table_ref[1, r], grp)
        first_ref[at, :] = first
        grp_ref[at, :] = grp
        chosen = jnp.where(row - first == lane, 1.0, 0.0)
        turn = lax.dot_general(
            chosen,
            rope_ref[...],
            (((1,), (0,)), ((), ())),
            precision=lax.Precision.HIGHEST,
            preferred_element_type=jnp.float32,
        )
        cos = turn[:, :128]
        sin = turn[:, 128:]
        for i, o_ref in enumerate(o_refs):
            c0 = i * HD
            for n, ref in enumerate((q_ref, k_ref)):
                y = ref[at, c0 : c0 + 128].astype(jnp.float32)
                swapped = jnp.where(even, pltpu.roll(y, 127, 1), pltpu.roll(y, 1, 1))
                o_ref[n, at, 0:128] = (y * cos + swapped * sin).astype(jnp.bfloat16)
                o_ref[n, at, 128:HD] = ref[at, c0 + 128 : c0 + HD]
            o_ref[2, at, :] = v_ref[at, c0 : c0 + HD]


def prepare(table, q, k, v):
    rows, feat = q.shape
    heads = feat // HD
    column = jax.ShapeDtypeStruct((rows, 128), jnp.int32)
    return pl.pallas_call(
        prep_kernel,
        out_shape=[column] * 2 + [jax.ShapeDtypeStruct((3, rows, HD), jnp.bfloat16)] * heads,
        in_specs=[SMEM] + [VMEM] * 4,
        out_specs=[VMEM] * (2 + heads),
        compiler_params=pltpu.CompilerParams(vmem_limit_bytes=4 << 20),
        name="prepare",
    )(table, q, k, v, rope_table())


def wide(x, width):
    return x if width == 128 else jnp.concatenate([x] * (width // 128), axis=1)


def attend_kernel(where_k, where_v, place_ref, first_ref, grp_ref, suf, *rest):
    o_ref, sc, p = rest[-3:]
    keys = [rest[i].at[j] for i, j in where_k]
    values = [rest[i].at[j] for i, j in where_v]
    half = 256
    for b in range(o_ref.shape[0] // RB):
        r0 = b * RB
        buf = b % 2
        at = slice(r0, r0 + RB)
        q = suf[0, at, :]
        grp = wide(grp_ref[at, :], half)
        for d in range(SLOTS):
            g = place_ref[d] // OWNERS
            o = place_ref[d] % OWNERS
            for j in range(BLK // half):
                s = lax.dot_general(
                    q,
                    keys[d][j * half : (j + 1) * half, :],
                    (((1,), (1,)), ((), ())),
                    preferred_element_type=jnp.float32,
                )
                c = pl.ds(pl.multiple_of(o * BLK + j * half, half), half)
                sc[buf, :, c] = jnp.where(grp == g, s, sc[buf, :, c])
        lo = max(0, r0 - MOST)
        width = r0 + RB - lo
        local = lax.dot_general(
            q,
            suf[1, lo : r0 + RB, :],
            (((1,), (1,)), ((), ())),
            preferred_element_type=jnp.float32,
        )
        row = r0 + lax.broadcasted_iota(jnp.int32, (RB, width), 0)
        key = lo + lax.broadcasted_iota(jnp.int32, (RB, width), 1)
        start = wide(first_ref[at, :], width)
        local = jnp.where((key <= row) & (key >= start), local, NEG_FILL)
        top = jnp.max(local, axis=1, keepdims=True)
        whole = sc[buf, :, 0:half]
        for c0 in range(half, SEEN, half):
            whole = jnp.maximum(whole, sc[buf, :, c0 : c0 + half])
        top = jnp.maximum(top, jnp.max(whole, axis=1, keepdims=True))
        e = jnp.exp2((local - top) * FACTOR)
        den = jnp.sum(e, axis=1, keepdims=True)
        acc = jnp.dot(
            e.astype(jnp.bfloat16), suf[2, lo : r0 + RB, :], preferred_element_type=jnp.float32
        )
        total = None
        for c0 in range(0, SEEN, half):
            e = jnp.exp2((sc[buf, :, c0 : c0 + half] - top) * FACTOR)
            p[buf, :, c0 : c0 + half] = e.astype(jnp.bfloat16)
            total = e if total is None else total + e
        den = den + jnp.sum(total, axis=1, keepdims=True)
        for d in range(SLOTS):
            g = place_ref[d] // OWNERS
            o = place_ref[d] % OWNERS
            part = jnp.dot(
                p[buf, :, pl.ds(pl.multiple_of(o * BLK, BLK), BLK)],
                values[d][...],
                preferred_element_type=jnp.float32,
            )
            acc = acc + jnp.where(grp == g, part, 0.0)
        o_ref[at, :] = (acc / den).astype(jnp.bfloat16)


def attend(place, first, grp, suf, pieces, where_k, where_v):
    rows = suf.shape[1]
    return pl.pallas_call(
        functools.partial(attend_kernel, where_k, where_v),
        out_shape=jax.ShapeDtypeStruct((rows, HD), jnp.bfloat16),
        in_specs=[SMEM] + [VMEM] * (3 + len(pieces)),
        out_specs=VMEM,
        scratch_shapes=[
            pltpu.VMEM((2, RB, SEEN), jnp.float32),
            pltpu.VMEM((2, RB, SEEN), jnp.bfloat16),
        ],
        compiler_params=pltpu.CompilerParams(vmem_limit_bytes=8 << 20),
        name="attend",
    )(place, first, grp, suf, *pieces)


def proj_kernel(head, where_ref, *refs):
    att = refs[:5]
    own = refs[5]
    far = refs[6:10]
    add_ref = refs[10] if len(refs) == 12 else None
    o_ref = refs[-1]
    cols = o_ref.shape[1] // 2
    rows = o_ref.shape[0]
    mine = where_ref[1] == head
    side = where_ref[2]
    tall = 256
    for x in range(2):
        c0 = pl.multiple_of(lax.bitwise_xor(side, x) * cols, cols)
        w = [own[head * HD : (head + 1) * HD, pl.ds(c0, cols)]]
        w += [jnp.where(mine, far[x][m], far[2 + x][m]) for m in range(3)]
        for r0 in range(0, rows, tall):
            at = slice(r0, r0 + tall)
            acc = jnp.dot(att[0][at, :], w[0], preferred_element_type=jnp.float32)
            for m in range(1, 4):
                a = att[m][at, :]
                if m == 3:
                    a = a + att[4][at, :]
                acc = acc + jnp.dot(a, w[m], preferred_element_type=jnp.float32)
            if add_ref is not None:
                acc = acc + add_ref[at, pl.ds(c0, cols)]
            o_ref[at, pl.ds(c0, cols)] = acc.astype(o_ref.dtype)


def project(head, where, att, own, far, add=None):
    rows = att[0].shape[0]
    cols = own.shape[1]
    extra = [] if add is None else [add]
    return pl.pallas_call(
        functools.partial(proj_kernel, head),
        out_shape=jax.ShapeDtypeStruct((rows, cols), jnp.float32 if add is None else jnp.bfloat16),
        in_specs=[SMEM] + [VMEM] * (len(att) + 1 + len(far) + len(extra)),
        out_specs=VMEM,
        compiler_params=pltpu.CompilerParams(vmem_limit_bytes=6 << 20),
        name="project",
    )(where, *att, own, *far, *extra)


def swap(x, axis, mask, size):
    return lax.ppermute(x, axis, [(i, i ^ mask) for i in range(size)])


def after(x, *deps):
    return lax.optimization_barrier((x,) + deps)[0]


over_x = functools.partial(swap, axis="req", mask=2, size=8)
over_y = functools.partial(swap, axis="req", mask=4, size=8)
over_core = functools.partial(swap, axis="req", mask=1, size=8)


def over_tp(a):
    two = swap(a, "tp", 2, 4)
    one = swap(a, "tp", 1, 4)
    three = lax.ppermute(after(a, two), "tp", [(1, 2), (2, 1)])
    forward = lax.ppermute(two, "tp", [(2, 3), (1, 0)])
    return [a, one, two, three, forward]


WHERE_K = ((0, 0), (5, 0), (1, 0), (6, 0), (2, 0), (7, 0), (3, 0), (8, 0))
WHERE_V = ((0, 1), (5, 1), (1, 1), (6, 1), (2, 1), (7, 1), (4, 0), (9, 0))


def split_heads(suffix_heads, prefix_cache, lengths, groups, owners, out_weight):
    me = lax.axis_index("req")
    z = lax.axis_index("tp")
    core = me & 1
    side = (me >> 1) & 1
    where = jnp.stack([z, core, side]).astype(jnp.int32)
    place = jnp.sum(
        jnp.where(
            owners[None] == (me ^ jnp.arange(SLOTS, dtype=jnp.int32))[:, None, None],
            jnp.arange(SLOTS, dtype=jnp.int32).reshape(1, GROUPS, OWNERS),
            0,
        ),
        axis=(1, 2),
    ).astype(jnp.int32)
    tp_size = 4

    cols = out_weight.shape[1] // tp_size
    z_u, core_u, side_u = (i.astype(jnp.uint32) for i in (z, core, side))
    starts = [core_u * HD, z_u * cols]
    starts += [(z_u ^ m) * cols + side_u * (cols // 2) for m in range(1, tp_size)]
    prefix = jnp.swapaxes(prefix_cache, 0, 1)
    sends = [
        lax.dynamic_slice(out_weight, (starts[0], starts[1 + m]), (HD, cols // 2))
        for m in range(1, tp_size)
    ]
    w_own = lax.dynamic_slice(
        out_weight, (jnp.zeros_like(starts[0]), starts[1]), (out_weight.shape[0], cols)
    )

    kv0 = prefix[:, :, :HD]
    kvx0 = over_x(kv0)
    kvy0 = over_y(kv0)
    w_one, w_two = (swap(sends[m - 1], "tp", m, tp_size) for m in (1, 2))
    table = jnp.concatenate([lengths, groups], axis=0)
    kvc0 = over_core(kv0)
    first, grp, suf0, suf1 = prepare(
        after(table, kvc0), suffix_heads[:, 0], suffix_heads[:, 1], suffix_heads[:, 2]
    )
    kxy0 = over_y(after(kvx0[0:1], suf0, w_own, w_two))
    vyx0 = over_x(after(kvy0[1:2], suf0, w_own, w_two))
    kv1 = after(prefix[:, :, HD:], kxy0, vyx0)
    kvx1 = over_x(kv1)
    kvy1 = over_y(kv1)
    pieces0 = [kv0, kvx0, kvy0, kxy0, vyx0]
    pieces0 += [kvc0] + [over_core(after(p, w_one)) for p in pieces0[1:3]]
    pieces0 += [over_core(p) for p in pieces0[3:5]]
    att0 = attend(place, first, grp, suf0, pieces0, WHERE_K, WHERE_V)

    w_three = swap(after(sends[2], w_two), "tp", 3, tp_size)
    kxy1 = over_y(after(kvx1[0:1], att0, w_three))
    vyx1 = over_x(after(kvy1[1:2], att0, w_three))
    pieces1 = [kv1, kvx1, kvy1, kxy1, vyx1]
    spread0 = over_tp(att0)
    pieces1 += [over_core(after(p, spread0[2])) for p in pieces1]
    att1 = attend(place, first, grp, suf1, pieces1, WHERE_K, WHERE_V)

    w_far = jnp.stack([after(w_one, att0), w_two, w_three])
    w_core = over_core(w_far)
    w_x = over_x(after(w_far, kxy1, vyx1))
    spread1 = over_tp(after(att1, *spread0[1:]))
    w_core_x = over_core(after(w_x, att1))
    far = [w_far, w_x, w_core, w_core_x]
    half = project(0, where, spread0, w_own, far)
    return project(1, where, spread1, w_own, far, half)


def whole_heads(suffix_heads, prefix_cache, lengths, groups, owners, out_weight):
    heads = suffix_heads.shape[2] // HD
    received = [
        from_root(prefix_cache, "req", owners[i // OWNERS, i % OWNERS]) for i in range(SLOTS)
    ]
    place = jnp.arange(SLOTS, dtype=jnp.int32)
    first, grp, *sufs = prepare(
        jnp.concatenate([lengths, groups], axis=0),
        suffix_heads[:, 0],
        suffix_heads[:, 1],
        suffix_heads[:, 2],
    )
    where_k = tuple((d, 0) for d in range(SLOTS))
    where_v = tuple((d, 1) for d in range(SLOTS))
    attended = []
    for h in range(heads):
        pieces = [jnp.swapaxes(s[:, :, h * HD : (h + 1) * HD], 0, 1) for s in received]
        attended.append(attend(place, first, grp, sufs[h], pieces, where_k, where_v))
    partial_out = jnp.dot(
        jnp.concatenate(attended, axis=1), out_weight, preferred_element_type=jnp.float32
    )
    return lax.psum_scatter(partial_out.astype(jnp.bfloat16), "tp", scatter_dimension=1, tiled=True)


def per_device(req_size, tp_size, *args):
    if req_size == 8 and tp_size == 4 and args[0].shape[2] == 2 * HD:
        return split_heads(*args)
    return whole_heads(*args)


def solution(mesh):
    placed = (
        P("req", None, "tp"),
        P("req", None, "tp"),
        P("req", None),
        P("req", None),
        P(),
        P("tp", None),
    )
    return jax.shard_map(
        functools.partial(per_device, mesh.shape["req"], mesh.shape["tp"]),
        mesh=mesh,
        in_specs=placed,
        out_specs=P("req", "tp"),
        check_vma=False,
    )
```

```python
import functools
import jax
import jax.numpy as jnp
import numpy as np
from jax import lax
from jax.experimental import pallas as pl
from jax.experimental.pallas import tpu as pltpu
from jax.sharding import PartitionSpec as P

HD = 256
ROT = 64
BLK = 512
OWNERS = 2
GROUPS = 4
SLOTS = GROUPS * OWNERS
MOST = 128
SEEN = OWNERS * BLK

NEG_FILL = -1e30
ROPE_BASE = 10000.0
FACTOR = HD ** (-0.5) * 1.4426950408889634

RB = 128

VMEM = pl.BlockSpec(memory_space=pltpu.VMEM)
SMEM = pl.BlockSpec(memory_space=pltpu.SMEM)


def from_root(x, axis, root):
    mine = lax.axis_index(axis) == root
    return lax.psum(jnp.where(mine, x, jnp.zeros_like(x)), axis)


def rope_table():
    inverse = np.float32(ROPE_BASE) ** (-2.0 * np.arange(ROT // 2, dtype=np.float32) / ROT)
    inverse = np.concatenate([np.repeat(inverse, 2), np.zeros(128 - ROT)]).astype(np.float32)
    angles = np.arange(SEEN, SEEN + MOST, dtype=np.float32)[:, None] * inverse[None, :]
    angles = angles.astype(np.float64)
    sign = np.where(np.arange(128) % 2 == 0, -1.0, 1.0)
    table = np.concatenate([np.cos(angles), np.sin(angles) * sign[None, :]], axis=1)
    return jnp.asarray(table.astype(np.float32))


def prep_kernel(table_ref, q_ref, k_ref, v_ref, rope_ref, first_ref, grp_ref, *o_refs):
    rows = q_ref.shape[0]
    requests = table_ref.shape[1]
    lane = lax.broadcasted_iota(jnp.int32, (RB, 128), 1)
    even = (lane % 2) == 0
    for r0 in range(0, rows, RB):
        at = slice(r0, r0 + RB)
        row = r0 + lax.broadcasted_iota(jnp.int32, (RB, 128), 0)
        start = jnp.int32(0)
        first = jnp.zeros((RB, 128), jnp.int32)
        grp = jnp.zeros((RB, 128), jnp.int32) + table_ref[1, 0]
        for r in range(1, requests):
            start = start + table_ref[0, r - 1]
            later = row >= start
            first = jnp.where(later, start, first)
            grp = jnp.where(later, table_ref[1, r], grp)
        first_ref[at, :] = first
        grp_ref[at, :] = grp
        chosen = jnp.where(row - first == lane, 1.0, 0.0)
        turn = lax.dot_general(
            chosen,
            rope_ref[...],
            (((1,), (0,)), ((), ())),
            precision=lax.Precision.HIGHEST,
            preferred_element_type=jnp.float32,
        )
        cos = turn[:, :128]
        sin = turn[:, 128:]
        for i, o_ref in enumerate(o_refs):
            c0 = i * HD
            for n, ref in enumerate((q_ref, k_ref)):
                y = ref[at, c0 : c0 + 128].astype(jnp.float32)
                swapped = jnp.where(even, pltpu.roll(y, 127, 1), pltpu.roll(y, 1, 1))
                o_ref[n, at, 0:128] = (y * cos + swapped * sin).astype(jnp.bfloat16)
                o_ref[n, at, 128:HD] = ref[at, c0 + 128 : c0 + HD]
            o_ref[2, at, :] = v_ref[at, c0 : c0 + HD]


def prepare(table, q, k, v):
    rows, feat = q.shape
    heads = feat // HD
    column = jax.ShapeDtypeStruct((rows, 128), jnp.int32)
    return pl.pallas_call(
        prep_kernel,
        out_shape=[column] * 2 + [jax.ShapeDtypeStruct((3, rows, HD), jnp.bfloat16)] * heads,
        in_specs=[SMEM] + [VMEM] * 4,
        out_specs=[VMEM] * (2 + heads),
        compiler_params=pltpu.CompilerParams(vmem_limit_bytes=4 << 20),
        name="prepare",
    )(table, q, k, v, rope_table())


def wide(x, width):
    return x if width == 128 else jnp.concatenate([x] * (width // 128), axis=1)


def attend_kernel(where_k, where_v, place_ref, first_ref, grp_ref, suf, *rest):
    o_ref, sc, p = rest[-3:]
    keys = [rest[i].at[j] for i, j in where_k]
    values = [rest[i].at[j] for i, j in where_v]
    half = 256
    for b in range(o_ref.shape[0] // RB):
        r0 = b * RB
        buf = b % 2
        at = slice(r0, r0 + RB)
        q = suf[0, at, :]
        grp = wide(grp_ref[at, :], half)
        for d in range(SLOTS):
            g = place_ref[d] // OWNERS
            o = place_ref[d] % OWNERS
            for j in range(BLK // half):
                s = lax.dot_general(
                    q,
                    keys[d][j * half : (j + 1) * half, :],
                    (((1,), (1,)), ((), ())),
                    preferred_element_type=jnp.float32,
                )
                c = pl.ds(pl.multiple_of(o * BLK + j * half, half), half)
                sc[buf, :, c] = jnp.where(grp == g, s, sc[buf, :, c])
        lo = max(0, r0 - MOST)
        width = r0 + RB - lo
        local = lax.dot_general(
            q,
            suf[1, lo : r0 + RB, :],
            (((1,), (1,)), ((), ())),
            preferred_element_type=jnp.float32,
        )
        row = r0 + lax.broadcasted_iota(jnp.int32, (RB, width), 0)
        key = lo + lax.broadcasted_iota(jnp.int32, (RB, width), 1)
        start = wide(first_ref[at, :], width)
        local = jnp.where((key <= row) & (key >= start), local, NEG_FILL)
        top = jnp.max(local, axis=1, keepdims=True)
        whole = sc[buf, :, 0:half]
        for c0 in range(half, SEEN, half):
            whole = jnp.maximum(whole, sc[buf, :, c0 : c0 + half])
        top = jnp.maximum(top, jnp.max(whole, axis=1, keepdims=True))
        e = jnp.exp2((local - top) * FACTOR)
        den = jnp.sum(e, axis=1, keepdims=True)
        acc = jnp.dot(
            e.astype(jnp.bfloat16), suf[2, lo : r0 + RB, :], preferred_element_type=jnp.float32
        )
        total = None
        for c0 in range(0, SEEN, half):
            e = jnp.exp2((sc[buf, :, c0 : c0 + half] - top) * FACTOR)
            p[buf, :, c0 : c0 + half] = e.astype(jnp.bfloat16)
            total = e if total is None else total + e
        den = den + jnp.sum(total, axis=1, keepdims=True)
        for d in range(SLOTS):
            g = place_ref[d] // OWNERS
            o = place_ref[d] % OWNERS
            part = jnp.dot(
                p[buf, :, pl.ds(pl.multiple_of(o * BLK, BLK), BLK)],
                values[d][...],
                preferred_element_type=jnp.float32,
            )
            acc = acc + jnp.where(grp == g, part, 0.0)
        o_ref[at, :] = (acc / den).astype(jnp.bfloat16)


def attend(place, first, grp, suf, pieces, where_k, where_v):
    rows = suf.shape[1]
    return pl.pallas_call(
        functools.partial(attend_kernel, where_k, where_v),
        out_shape=jax.ShapeDtypeStruct((rows, HD), jnp.bfloat16),
        in_specs=[SMEM] + [VMEM] * (3 + len(pieces)),
        out_specs=VMEM,
        scratch_shapes=[
            pltpu.VMEM((2, RB, SEEN), jnp.float32),
            pltpu.VMEM((2, RB, SEEN), jnp.bfloat16),
        ],
        compiler_params=pltpu.CompilerParams(vmem_limit_bytes=8 << 20),
        name="attend",
    )(place, first, grp, suf, *pieces)


def proj_kernel(head, where_ref, *refs):
    att = refs[:5]
    own, near, other = refs[5:8]
    add_ref = refs[8] if len(refs) == 10 else None
    o_ref = refs[-1]
    cols = o_ref.shape[1] // 4
    rows = o_ref.shape[0]
    mine = where_ref[0] == head
    for x in range(4):
        c0 = pl.multiple_of(lax.bitwise_xor(where_ref[1], x) * cols, cols)
        acc = jnp.dot(
            att[0][...],
            own[head * HD : (head + 1) * HD, pl.ds(c0, cols)],
            preferred_element_type=jnp.float32,
        )
        for m in range(1, 4):
            w = jnp.where(mine, near[3 * x + m - 1], other[3 * x + m - 1])
            a = att[m][...]
            if m == 3:
                a = a + att[4][...]
            acc = acc + jnp.dot(a, w, preferred_element_type=jnp.float32)
        if add_ref is not None:
            acc = acc + add_ref[:, pl.ds(c0, cols)]
        o_ref[:, pl.ds(c0, cols)] = acc.astype(o_ref.dtype)


def project(head, where, att, own, near, other, add=None):
    rows = att[0].shape[0]
    cols = own.shape[1]
    extra = [] if add is None else [add]
    return pl.pallas_call(
        functools.partial(proj_kernel, head),
        out_shape=jax.ShapeDtypeStruct((rows, cols), jnp.float32 if add is None else jnp.bfloat16),
        in_specs=[SMEM] + [VMEM] * (len(att) + 3 + len(extra)),
        out_specs=VMEM,
        compiler_params=pltpu.CompilerParams(vmem_limit_bytes=6 << 20),
        name="project",
    )(where, *att, own, near, other, *extra)


def swap(x, axis, mask, size):
    return lax.ppermute(x, axis, [(i, i ^ mask) for i in range(size)])


def after(x, *deps):
    return lax.optimization_barrier((x,) + deps)[0]


over_x = functools.partial(swap, axis="req", mask=2, size=8)
over_y = functools.partial(swap, axis="req", mask=4, size=8)
over_core = functools.partial(swap, axis="req", mask=1, size=8)


def over_tp(a):
    two = swap(a, "tp", 2, 4)
    one = swap(a, "tp", 1, 4)
    three = lax.ppermute(a, "tp", [(1, 2), (2, 1)])
    forward = lax.ppermute(two, "tp", [(2, 3), (1, 0)])
    return [a, one, two, three, forward]


WHERE_K = ((0, 0), (5, 0), (1, 0), (6, 0), (2, 0), (7, 0), (3, 0), (8, 0))
WHERE_V = ((0, 1), (5, 1), (1, 1), (6, 1), (2, 1), (7, 1), (4, 0), (9, 0))


def split_heads(suffix_heads, prefix_cache, lengths, groups, owners, out_weight):
    me = lax.axis_index("req")
    z = lax.axis_index("tp")
    core = me & 1
    chip = me >> 1
    where = jnp.stack([core, chip]).astype(jnp.int32)
    place = jnp.sum(
        jnp.where(
            owners[None] == (me ^ jnp.arange(SLOTS, dtype=jnp.int32))[:, None, None],
            jnp.arange(SLOTS, dtype=jnp.int32).reshape(1, GROUPS, OWNERS),
            0,
        ),
        axis=(1, 2),
    ).astype(jnp.int32)
    tp_size = 4

    cols = out_weight.shape[1] // tp_size
    z_u, core_u, chip_u = (i.astype(jnp.uint32) for i in (z, core, chip))
    starts = [core_u * HD, z_u * cols]
    starts += [(z_u ^ m) * cols + chip_u * (cols // 4) for m in range(1, tp_size)]
    prefix = jnp.swapaxes(prefix_cache, 0, 1)
    kv0, *starts = lax.optimization_barrier((prefix[:, :, :HD], *starts))
    sends = [
        lax.dynamic_slice(out_weight, (starts[0], starts[1 + m]), (HD, cols // 4))
        for m in range(1, tp_size)
    ]
    w_own = lax.dynamic_slice(
        out_weight, (jnp.zeros_like(starts[0]), starts[1]), (out_weight.shape[0], cols)
    )

    kvx0 = over_x(kv0)
    kvy0 = over_y(kv0)
    kvc0 = over_core(kv0)
    w_one, w_two, w_three = (
        swap(after(sends[m - 1], kvc0), "tp", m, tp_size) for m in range(1, tp_size)
    )
    table = jnp.concatenate([lengths, groups], axis=0)
    first, grp, suf0, suf1 = prepare(
        after(table, kvc0), suffix_heads[:, 0], suffix_heads[:, 1], suffix_heads[:, 2]
    )
    kxy0 = over_y(after(kvx0[0:1], suf0, w_one, w_two))
    vyx0 = over_x(after(kvy0[1:2], suf0, w_one, w_two))
    kv1 = after(prefix[:, :, HD:], kxy0, vyx0, w_own)
    kvx1 = over_x(kv1)
    kvy1 = over_y(kv1)
    pieces0 = [kv0, kvx0, kvy0, kxy0, vyx0]
    pieces0 += [kvc0] + [over_core(after(p, suf0)) for p in pieces0[1:3]]
    pieces0 += [over_core(p) for p in pieces0[3:5]]
    att0 = attend(after(place, w_three), first, grp, suf0, pieces0, WHERE_K, WHERE_V)

    kxy1 = over_y(after(kvx1[0:1], att0))
    vyx1 = over_x(after(kvy1[1:2], att0))
    pieces1 = [kv1, kvx1, kvy1, kxy1, vyx1]
    spread0 = over_tp(att0)
    pieces1 += [over_core(p) for p in pieces1[:3]]
    pieces1 += [over_core(after(p, *spread0[1:4])) for p in pieces1[3:5]]
    att1 = attend(place, first, grp, suf1, pieces1, WHERE_K, WHERE_V)

    w_far = jnp.stack([after(w_one, att0), w_two, w_three])
    w_x = over_x(after(w_far, kxy1, vyx1))
    w_y = over_y(after(w_far, kxy1, vyx1))
    w_xy = over_y(w_x)
    w_chips = jnp.concatenate([w_far, w_x, w_y, w_xy])
    spread1 = over_tp(att1)
    w_core = over_core(after(w_chips, *spread1[1:4]))
    half = project(0, where, spread0, w_own, w_chips, w_core)
    return project(1, where, spread1, w_own, w_chips, w_core, half)


def whole_heads(suffix_heads, prefix_cache, lengths, groups, owners, out_weight):
    heads = suffix_heads.shape[2] // HD
    received = [
        from_root(prefix_cache, "req", owners[i // OWNERS, i % OWNERS]) for i in range(SLOTS)
    ]
    place = jnp.arange(SLOTS, dtype=jnp.int32)
    first, grp, *sufs = prepare(
        jnp.concatenate([lengths, groups], axis=0),
        suffix_heads[:, 0],
        suffix_heads[:, 1],
        suffix_heads[:, 2],
    )
    where_k = tuple((d, 0) for d in range(SLOTS))
    where_v = tuple((d, 1) for d in range(SLOTS))
    attended = []
    for h in range(heads):
        pieces = [jnp.swapaxes(s[:, :, h * HD : (h + 1) * HD], 0, 1) for s in received]
        attended.append(attend(place, first, grp, sufs[h], pieces, where_k, where_v))
    partial_out = jnp.dot(
        jnp.concatenate(attended, axis=1), out_weight, preferred_element_type=jnp.float32
    )
    return lax.psum_scatter(partial_out.astype(jnp.bfloat16), "tp", scatter_dimension=1, tiled=True)


def per_device(req_size, tp_size, *args):
    if req_size == 8 and tp_size == 4 and args[0].shape[2] == 2 * HD:
        return split_heads(*args)
    return whole_heads(*args)


def solution(mesh):
    placed = (
        P("req", None, "tp"),
        P("req", None, "tp"),
        P("req", None),
        P("req", None),
        P(),
        P("tp", None),
    )
    return jax.shard_map(
        functools.partial(per_device, mesh.shape["req"], mesh.shape["tp"]),
        mesh=mesh,
        in_specs=placed,
        out_specs=P("req", "tp"),
        check_vma=False,
    )
```

```python
import functools
import jax
import jax.numpy as jnp
import numpy as np
from jax import lax
from jax.experimental import pallas as pl
from jax.experimental.pallas import tpu as pltpu
from jax.sharding import PartitionSpec as P

HD = 256
ROT = 64
BLK = 512
OWNERS = 2
GROUPS = 4
SLOTS = GROUPS * OWNERS
MOST = 128
SEEN = OWNERS * BLK

NEG_FILL = -1e30
ROPE_BASE = 10000.0
FACTOR = HD ** (-0.5) * 1.4426950408889634

RB = 128

VMEM = pl.BlockSpec(memory_space=pltpu.VMEM)
SMEM = pl.BlockSpec(memory_space=pltpu.SMEM)


def from_root(x, axis, root):
    mine = lax.axis_index(axis) == root
    return lax.psum(jnp.where(mine, x, jnp.zeros_like(x)), axis)


def rope_table():
    inverse = np.float32(ROPE_BASE) ** (-2.0 * np.arange(ROT // 2, dtype=np.float32) / ROT)
    inverse = np.concatenate([np.repeat(inverse, 2), np.zeros(128 - ROT)]).astype(np.float32)
    angles = np.arange(SEEN, SEEN + MOST, dtype=np.float32)[:, None] * inverse[None, :]
    angles = angles.astype(np.float64)
    sign = np.where(np.arange(128) % 2 == 0, -1.0, 1.0)
    table = np.concatenate([np.cos(angles), np.sin(angles) * sign[None, :]], axis=1)
    return jnp.asarray(table.astype(np.float32))


def prep_kernel(spans, where_ref, *refs):
    tables = refs[:spans]
    q_ref, k_ref, v_ref, rope_ref = refs[spans : spans + 4]
    first_ref, grp_ref = refs[spans + 4 : spans + 6]
    o_refs = refs[spans + 6 :]
    rows = q_ref.shape[0]
    heads = len(o_refs)
    lane = lax.broadcasted_iota(jnp.int32, (RB, 128), 1)
    even = (lane % 2) == 0
    for n in range(spans):
        requests = tables[n].shape[1]
        for r0 in range(0, rows, RB):
            row = r0 + lax.broadcasted_iota(jnp.int32, (RB, 128), 0)
            start = jnp.int32(0)
            first = jnp.zeros((RB, 128), jnp.int32)
            grp = jnp.zeros((RB, 128), jnp.int32) + tables[n][1, 0]
            for r in range(1, requests):
                start = start + tables[n][0, r - 1]
                later = row >= start
                first = jnp.where(later, start, first)
                grp = jnp.where(later, tables[n][1, r], grp)
            first_ref[n * rows + r0 : n * rows + r0 + RB, :] = first
            grp_ref[n * rows + r0 : n * rows + r0 + RB, :] = grp
    for r0 in range(0, rows, RB):
        at = slice(r0, r0 + RB)
        row = r0 + lax.broadcasted_iota(jnp.int32, (RB, 128), 0)
        chosen = jnp.where(row - first_ref[at, :] == lane, 1.0, 0.0)
        turn = lax.dot_general(
            chosen,
            rope_ref[...],
            (((1,), (0,)), ((), ())),
            precision=lax.Precision.HIGHEST,
            preferred_element_type=jnp.float32,
        )
        cos = turn[:, :128]
        sin = turn[:, 128:]
        for i, o_ref in enumerate(o_refs):
            flip = where_ref[1] > 0
            for n, ref in enumerate((q_ref, k_ref)):
                x = ref[at, i * HD : (i + 1) * HD]
                if heads == 2:
                    x = jnp.where(flip, ref[at, (1 - i) * HD : (2 - i) * HD], x)
                y = x[:, :128].astype(jnp.float32)
                swapped = jnp.where(even, pltpu.roll(y, 127, 1), pltpu.roll(y, 1, 1))
                o_ref[n, at, 0:128] = (y * cos + swapped * sin).astype(jnp.bfloat16)
                o_ref[n, at, 128:HD] = x[:, 128:]
            v = v_ref[at, i * HD : (i + 1) * HD]
            if heads == 2:
                v = jnp.where(flip, v_ref[at, (1 - i) * HD : (2 - i) * HD], v)
            o_ref[2, at, :] = v


def prepare(where, tables, q, k, v):
    rows, feat = q.shape
    heads = feat // HD
    spans = len(tables)
    column = jax.ShapeDtypeStruct((spans * rows, 128), jnp.int32)
    return pl.pallas_call(
        functools.partial(prep_kernel, spans),
        out_shape=[column] * 2 + [jax.ShapeDtypeStruct((3, rows, HD), jnp.bfloat16)] * heads,
        in_specs=[SMEM] * (1 + spans) + [VMEM] * 4,
        out_specs=[VMEM] * (2 + heads),
        compiler_params=pltpu.CompilerParams(vmem_limit_bytes=4 << 20),
        name="prepare",
    )(where, *tables, q, k, v, rope_table())


def wide(x, width):
    return x if width == 128 else jnp.concatenate([x] * (width // 128), axis=1)


def flatten(refs, counts):
    return [ref.at[j] for ref, count in zip(refs, counts) for j in range(count)]


def score_kernel(nb, counts, place_ref, first_ref, grp_ref, *rest):
    sufs = rest[:nb]
    n_pieces = len(counts)
    pieces = flatten(rest[nb : nb + n_pieces], counts)
    p_ref, near_ref, den_ref, sc = rest[nb + n_pieces :]
    half = 256
    for n in range(nb):
        rows = sufs[n].shape[1]
        for b in range(rows // RB):
            r0 = b * RB
            t0 = n * rows + r0
            buf = (t0 // RB) % 2
            q = sufs[n][0, r0 : r0 + RB, :]
            grp = wide(grp_ref[t0 : t0 + RB, :], half)
            for d in range(SLOTS):
                g = place_ref[d] // OWNERS
                o = place_ref[d] % OWNERS
                for j in range(BLK // half):
                    s = lax.dot_general(
                        q,
                        pieces[d][j * half : (j + 1) * half, :],
                        (((1,), (1,)), ((), ())),
                        preferred_element_type=jnp.float32,
                    )
                    at = pl.ds(pl.multiple_of(o * BLK + j * half, half), half)
                    sc[buf, :, at] = jnp.where(grp == g, s, sc[buf, :, at])
            lo = max(0, r0 - MOST)
            width = r0 + RB - lo
            local = lax.dot_general(
                q,
                sufs[n][1, lo : r0 + RB, :],
                (((1,), (1,)), ((), ())),
                preferred_element_type=jnp.float32,
            )
            row = r0 + lax.broadcasted_iota(jnp.int32, (RB, width), 0)
            key = lo + lax.broadcasted_iota(jnp.int32, (RB, width), 1)
            start = wide(first_ref[t0 : t0 + RB, :], width)
            local = jnp.where((key <= row) & (key >= start), local, NEG_FILL)
            top = jnp.max(local, axis=1, keepdims=True)
            whole = sc[buf, :, 0:half]
            for c0 in range(half, SEEN, half):
                whole = jnp.maximum(whole, sc[buf, :, c0 : c0 + half])
            top = jnp.maximum(top, jnp.max(whole, axis=1, keepdims=True))
            e = jnp.exp2((local - top) * FACTOR)
            den = jnp.sum(e, axis=1, keepdims=True)
            near_ref[t0 : t0 + RB, 0:width] = e.astype(jnp.bfloat16)
            total = None
            for c0 in range(0, SEEN, half):
                e = jnp.exp2((sc[buf, :, c0 : c0 + half] - top) * FACTOR)
                p_ref[t0 : t0 + RB, c0 : c0 + half] = e.astype(jnp.bfloat16)
                total = e if total is None else total + e
            den = den + jnp.sum(total, axis=1, keepdims=True)
            den_ref[t0 : t0 + RB, :] = jnp.broadcast_to(den, (RB, 128))


def score(place, first, grp, sufs, pieces):
    rows = sum(s.shape[1] for s in sufs)
    return pl.pallas_call(
        functools.partial(score_kernel, len(sufs), tuple(p.shape[0] for p in pieces)),
        out_shape=[
            jax.ShapeDtypeStruct((rows, SEEN), jnp.bfloat16),
            jax.ShapeDtypeStruct((rows, RB + MOST), jnp.bfloat16),
            jax.ShapeDtypeStruct((rows, 128), jnp.float32),
        ],
        in_specs=[SMEM] + [VMEM] * (2 + len(sufs) + len(pieces)),
        out_specs=[VMEM] * 3,
        scratch_shapes=[pltpu.VMEM((2, RB, SEEN), jnp.float32)],
        compiler_params=pltpu.CompilerParams(vmem_limit_bytes=4 << 20),
        name="score",
    )(place, first, grp, *sufs, *pieces)


def mix_kernel(nb, counts, col, place_ref, grp_ref, p_ref, near_ref, den_ref, *rest):
    sufs = rest[:nb]
    n_pieces = len(counts)
    pieces = flatten(rest[nb : nb + n_pieces], counts)
    outs = rest[nb + n_pieces :]
    width = outs[0].shape[1]
    for n in reversed(range(nb)):
        rows = outs[n].shape[0]
        for b in range(rows // RB):
            r0 = b * RB
            t0 = n * rows + r0
            grp = wide(grp_ref[t0 : t0 + RB, :], width)
            lo = max(0, r0 - MOST)
            acc = jnp.dot(
                near_ref[t0 : t0 + RB, 0 : r0 + RB - lo],
                sufs[n][2, lo : r0 + RB, col : col + width],
                preferred_element_type=jnp.float32,
            )
            for d in range(SLOTS):
                g = place_ref[d] // OWNERS
                o = place_ref[d] % OWNERS
                part = jnp.dot(
                    p_ref[t0 : t0 + RB, pl.ds(pl.multiple_of(o * BLK, BLK), BLK)],
                    pieces[d][...],
                    preferred_element_type=jnp.float32,
                )
                acc = acc + jnp.where(grp == g, part, 0.0)
            den = wide(den_ref[t0 : t0 + RB, :], width)
            outs[n][r0 : r0 + RB, :] = (acc / den).astype(jnp.bfloat16)


def mix(col, width, place, grp, scored, sufs, pieces):
    rows = sufs[0].shape[1]
    nb = len(sufs)
    return pl.pallas_call(
        functools.partial(mix_kernel, nb, tuple(p.shape[0] for p in pieces), col),
        out_shape=[jax.ShapeDtypeStruct((rows, width), jnp.bfloat16)] * nb,
        in_specs=[SMEM] + [VMEM] * (4 + nb + len(pieces)),
        out_specs=[VMEM] * nb,
        compiler_params=pltpu.CompilerParams(vmem_limit_bytes=4 << 20),
        name="mix",
    )(place, grp, *scored, *sufs, *pieces)


def proj_kernel(where_ref, *refs):
    att = refs[:10]
    own = refs[10]
    far = refs[11:15]
    o_ref = refs[15]
    cols = o_ref.shape[1] // 2
    rows = o_ref.shape[0]
    core = where_ref[1]
    side = where_ref[2]
    tall = 256
    for r0 in range(0, rows, tall):
        for x in range(2):
            c0 = pl.multiple_of(lax.bitwise_xor(side, x) * cols, cols)
            acc = jnp.zeros((tall, cols), jnp.float32)
            for h in range(2):
                head = lax.bitwise_xor(core, h)
                for m in range(4):
                    a = att[h * 5 + m][r0 : r0 + tall, :]
                    if m == 3:
                        a = a + att[h * 5 + 4][r0 : r0 + tall, :]
                    if m == 0:
                        w = own[pl.ds(pl.multiple_of(head * HD, HD), HD), pl.ds(c0, cols)]
                    else:
                        w = far[2 * h + x][m - 1]
                    acc = acc + jnp.dot(a, w, preferred_element_type=jnp.float32)
            o_ref[r0 : r0 + tall, pl.ds(c0, cols)] = acc.astype(jnp.bfloat16)


def project(where, att, own, far):
    rows = att[0].shape[0]
    cols = own.shape[1]
    return pl.pallas_call(
        proj_kernel,
        out_shape=jax.ShapeDtypeStruct((rows, cols), jnp.bfloat16),
        in_specs=[SMEM] + [VMEM] * (len(att) + 1 + len(far)),
        out_specs=VMEM,
        compiler_params=pltpu.CompilerParams(vmem_limit_bytes=6 << 20),
        name="project",
    )(where, *att, own, *far)


def swap(x, axis, mask, size):
    return lax.ppermute(x, axis, [(i, i ^ mask) for i in range(size)])


def after(x, *deps):
    return lax.optimization_barrier((x,) + deps)[0]


over_x = functools.partial(swap, axis="req", mask=2, size=8)
over_y = functools.partial(swap, axis="req", mask=4, size=8)
over_core = functools.partial(swap, axis="req", mask=1, size=8)


def split_heads(suffix_heads, prefix_cache, lengths, groups, owners, out_weight):
    me = lax.axis_index("req")
    z = lax.axis_index("tp")
    core = me & 1
    side = (me >> 1) & 1
    where = jnp.stack([z, core, side]).astype(jnp.int32)
    place = jnp.sum(
        jnp.where(
            owners[None] == (me ^ jnp.arange(SLOTS, dtype=jnp.int32))[:, None, None],
            jnp.arange(SLOTS, dtype=jnp.int32).reshape(1, GROUPS, OWNERS),
            0,
        ),
        axis=(1, 2),
    ).astype(jnp.int32)
    tp_size = 4
    first_head = core == 0

    cols = out_weight.shape[1] // tp_size
    z_u, core_u, side_u = (i.astype(jnp.uint32) for i in (z, core, side))
    starts = [core_u * HD, z_u * cols]
    starts += [(z_u ^ m) * cols + side_u * (cols // 2) for m in range(1, tp_size)]
    first_head, *starts = lax.optimization_barrier((first_head, *starts))
    sends = [
        lax.dynamic_slice(out_weight, (starts[0], starts[1 + m]), (HD, cols // 2))
        for m in range(1, tp_size)
    ]
    w_own = lax.dynamic_slice(
        out_weight, (jnp.zeros_like(starts[0]), starts[1]), (out_weight.shape[0], cols)
    )

    k = prefix_cache[:, 0]
    k_own = jnp.where(first_head, k[:, :HD], k[:, HD:])
    k_other = jnp.where(first_head, k[:, HD:], k[:, :HD])
    k_both = jnp.stack([k_own, over_core(k_other)])
    kx = over_x(k_both)
    ky = over_y(k_both)
    w_one, w_two = (swap(sends[m - 1], "tp", m, tp_size) for m in (1, 2))

    table = jnp.concatenate([lengths, groups], axis=0)
    table_pair = over_core(table)
    suffix = after(suffix_heads, k_both)
    first, grp, mine, other = prepare(
        after(where, k_both), (table, table_pair), suffix[:, 0], suffix[:, 1], suffix[:, 2]
    )
    sufs = [mine, over_core(other)]
    v = after(prefix_cache, k_both)[:, 1]
    v_own = jnp.where(first_head, v[:, :HD], v[:, HD:])
    v_other = jnp.where(first_head, v[:, HD:], v[:, :HD])
    v_both = jnp.stack([v_own, over_core(v_other)])

    kxy = over_y(after(kx[0:1], mine, v_both))
    kyx = over_x(after(ky[1:2], mine, v_both))
    v_both = after(v_both, kxy, kyx, w_one, w_two, sufs[1])
    vx = over_x(v_both)
    vy = over_y(v_both)
    w_three = swap(after(sends[2], w_two), "tp", 3, tp_size)
    scored = score(after(place, w_own), first, grp, sufs, (k_both, kx, ky, kxy, kyx))
    w_far = jnp.stack([after(w_one, scored[0]), w_two, w_three])
    w_core = over_core(w_far)
    vxy = over_y(after(vx[0:1], scored[0], w_far))
    vyx = over_x(after(vy[1:2], scored[0], w_far))
    own, pair = mix(0, HD, place, grp, scored, sufs, (v_both, vx, vy, vxy, vyx))
    w_x = over_x(after(w_far, vxy, vyx))

    back = over_core(pair)
    two_own = swap(own, "tp", 2, tp_size)
    two_back = swap(back, "tp", 2, tp_size)
    one_own = swap(own, "tp", 1, tp_size)
    one_back = swap(back, "tp", 1, tp_size)
    w_core_x = over_core(after(w_x, two_own, two_back, one_own, one_back))
    att = []
    for a, one, two in ((own, one_own, two_own), (back, one_back, two_back)):
        three = lax.ppermute(after(a, one, two), "tp", [(1, 2), (2, 1)])
        forward = lax.ppermute(two, "tp", [(2, 3), (1, 0)])
        att += [a, one, two, three, forward]
    return project(where, att, w_own, [w_far, w_x, w_core, w_core_x])


def whole_heads(suffix_heads, prefix_cache, lengths, groups, owners, out_weight):
    heads = suffix_heads.shape[2] // HD
    received = [
        from_root(prefix_cache, "req", owners[i // OWNERS, i % OWNERS]) for i in range(SLOTS)
    ]
    place = jnp.arange(SLOTS, dtype=jnp.int32)
    first, grp, *sufs = prepare(
        jnp.zeros((3,), jnp.int32),
        (jnp.concatenate([lengths, groups], axis=0),),
        suffix_heads[:, 0],
        suffix_heads[:, 1],
        suffix_heads[:, 2],
    )
    attended = []
    for h in range(heads):
        keys = [s[None, :, 0, h * HD : (h + 1) * HD] for s in received]
        values = [s[None, :, 1, h * HD : (h + 1) * HD] for s in received]
        scored = score(place, first, grp, [sufs[h]], keys)
        attended += mix(0, HD, place, grp, scored, [sufs[h]], values)
    partial_out = jnp.dot(
        jnp.concatenate(attended, axis=1), out_weight, preferred_element_type=jnp.float32
    )
    return lax.psum_scatter(partial_out.astype(jnp.bfloat16), "tp", scatter_dimension=1, tiled=True)


def per_device(req_size, tp_size, *args):
    if req_size == 8 and tp_size == 4 and args[0].shape[2] == 2 * HD:
        return split_heads(*args)
    return whole_heads(*args)


def solution(mesh):
    placed = (
        P("req", None, "tp"),
        P("req", None, "tp"),
        P("req", None),
        P("req", None),
        P(),
        P("tp", None),
    )
    return jax.shard_map(
        functools.partial(per_device, mesh.shape["req"], mesh.shape["tp"]),
        mesh=mesh,
        in_specs=placed,
        out_specs=P("req", "tp"),
        check_vma=False,
    )
```

```python
import functools
import jax
import jax.numpy as jnp
import numpy as np
from jax import lax
from jax.experimental import pallas as pl
from jax.experimental.pallas import tpu as pltpu
from jax.sharding import PartitionSpec as P

HD = 256
ROT = 64
BLK = 512
OWNERS = 2
GROUPS = 4
SLOTS = GROUPS * OWNERS
MOST = 128
SEEN = OWNERS * BLK

NEG_FILL = -1e30
ROPE_BASE = 10000.0
FACTOR = HD ** (-0.5) * 1.4426950408889634

RB = 128

VMEM = pl.BlockSpec(memory_space=pltpu.VMEM)
SMEM = pl.BlockSpec(memory_space=pltpu.SMEM)


def from_root(x, axis, root):
    mine = lax.axis_index(axis) == root
    return lax.psum(jnp.where(mine, x, jnp.zeros_like(x)), axis)


def rope_table():
    inverse = np.float32(ROPE_BASE) ** (-2.0 * np.arange(ROT // 2, dtype=np.float32) / ROT)
    inverse = np.concatenate([np.repeat(inverse, 2), np.zeros(128 - ROT)]).astype(np.float32)
    angles = np.arange(SEEN, SEEN + MOST, dtype=np.float32)[:, None] * inverse[None, :]
    angles = angles.astype(np.float64)
    sign = np.where(np.arange(128) % 2 == 0, -1.0, 1.0)
    table = np.concatenate([np.cos(angles), np.sin(angles) * sign[None, :]], axis=1)
    return jnp.asarray(table.astype(np.float32))


def prep_kernel(spans, where_ref, *refs):
    tables = refs[:spans]
    q_ref, k_ref, v_ref, rope_ref = refs[spans : spans + 4]
    first_ref, grp_ref = refs[spans + 4 : spans + 6]
    o_refs = refs[spans + 6 :]
    rows = q_ref.shape[0]
    heads = len(o_refs)
    lane = lax.broadcasted_iota(jnp.int32, (RB, 128), 1)
    even = (lane % 2) == 0
    for n in range(spans):
        requests = tables[n].shape[1]
        for r0 in range(0, rows, RB):
            row = r0 + lax.broadcasted_iota(jnp.int32, (RB, 128), 0)
            start = jnp.int32(0)
            first = jnp.zeros((RB, 128), jnp.int32)
            grp = jnp.zeros((RB, 128), jnp.int32) + tables[n][1, 0]
            for r in range(1, requests):
                start = start + tables[n][0, r - 1]
                later = row >= start
                first = jnp.where(later, start, first)
                grp = jnp.where(later, tables[n][1, r], grp)
            first_ref[n * rows + r0 : n * rows + r0 + RB, :] = first
            grp_ref[n * rows + r0 : n * rows + r0 + RB, :] = grp
    for r0 in range(0, rows, RB):
        at = slice(r0, r0 + RB)
        row = r0 + lax.broadcasted_iota(jnp.int32, (RB, 128), 0)
        chosen = jnp.where(row - first_ref[at, :] == lane, 1.0, 0.0)
        turn = lax.dot_general(
            chosen,
            rope_ref[...],
            (((1,), (0,)), ((), ())),
            precision=lax.Precision.HIGHEST,
            preferred_element_type=jnp.float32,
        )
        cos = turn[:, :128]
        sin = turn[:, 128:]
        for i, o_ref in enumerate(o_refs):
            flip = where_ref[1] > 0
            for n, ref in enumerate((q_ref, k_ref)):
                x = ref[at, i * HD : (i + 1) * HD]
                if heads == 2:
                    x = jnp.where(flip, ref[at, (1 - i) * HD : (2 - i) * HD], x)
                y = x[:, :128].astype(jnp.float32)
                swapped = jnp.where(even, pltpu.roll(y, 127, 1), pltpu.roll(y, 1, 1))
                o_ref[n, at, 0:128] = (y * cos + swapped * sin).astype(jnp.bfloat16)
                o_ref[n, at, 128:HD] = x[:, 128:]
            v = v_ref[at, i * HD : (i + 1) * HD]
            if heads == 2:
                v = jnp.where(flip, v_ref[at, (1 - i) * HD : (2 - i) * HD], v)
            o_ref[2, at, :] = v


def prepare(where, tables, q, k, v):
    rows, feat = q.shape
    heads = feat // HD
    spans = len(tables)
    column = jax.ShapeDtypeStruct((spans * rows, 128), jnp.int32)
    return pl.pallas_call(
        functools.partial(prep_kernel, spans),
        out_shape=[column] * 2 + [jax.ShapeDtypeStruct((3, rows, HD), jnp.bfloat16)] * heads,
        in_specs=[SMEM] * (1 + spans) + [VMEM] * 4,
        out_specs=[VMEM] * (2 + heads),
        compiler_params=pltpu.CompilerParams(vmem_limit_bytes=4 << 20),
        name="prepare",
    )(where, *tables, q, k, v, rope_table())


def wide(x, width):
    return x if width == 128 else jnp.concatenate([x] * (width // 128), axis=1)


def flatten(refs, counts):
    return [ref.at[j] for ref, count in zip(refs, counts) for j in range(count)]


def score_kernel(nb, counts, place_ref, first_ref, grp_ref, *rest):
    sufs = rest[:nb]
    n_pieces = len(counts)
    pieces = flatten(rest[nb : nb + n_pieces], counts)
    p_ref, near_ref, den_ref, sc = rest[nb + n_pieces :]
    half = 256
    for n in range(nb):
        rows = sufs[n].shape[1]
        for b in range(rows // RB):
            r0 = b * RB
            t0 = n * rows + r0
            buf = (t0 // RB) % 2
            q = sufs[n][0, r0 : r0 + RB, :]
            grp = wide(grp_ref[t0 : t0 + RB, :], half)
            for d in range(SLOTS):
                g = place_ref[d] // OWNERS
                o = place_ref[d] % OWNERS
                for j in range(BLK // half):
                    s = lax.dot_general(
                        q,
                        pieces[d][j * half : (j + 1) * half, :],
                        (((1,), (1,)), ((), ())),
                        preferred_element_type=jnp.float32,
                    )
                    at = pl.ds(pl.multiple_of(o * BLK + j * half, half), half)
                    sc[buf, :, at] = jnp.where(grp == g, s, sc[buf, :, at])
            lo = max(0, r0 - MOST)
            width = r0 + RB - lo
            local = lax.dot_general(
                q,
                sufs[n][1, lo : r0 + RB, :],
                (((1,), (1,)), ((), ())),
                preferred_element_type=jnp.float32,
            )
            row = r0 + lax.broadcasted_iota(jnp.int32, (RB, width), 0)
            key = lo + lax.broadcasted_iota(jnp.int32, (RB, width), 1)
            start = wide(first_ref[t0 : t0 + RB, :], width)
            local = jnp.where((key <= row) & (key >= start), local, NEG_FILL)
            top = jnp.max(local, axis=1, keepdims=True)
            whole = sc[buf, :, 0:half]
            for c0 in range(half, SEEN, half):
                whole = jnp.maximum(whole, sc[buf, :, c0 : c0 + half])
            top = jnp.maximum(top, jnp.max(whole, axis=1, keepdims=True))
            e = jnp.exp2((local - top) * FACTOR)
            den = jnp.sum(e, axis=1, keepdims=True)
            near_ref[t0 : t0 + RB, 0:width] = e.astype(jnp.bfloat16)
            total = None
            for c0 in range(0, SEEN, half):
                e = jnp.exp2((sc[buf, :, c0 : c0 + half] - top) * FACTOR)
                p_ref[t0 : t0 + RB, c0 : c0 + half] = e.astype(jnp.bfloat16)
                total = e if total is None else total + e
            den = den + jnp.sum(total, axis=1, keepdims=True)
            den_ref[t0 : t0 + RB, :] = jnp.broadcast_to(den, (RB, 128))


def score(place, first, grp, sufs, pieces):
    rows = sum(s.shape[1] for s in sufs)
    return pl.pallas_call(
        functools.partial(score_kernel, len(sufs), tuple(p.shape[0] for p in pieces)),
        out_shape=[
            jax.ShapeDtypeStruct((rows, SEEN), jnp.bfloat16),
            jax.ShapeDtypeStruct((rows, RB + MOST), jnp.bfloat16),
            jax.ShapeDtypeStruct((rows, 128), jnp.float32),
        ],
        in_specs=[SMEM] + [VMEM] * (2 + len(sufs) + len(pieces)),
        out_specs=[VMEM] * 3,
        scratch_shapes=[pltpu.VMEM((2, RB, SEEN), jnp.float32)],
        compiler_params=pltpu.CompilerParams(vmem_limit_bytes=4 << 20),
        name="score",
    )(place, first, grp, *sufs, *pieces)


def mix_kernel(nb, base, counts, col, place_ref, grp_ref, p_ref, near_ref, den_ref, *rest):
    sufs = rest[:nb]
    n_pieces = len(counts)
    pieces = flatten(rest[nb : nb + n_pieces], counts)
    outs = rest[nb + n_pieces :]
    width = outs[0].shape[1]
    for n in reversed(range(nb)):
        rows = outs[n].shape[0]
        for b in range(rows // RB):
            r0 = b * RB
            t0 = base + n * rows + r0
            grp = wide(grp_ref[t0 : t0 + RB, :], width)
            lo = max(0, r0 - MOST)
            acc = jnp.dot(
                near_ref[t0 : t0 + RB, 0 : r0 + RB - lo],
                sufs[n][2, lo : r0 + RB, col : col + width],
                preferred_element_type=jnp.float32,
            )
            for d in range(SLOTS):
                g = place_ref[d] // OWNERS
                o = place_ref[d] % OWNERS
                part = jnp.dot(
                    p_ref[t0 : t0 + RB, pl.ds(pl.multiple_of(o * BLK, BLK), BLK)],
                    pieces[d][...],
                    preferred_element_type=jnp.float32,
                )
                acc = acc + jnp.where(grp == g, part, 0.0)
            den = wide(den_ref[t0 : t0 + RB, :], width)
            outs[n][r0 : r0 + RB, :] = (acc / den).astype(jnp.bfloat16)


def mix(col, width, place, grp, scored, sufs, pieces, base=0):
    rows = sufs[0].shape[1]
    nb = len(sufs)
    return pl.pallas_call(
        functools.partial(mix_kernel, nb, base, tuple(p.shape[0] for p in pieces), col),
        out_shape=[jax.ShapeDtypeStruct((rows, width), jnp.bfloat16)] * nb,
        in_specs=[SMEM] + [VMEM] * (4 + nb + len(pieces)),
        out_specs=[VMEM] * nb,
        compiler_params=pltpu.CompilerParams(vmem_limit_bytes=4 << 20),
        name="mix",
    )(place, grp, *scored, *sufs, *pieces)


def proj_kernel(steps, last, where_ref, *refs):
    att = refs[: 2 * len(steps)]
    own, *far = refs[2 * len(steps) : 2 * len(steps) + 5]
    o_ref = refs[-1]
    cols = o_ref.shape[1] // 2
    rows = o_ref.shape[0]
    core = where_ref[1]
    side = where_ref[2]
    tall = 256
    for r0 in range(0, rows, tall):
        at = slice(r0, r0 + tall)
        for x in range(2):
            c = pl.ds(pl.multiple_of(lax.bitwise_xor(side, x) * cols, cols), cols)
            acc = refs[-2][at, c] if last else jnp.zeros((tall, cols), jnp.float32)
            for h in range(2):
                head = lax.bitwise_xor(core, h)
                lines = []
                for i, m in enumerate(steps):
                    lines.append((m, att[h * len(steps) + i][at, :]))
                if last:
                    lines = [(3, lines[0][1] + lines[1][1])]
                for m, a in lines:
                    if m == 0:
                        w = own[pl.ds(pl.multiple_of(head * HD, HD), HD), c]
                    else:
                        w = far[2 * h + x][m - 1]
                    acc = acc + jnp.dot(a, w, preferred_element_type=jnp.float32)
            o_ref[at, c] = acc.astype(o_ref.dtype)


def project(where, steps, att, own, far, add=None):
    rows = att[0].shape[0]
    cols = own.shape[1]
    extra = [] if add is None else [add]
    return pl.pallas_call(
        functools.partial(proj_kernel, steps, add is not None),
        out_shape=jax.ShapeDtypeStruct((rows, cols), jnp.float32 if add is None else jnp.bfloat16),
        in_specs=[SMEM] + [VMEM] * (len(att) + 1 + len(far) + len(extra)),
        out_specs=VMEM,
        compiler_params=pltpu.CompilerParams(vmem_limit_bytes=6 << 20),
        name="project",
    )(where, *att, own, *far, *extra)


def swap(x, axis, mask, size):
    return lax.ppermute(x, axis, [(i, i ^ mask) for i in range(size)])


def after(x, *deps):
    return lax.optimization_barrier((x,) + deps)[0]


over_x = functools.partial(swap, axis="req", mask=2, size=8)
over_y = functools.partial(swap, axis="req", mask=4, size=8)
over_core = functools.partial(swap, axis="req", mask=1, size=8)


def split_heads(suffix_heads, prefix_cache, lengths, groups, owners, out_weight):
    rows = suffix_heads.shape[0]
    me = lax.axis_index("req")
    z = lax.axis_index("tp")
    core = me & 1
    side = (me >> 1) & 1
    where = jnp.stack([z, core, side]).astype(jnp.int32)
    place = jnp.sum(
        jnp.where(
            owners[None] == (me ^ jnp.arange(SLOTS, dtype=jnp.int32))[:, None, None],
            jnp.arange(SLOTS, dtype=jnp.int32).reshape(1, GROUPS, OWNERS),
            0,
        ),
        axis=(1, 2),
    ).astype(jnp.int32)
    tp_size = 4
    first_head = core == 0

    cols = out_weight.shape[1] // tp_size
    z_u, core_u, side_u = (i.astype(jnp.uint32) for i in (z, core, side))
    starts = [core_u * HD, z_u * cols]
    starts += [(z_u ^ m) * cols + side_u * (cols // 2) for m in range(1, tp_size)]
    first_head, *starts = lax.optimization_barrier((first_head, *starts))
    sends = [
        lax.dynamic_slice(out_weight, (starts[0], starts[1 + m]), (HD, cols // 2))
        for m in range(1, tp_size)
    ]
    w_own = lax.dynamic_slice(
        out_weight, (jnp.zeros_like(starts[0]), starts[1]), (out_weight.shape[0], cols)
    )

    k = prefix_cache[:, 0]
    k_own = jnp.where(first_head, k[:, :HD], k[:, HD:])
    k_other = jnp.where(first_head, k[:, HD:], k[:, :HD])
    k_both = jnp.stack([k_own, over_core(k_other)])
    kx = over_x(k_both)
    ky = over_y(k_both)
    w_one, w_two = (swap(sends[m - 1], "tp", m, tp_size) for m in (1, 2))

    table = jnp.concatenate([lengths, groups], axis=0)
    table_pair = over_core(table)
    suffix = after(suffix_heads, k_both)
    first, grp, mine, other = prepare(
        after(where, k_both), (table, table_pair), suffix[:, 0], suffix[:, 1], suffix[:, 2]
    )
    sufs = [mine, over_core(other)]
    v = after(prefix_cache, k_both)[:, 1]
    v_own = jnp.where(first_head, v[:, :HD], v[:, HD:])
    v_other = jnp.where(first_head, v[:, HD:], v[:, :HD])
    v_both = jnp.stack([v_own, over_core(v_other)])

    kxy = over_y(after(kx[0:1], mine, v_both))
    kyx = over_x(after(ky[1:2], mine, v_both))
    v_both = after(v_both, kxy, kyx, w_one, w_two, w_own, sufs[1])
    vx = over_x(v_both)
    vy = over_y(v_both)
    w_three = swap(after(sends[2], w_two), "tp", 3, tp_size)
    scored = score(place, first, grp, sufs, (k_both, kx, ky, kxy, kyx))
    w_far = jnp.stack([after(w_one, scored[0]), w_two, w_three])
    w_core = over_core(w_far)
    vxy = over_y(after(vx[0:1], scored[0], w_far))
    vyx = over_x(after(vy[1:2], scored[0], w_far))
    v_pieces = (v_both, vx, vy, vxy, vyx)
    (own,) = mix(0, HD, place, grp, scored, sufs[:1], v_pieces)
    (pair,) = mix(0, HD, place, grp, scored, sufs[1:], v_pieces, rows)
    w_x = over_x(after(w_far, vxy, vyx))

    back = over_core(pair)
    two_own = swap(own, "tp", 2, tp_size)
    one_own = swap(own, "tp", 1, tp_size)
    two_back = swap(back, "tp", 2, tp_size)
    one_back = swap(back, "tp", 1, tp_size)
    three_own = lax.ppermute(after(own, two_own, one_own, one_back), "tp", [(1, 2), (2, 1)])
    forward_own = lax.ppermute(after(two_own, one_own, one_back), "tp", [(2, 3), (1, 0)])
    three_back = lax.ppermute(after(back, two_back, one_back), "tp", [(1, 2), (2, 1)])
    forward_back = lax.ppermute(two_back, "tp", [(2, 3), (1, 0)])
    w_core_x = over_core(after(w_x, two_back, one_back, three_own, forward_own))
    far = [w_far, w_x, w_core, w_core_x]
    near = project(where, (0, 1, 2), (own, one_own, two_own, back, one_back, two_back), w_own, far)
    last = (three_own, forward_own, three_back, forward_back)
    return project(where, (3, 3), last, w_own, far, near)


def whole_heads(suffix_heads, prefix_cache, lengths, groups, owners, out_weight):
    heads = suffix_heads.shape[2] // HD
    received = [
        from_root(prefix_cache, "req", owners[i // OWNERS, i % OWNERS]) for i in range(SLOTS)
    ]
    place = jnp.arange(SLOTS, dtype=jnp.int32)
    first, grp, *sufs = prepare(
        jnp.zeros((3,), jnp.int32),
        (jnp.concatenate([lengths, groups], axis=0),),
        suffix_heads[:, 0],
        suffix_heads[:, 1],
        suffix_heads[:, 2],
    )
    attended = []
    for h in range(heads):
        keys = [s[None, :, 0, h * HD : (h + 1) * HD] for s in received]
        values = [s[None, :, 1, h * HD : (h + 1) * HD] for s in received]
        scored = score(place, first, grp, [sufs[h]], keys)
        attended += mix(0, HD, place, grp, scored, [sufs[h]], values)
    partial_out = jnp.dot(
        jnp.concatenate(attended, axis=1), out_weight, preferred_element_type=jnp.float32
    )
    return lax.psum_scatter(partial_out.astype(jnp.bfloat16), "tp", scatter_dimension=1, tiled=True)


def per_device(req_size, tp_size, *args):
    if req_size == 8 and tp_size == 4 and args[0].shape[2] == 2 * HD:
        return split_heads(*args)
    return whole_heads(*args)


def solution(mesh):
    placed = (
        P("req", None, "tp"),
        P("req", None, "tp"),
        P("req", None),
        P("req", None),
        P(),
        P("tp", None),
    )
    return jax.shard_map(
        functools.partial(per_device, mesh.shape["req"], mesh.shape["tp"]),
        mesh=mesh,
        in_specs=placed,
        out_specs=P("req", "tp"),
        check_vma=False,
    )
```

```python
import functools
import jax
import jax.numpy as jnp
import numpy as np
from jax import lax
from jax.experimental import pallas as pl
from jax.experimental.pallas import tpu as pltpu
from jax.sharding import PartitionSpec as P

HD = 256
ROT = 64
BLK = 512
OWNERS = 2
GROUPS = 4
SLOTS = GROUPS * OWNERS
MOST = 128
SEEN = OWNERS * BLK

NEG_FILL = -1e30
ROPE_BASE = 10000.0
FACTOR = HD ** (-0.5) * 1.4426950408889634

RB = 128

VMEM = pl.BlockSpec(memory_space=pltpu.VMEM)
SMEM = pl.BlockSpec(memory_space=pltpu.SMEM)


def from_root(x, axis, root):
    mine = lax.axis_index(axis) == root
    return lax.psum(jnp.where(mine, x, jnp.zeros_like(x)), axis)


def rope_table():
    inverse = np.float32(ROPE_BASE) ** (-2.0 * np.arange(ROT // 2, dtype=np.float32) / ROT)
    inverse = np.concatenate([np.repeat(inverse, 2), np.zeros(128 - ROT)]).astype(np.float32)
    angles = np.arange(SEEN, SEEN + MOST, dtype=np.float32)[:, None] * inverse[None, :]
    angles = angles.astype(np.float64)
    sign = np.where(np.arange(128) % 2 == 0, -1.0, 1.0)
    table = np.concatenate([np.cos(angles), np.sin(angles) * sign[None, :]], axis=1)
    return jnp.asarray(table.astype(np.float32))


def prep_kernel(spans, where_ref, *refs):
    tables = refs[:spans]
    q_ref, k_ref, v_ref, rope_ref = refs[spans : spans + 4]
    first_ref, grp_ref = refs[spans + 4 : spans + 6]
    o_refs = refs[spans + 6 :]
    rows = q_ref.shape[0]
    heads = len(o_refs)
    lane = lax.broadcasted_iota(jnp.int32, (RB, 128), 1)
    even = (lane % 2) == 0
    for n in range(spans):
        requests = tables[n].shape[1]
        for r0 in range(0, rows, RB):
            row = r0 + lax.broadcasted_iota(jnp.int32, (RB, 128), 0)
            start = jnp.int32(0)
            first = jnp.zeros((RB, 128), jnp.int32)
            grp = jnp.zeros((RB, 128), jnp.int32) + tables[n][1, 0]
            for r in range(1, requests):
                start = start + tables[n][0, r - 1]
                later = row >= start
                first = jnp.where(later, start, first)
                grp = jnp.where(later, tables[n][1, r], grp)
            first_ref[n * rows + r0 : n * rows + r0 + RB, :] = first
            grp_ref[n * rows + r0 : n * rows + r0 + RB, :] = grp
    for r0 in range(0, rows, RB):
        at = slice(r0, r0 + RB)
        row = r0 + lax.broadcasted_iota(jnp.int32, (RB, 128), 0)
        chosen = jnp.where(row - first_ref[at, :] == lane, 1.0, 0.0)
        turn = lax.dot_general(
            chosen,
            rope_ref[...],
            (((1,), (0,)), ((), ())),
            precision=lax.Precision.HIGHEST,
            preferred_element_type=jnp.float32,
        )
        cos = turn[:, :128]
        sin = turn[:, 128:]
        for i, o_ref in enumerate(o_refs):
            flip = where_ref[1] > 0
            for n, ref in enumerate((q_ref, k_ref)):
                x = ref[at, i * HD : (i + 1) * HD]
                if heads == 2:
                    x = jnp.where(flip, ref[at, (1 - i) * HD : (2 - i) * HD], x)
                y = x[:, :128].astype(jnp.float32)
                swapped = jnp.where(even, pltpu.roll(y, 127, 1), pltpu.roll(y, 1, 1))
                o_ref[n, at, 0:128] = (y * cos + swapped * sin).astype(jnp.bfloat16)
                o_ref[n, at, 128:HD] = x[:, 128:]
            v = v_ref[at, i * HD : (i + 1) * HD]
            if heads == 2:
                v = jnp.where(flip, v_ref[at, (1 - i) * HD : (2 - i) * HD], v)
            o_ref[2, at, :] = v


def prepare(where, tables, q, k, v):
    rows, feat = q.shape
    heads = feat // HD
    spans = len(tables)
    column = jax.ShapeDtypeStruct((spans * rows, 128), jnp.int32)
    return pl.pallas_call(
        functools.partial(prep_kernel, spans),
        out_shape=[column] * 2 + [jax.ShapeDtypeStruct((3, rows, HD), jnp.bfloat16)] * heads,
        in_specs=[SMEM] * (1 + spans) + [VMEM] * 4,
        out_specs=[VMEM] * (2 + heads),
        compiler_params=pltpu.CompilerParams(vmem_limit_bytes=4 << 20),
        name="prepare",
    )(where, *tables, q, k, v, rope_table())


def wide(x, width):
    return x if width == 128 else jnp.concatenate([x] * (width // 128), axis=1)


def flatten(refs, counts):
    return [ref.at[j] for ref, count in zip(refs, counts) for j in range(count)]


def score_kernel(nb, counts, place_ref, first_ref, grp_ref, *rest):
    sufs = rest[:nb]
    n_pieces = len(counts)
    pieces = flatten(rest[nb : nb + n_pieces], counts)
    p_ref, near_ref, den_ref, sc = rest[nb + n_pieces :]
    half = 256
    for n in range(nb):
        rows = sufs[n].shape[1]
        for b in range(rows // RB):
            r0 = b * RB
            t0 = n * rows + r0
            buf = (t0 // RB) % 2
            q = sufs[n][0, r0 : r0 + RB, :]
            grp = wide(grp_ref[t0 : t0 + RB, :], half)
            for d in range(SLOTS):
                g = place_ref[d] // OWNERS
                o = place_ref[d] % OWNERS
                for j in range(BLK // half):
                    s = lax.dot_general(
                        q,
                        pieces[d][j * half : (j + 1) * half, :],
                        (((1,), (1,)), ((), ())),
                        preferred_element_type=jnp.float32,
                    )
                    at = pl.ds(pl.multiple_of(o * BLK + j * half, half), half)
                    sc[buf, :, at] = jnp.where(grp == g, s, sc[buf, :, at])
            lo = max(0, r0 - MOST)
            width = r0 + RB - lo
            local = lax.dot_general(
                q,
                sufs[n][1, lo : r0 + RB, :],
                (((1,), (1,)), ((), ())),
                preferred_element_type=jnp.float32,
            )
            row = r0 + lax.broadcasted_iota(jnp.int32, (RB, width), 0)
            key = lo + lax.broadcasted_iota(jnp.int32, (RB, width), 1)
            start = wide(first_ref[t0 : t0 + RB, :], width)
            local = jnp.where((key <= row) & (key >= start), local, NEG_FILL)
            top = jnp.max(local, axis=1, keepdims=True)
            whole = sc[buf, :, 0:half]
            for c0 in range(half, SEEN, half):
                whole = jnp.maximum(whole, sc[buf, :, c0 : c0 + half])
            top = jnp.maximum(top, jnp.max(whole, axis=1, keepdims=True))
            e = jnp.exp2((local - top) * FACTOR)
            den = jnp.sum(e, axis=1, keepdims=True)
            near_ref[t0 : t0 + RB, 0:width] = e.astype(jnp.bfloat16)
            total = None
            for c0 in range(0, SEEN, half):
                e = jnp.exp2((sc[buf, :, c0 : c0 + half] - top) * FACTOR)
                p_ref[t0 : t0 + RB, c0 : c0 + half] = e.astype(jnp.bfloat16)
                total = e if total is None else total + e
            den = den + jnp.sum(total, axis=1, keepdims=True)
            den_ref[t0 : t0 + RB, :] = jnp.broadcast_to(den, (RB, 128))


def score(place, first, grp, sufs, pieces):
    rows = sum(s.shape[1] for s in sufs)
    return pl.pallas_call(
        functools.partial(score_kernel, len(sufs), tuple(p.shape[0] for p in pieces)),
        out_shape=[
            jax.ShapeDtypeStruct((rows, SEEN), jnp.bfloat16),
            jax.ShapeDtypeStruct((rows, RB + MOST), jnp.bfloat16),
            jax.ShapeDtypeStruct((rows, 128), jnp.float32),
        ],
        in_specs=[SMEM] + [VMEM] * (2 + len(sufs) + len(pieces)),
        out_specs=[VMEM] * 3,
        scratch_shapes=[pltpu.VMEM((2, RB, SEEN), jnp.float32)],
        compiler_params=pltpu.CompilerParams(vmem_limit_bytes=4 << 20),
        name="score",
    )(place, first, grp, *sufs, *pieces)


def mix_kernel(nb, base, counts, col, place_ref, grp_ref, p_ref, near_ref, den_ref, *rest):
    sufs = rest[:nb]
    n_pieces = len(counts)
    pieces = flatten(rest[nb : nb + n_pieces], counts)
    outs = rest[nb + n_pieces :]
    width = outs[0].shape[1]
    for n in reversed(range(nb)):
        rows = outs[n].shape[0]
        for b in range(rows // RB):
            r0 = b * RB
            t0 = base + n * rows + r0
            grp = wide(grp_ref[t0 : t0 + RB, :], width)
            lo = max(0, r0 - MOST)
            acc = jnp.dot(
                near_ref[t0 : t0 + RB, 0 : r0 + RB - lo],
                sufs[n][2, lo : r0 + RB, col : col + width],
                preferred_element_type=jnp.float32,
            )
            for d in range(SLOTS):
                g = place_ref[d] // OWNERS
                o = place_ref[d] % OWNERS
                part = jnp.dot(
                    p_ref[t0 : t0 + RB, pl.ds(pl.multiple_of(o * BLK, BLK), BLK)],
                    pieces[d][...],
                    preferred_element_type=jnp.float32,
                )
                acc = acc + jnp.where(grp == g, part, 0.0)
            den = wide(den_ref[t0 : t0 + RB, :], width)
            outs[n][r0 : r0 + RB, :] = (acc / den).astype(jnp.bfloat16)


def mix(col, width, place, grp, scored, sufs, pieces, base=0):
    rows = sufs[0].shape[1]
    nb = len(sufs)
    return pl.pallas_call(
        functools.partial(mix_kernel, nb, base, tuple(p.shape[0] for p in pieces), col),
        out_shape=[jax.ShapeDtypeStruct((rows, width), jnp.bfloat16)] * nb,
        in_specs=[SMEM] + [VMEM] * (4 + nb + len(pieces)),
        out_specs=[VMEM] * nb,
        compiler_params=pltpu.CompilerParams(vmem_limit_bytes=4 << 20),
        name="mix",
    )(place, grp, *scored, *sufs, *pieces)


def proj_kernel(steps, last, where_ref, *refs):
    att = refs[: 2 * len(steps)]
    own, *far = refs[2 * len(steps) : 2 * len(steps) + 5]
    o_ref = refs[-1]
    cols = o_ref.shape[1] // 2
    rows = o_ref.shape[0]
    core = where_ref[1]
    side = where_ref[2]
    tall = 256
    for r0 in range(0, rows, tall):
        at = slice(r0, r0 + tall)
        for x in range(2):
            c = pl.ds(pl.multiple_of(lax.bitwise_xor(side, x) * cols, cols), cols)
            acc = refs[-2][at, c] if last else jnp.zeros((tall, cols), jnp.float32)
            for h in range(2):
                head = lax.bitwise_xor(core, h)
                lines = []
                for i, m in enumerate(steps):
                    lines.append((m, att[h * len(steps) + i][at, :]))
                if last:
                    lines = [(3, lines[0][1] + lines[1][1])]
                for m, a in lines:
                    if m == 0:
                        w = own[pl.ds(pl.multiple_of(head * HD, HD), HD), c]
                    else:
                        w = far[2 * h + x][m - 1]
                    acc = acc + jnp.dot(a, w, preferred_element_type=jnp.float32)
            o_ref[at, c] = acc.astype(o_ref.dtype)


def project(where, steps, att, own, far, add=None):
    rows = att[0].shape[0]
    cols = own.shape[1]
    extra = [] if add is None else [add]
    return pl.pallas_call(
        functools.partial(proj_kernel, steps, add is not None),
        out_shape=jax.ShapeDtypeStruct((rows, cols), jnp.float32 if add is None else jnp.bfloat16),
        in_specs=[SMEM] + [VMEM] * (len(att) + 1 + len(far) + len(extra)),
        out_specs=VMEM,
        compiler_params=pltpu.CompilerParams(vmem_limit_bytes=6 << 20),
        name="project",
    )(where, *att, own, *far, *extra)


def swap(x, axis, mask, size):
    return lax.ppermute(x, axis, [(i, i ^ mask) for i in range(size)])


def after(x, *deps):
    return lax.optimization_barrier((x,) + deps)[0]


over_x = functools.partial(swap, axis="req", mask=2, size=8)
over_y = functools.partial(swap, axis="req", mask=4, size=8)
over_core = functools.partial(swap, axis="req", mask=1, size=8)


def split_heads(suffix_heads, prefix_cache, lengths, groups, owners, out_weight):
    rows = suffix_heads.shape[0]
    me = lax.axis_index("req")
    z = lax.axis_index("tp")
    core = me & 1
    side = (me >> 1) & 1
    where = jnp.stack([z, core, side]).astype(jnp.int32)
    place = jnp.sum(
        jnp.where(
            owners[None] == (me ^ jnp.arange(SLOTS, dtype=jnp.int32))[:, None, None],
            jnp.arange(SLOTS, dtype=jnp.int32).reshape(1, GROUPS, OWNERS),
            0,
        ),
        axis=(1, 2),
    ).astype(jnp.int32)
    tp_size = 4
    first_head = core == 0

    cols = out_weight.shape[1] // tp_size
    z_u, core_u, side_u = (i.astype(jnp.uint32) for i in (z, core, side))
    starts = [core_u * HD, z_u * cols]
    starts += [(z_u ^ m) * cols + side_u * (cols // 2) for m in range(1, tp_size)]
    first_head, *starts = lax.optimization_barrier((first_head, *starts))
    sends = [
        lax.dynamic_slice(out_weight, (starts[0], starts[1 + m]), (HD, cols // 2))
        for m in range(1, tp_size)
    ]
    w_own = lax.dynamic_slice(
        out_weight, (jnp.zeros_like(starts[0]), starts[1]), (out_weight.shape[0], cols)
    )

    k = prefix_cache[:, 0]
    k_own = jnp.where(first_head, k[:, :HD], k[:, HD:])
    k_other = jnp.where(first_head, k[:, HD:], k[:, :HD])
    k_both = jnp.stack([k_own, over_core(k_other)])
    kx = over_x(k_both)
    ky = over_y(k_both)
    w_one, w_two = (swap(sends[m - 1], "tp", m, tp_size) for m in (1, 2))

    table = jnp.concatenate([lengths, groups], axis=0)
    table_pair = over_core(table)
    suffix = after(suffix_heads, k_both)
    first, grp, mine, other = prepare(
        after(where, k_both), (table, table_pair), suffix[:, 0], suffix[:, 1], suffix[:, 2]
    )
    sufs = [mine, over_core(other)]
    v = after(prefix_cache, k_both)[:, 1]
    v_own = jnp.where(first_head, v[:, :HD], v[:, HD:])
    v_other = jnp.where(first_head, v[:, HD:], v[:, :HD])
    v_both = jnp.stack([v_own, over_core(v_other)])

    kxy = over_y(after(kx[0:1], mine, v_both))
    kyx = over_x(after(ky[1:2], mine, v_both))
    v_both = after(v_both, kxy, kyx, w_one, w_two, w_own, sufs[1])
    vx = over_x(v_both)
    vy = over_y(v_both)
    w_three = swap(after(sends[2], w_two), "tp", 3, tp_size)
    scored = score(place, first, grp, sufs, (k_both, kx, ky, kxy, kyx))
    w_far = jnp.stack([after(w_one, scored[0]), w_two, w_three])
    w_core = over_core(w_far)
    vxy = over_y(after(vx[0:1], scored[0], w_far))
    vyx = over_x(after(vy[1:2], scored[0], w_far))
    v_pieces = (v_both, vx, vy, vxy, vyx)
    (own,) = mix(0, HD, place, grp, scored, sufs[:1], v_pieces)
    (pair,) = mix(0, HD, place, grp, scored, sufs[1:], v_pieces, rows)
    w_x = over_x(after(w_far, vxy, vyx))

    back = over_core(pair)
    two_own = swap(own, "tp", 2, tp_size)
    one_own = swap(own, "tp", 1, tp_size)
    later = after(back, two_own, one_own)
    two_back = swap(later, "tp", 2, tp_size)
    one_back = swap(later, "tp", 1, tp_size)
    three_own = lax.ppermute(after(own, two_own), "tp", [(1, 2), (2, 1)])
    forward_own = lax.ppermute(two_own, "tp", [(2, 3), (1, 0)])
    three_back = lax.ppermute(after(later, two_back), "tp", [(1, 2), (2, 1)])
    forward_back = lax.ppermute(two_back, "tp", [(2, 3), (1, 0)])
    w_core_x = over_core(after(w_x, two_back, one_back, three_own, forward_own))
    far = [w_far, w_x, w_core, w_core_x]
    near = project(where, (0, 1, 2), (own, one_own, two_own, back, one_back, two_back), w_own, far)
    last = (three_own, forward_own, three_back, forward_back)
    return project(where, (3, 3), last, w_own, far, near)


def whole_heads(suffix_heads, prefix_cache, lengths, groups, owners, out_weight):
    heads = suffix_heads.shape[2] // HD
    received = [
        from_root(prefix_cache, "req", owners[i // OWNERS, i % OWNERS]) for i in range(SLOTS)
    ]
    place = jnp.arange(SLOTS, dtype=jnp.int32)
    first, grp, *sufs = prepare(
        jnp.zeros((3,), jnp.int32),
        (jnp.concatenate([lengths, groups], axis=0),),
        suffix_heads[:, 0],
        suffix_heads[:, 1],
        suffix_heads[:, 2],
    )
    attended = []
    for h in range(heads):
        keys = [s[None, :, 0, h * HD : (h + 1) * HD] for s in received]
        values = [s[None, :, 1, h * HD : (h + 1) * HD] for s in received]
        scored = score(place, first, grp, [sufs[h]], keys)
        attended += mix(0, HD, place, grp, scored, [sufs[h]], values)
    partial_out = jnp.dot(
        jnp.concatenate(attended, axis=1), out_weight, preferred_element_type=jnp.float32
    )
    return lax.psum_scatter(partial_out.astype(jnp.bfloat16), "tp", scatter_dimension=1, tiled=True)


def per_device(req_size, tp_size, *args):
    if req_size == 8 and tp_size == 4 and args[0].shape[2] == 2 * HD:
        return split_heads(*args)
    return whole_heads(*args)


def solution(mesh):
    placed = (
        P("req", None, "tp"),
        P("req", None, "tp"),
        P("req", None),
        P("req", None),
        P(),
        P("tp", None),
    )
    return jax.shard_map(
        functools.partial(per_device, mesh.shape["req"], mesh.shape["tp"]),
        mesh=mesh,
        in_specs=placed,
        out_specs=P("req", "tp"),
        check_vma=False,
    )
```

```python
import functools
import jax
import jax.numpy as jnp
import numpy as np
from jax import lax
from jax.experimental import pallas as pl
from jax.experimental.pallas import tpu as pltpu
from jax.sharding import PartitionSpec as P

HD = 256
ROT = 64
BLK = 512
OWNERS = 2
GROUPS = 4
SLOTS = GROUPS * OWNERS
MOST = 128
SEEN = OWNERS * BLK

NEG_FILL = -1e30
ROPE_BASE = 10000.0
FACTOR = HD ** (-0.5) * 1.4426950408889634

RB = 128

VMEM = pl.BlockSpec(memory_space=pltpu.VMEM)
SMEM = pl.BlockSpec(memory_space=pltpu.SMEM)


def from_root(x, axis, root):
    mine = lax.axis_index(axis) == root
    return lax.psum(jnp.where(mine, x, jnp.zeros_like(x)), axis)


def rope_table():
    inverse = np.float32(ROPE_BASE) ** (-2.0 * np.arange(ROT // 2, dtype=np.float32) / ROT)
    inverse = np.concatenate([np.repeat(inverse, 2), np.zeros(128 - ROT)]).astype(np.float32)
    angles = np.arange(SEEN, SEEN + MOST, dtype=np.float32)[:, None] * inverse[None, :]
    angles = angles.astype(np.float64)
    sign = np.where(np.arange(128) % 2 == 0, -1.0, 1.0)
    table = np.concatenate([np.cos(angles), np.sin(angles) * sign[None, :]], axis=1)
    return jnp.asarray(table.astype(np.float32))


def prep_kernel(spans, where_ref, *refs):
    tables = refs[:spans]
    q_ref, k_ref, v_ref, rope_ref = refs[spans : spans + 4]
    first_ref, grp_ref = refs[spans + 4 : spans + 6]
    o_refs = refs[spans + 6 :]
    rows = q_ref.shape[0]
    heads = len(o_refs)
    lane = lax.broadcasted_iota(jnp.int32, (RB, 128), 1)
    even = (lane % 2) == 0
    for n in range(spans):
        requests = tables[n].shape[1]
        for r0 in range(0, rows, RB):
            row = r0 + lax.broadcasted_iota(jnp.int32, (RB, 128), 0)
            start = jnp.int32(0)
            first = jnp.zeros((RB, 128), jnp.int32)
            grp = jnp.zeros((RB, 128), jnp.int32) + tables[n][1, 0]
            for r in range(1, requests):
                start = start + tables[n][0, r - 1]
                later = row >= start
                first = jnp.where(later, start, first)
                grp = jnp.where(later, tables[n][1, r], grp)
            first_ref[n * rows + r0 : n * rows + r0 + RB, :] = first
            grp_ref[n * rows + r0 : n * rows + r0 + RB, :] = grp
    for r0 in range(0, rows, RB):
        at = slice(r0, r0 + RB)
        row = r0 + lax.broadcasted_iota(jnp.int32, (RB, 128), 0)
        chosen = jnp.where(row - first_ref[at, :] == lane, 1.0, 0.0)
        turn = lax.dot_general(
            chosen,
            rope_ref[...],
            (((1,), (0,)), ((), ())),
            precision=lax.Precision.HIGHEST,
            preferred_element_type=jnp.float32,
        )
        cos = turn[:, :128]
        sin = turn[:, 128:]
        for i, o_ref in enumerate(o_refs):
            flip = where_ref[1] > 0
            for n, ref in enumerate((q_ref, k_ref)):
                x = ref[at, i * HD : (i + 1) * HD]
                if heads == 2:
                    x = jnp.where(flip, ref[at, (1 - i) * HD : (2 - i) * HD], x)
                y = x[:, :128].astype(jnp.float32)
                swapped = jnp.where(even, pltpu.roll(y, 127, 1), pltpu.roll(y, 1, 1))
                o_ref[n, at, 0:128] = (y * cos + swapped * sin).astype(jnp.bfloat16)
                o_ref[n, at, 128:HD] = x[:, 128:]
            v = v_ref[at, i * HD : (i + 1) * HD]
            if heads == 2:
                v = jnp.where(flip, v_ref[at, (1 - i) * HD : (2 - i) * HD], v)
            o_ref[2, at, :] = v


def prepare(where, tables, q, k, v):
    rows, feat = q.shape
    heads = feat // HD
    spans = len(tables)
    column = jax.ShapeDtypeStruct((spans * rows, 128), jnp.int32)
    return pl.pallas_call(
        functools.partial(prep_kernel, spans),
        out_shape=[column] * 2 + [jax.ShapeDtypeStruct((3, rows, HD), jnp.bfloat16)] * heads,
        in_specs=[SMEM] * (1 + spans) + [VMEM] * 4,
        out_specs=[VMEM] * (2 + heads),
        compiler_params=pltpu.CompilerParams(vmem_limit_bytes=4 << 20),
        name="prepare",
    )(where, *tables, q, k, v, rope_table())


def wide(x, width):
    return x if width == 128 else jnp.concatenate([x] * (width // 128), axis=1)


def flatten(refs, counts):
    return [ref.at[j] for ref, count in zip(refs, counts) for j in range(count)]


def score_kernel(nb, counts, place_ref, first_ref, grp_ref, *rest):
    sufs = rest[:nb]
    n_pieces = len(counts)
    pieces = flatten(rest[nb : nb + n_pieces], counts)
    p_ref, near_ref, den_ref, sc = rest[nb + n_pieces :]
    half = 256
    for n in range(nb):
        rows = sufs[n].shape[1]
        for b in range(rows // RB):
            r0 = b * RB
            t0 = n * rows + r0
            buf = (t0 // RB) % 2
            q = sufs[n][0, r0 : r0 + RB, :]
            grp = wide(grp_ref[t0 : t0 + RB, :], half)
            for d in range(SLOTS):
                g = place_ref[d] // OWNERS
                o = place_ref[d] % OWNERS
                for j in range(BLK // half):
                    s = lax.dot_general(
                        q,
                        pieces[d][j * half : (j + 1) * half, :],
                        (((1,), (1,)), ((), ())),
                        preferred_element_type=jnp.float32,
                    )
                    at = pl.ds(pl.multiple_of(o * BLK + j * half, half), half)
                    sc[buf, :, at] = jnp.where(grp == g, s, sc[buf, :, at])
            lo = max(0, r0 - MOST)
            width = r0 + RB - lo
            local = lax.dot_general(
                q,
                sufs[n][1, lo : r0 + RB, :],
                (((1,), (1,)), ((), ())),
                preferred_element_type=jnp.float32,
            )
            row = r0 + lax.broadcasted_iota(jnp.int32, (RB, width), 0)
            key = lo + lax.broadcasted_iota(jnp.int32, (RB, width), 1)
            start = wide(first_ref[t0 : t0 + RB, :], width)
            local = jnp.where((key <= row) & (key >= start), local, NEG_FILL)
            top = jnp.max(local, axis=1, keepdims=True)
            whole = sc[buf, :, 0:half]
            for c0 in range(half, SEEN, half):
                whole = jnp.maximum(whole, sc[buf, :, c0 : c0 + half])
            top = jnp.maximum(top, jnp.max(whole, axis=1, keepdims=True))
            e = jnp.exp2((local - top) * FACTOR)
            den = jnp.sum(e, axis=1, keepdims=True)
            near_ref[t0 : t0 + RB, 0:width] = e.astype(jnp.bfloat16)
            total = None
            for c0 in range(0, SEEN, half):
                e = jnp.exp2((sc[buf, :, c0 : c0 + half] - top) * FACTOR)
                p_ref[t0 : t0 + RB, c0 : c0 + half] = e.astype(jnp.bfloat16)
                total = e if total is None else total + e
            den = den + jnp.sum(total, axis=1, keepdims=True)
            den_ref[t0 : t0 + RB, :] = jnp.broadcast_to(den, (RB, 128))


def score(place, first, grp, sufs, pieces):
    rows = sum(s.shape[1] for s in sufs)
    return pl.pallas_call(
        functools.partial(score_kernel, len(sufs), tuple(p.shape[0] for p in pieces)),
        out_shape=[
            jax.ShapeDtypeStruct((rows, SEEN), jnp.bfloat16),
            jax.ShapeDtypeStruct((rows, RB + MOST), jnp.bfloat16),
            jax.ShapeDtypeStruct((rows, 128), jnp.float32),
        ],
        in_specs=[SMEM] + [VMEM] * (2 + len(sufs) + len(pieces)),
        out_specs=[VMEM] * 3,
        scratch_shapes=[pltpu.VMEM((2, RB, SEEN), jnp.float32)],
        compiler_params=pltpu.CompilerParams(vmem_limit_bytes=4 << 20),
        name="score",
    )(place, first, grp, *sufs, *pieces)


def mix_kernel(nb, base, counts, col, place_ref, grp_ref, p_ref, near_ref, den_ref, *rest):
    sufs = rest[:nb]
    n_pieces = len(counts)
    pieces = flatten(rest[nb : nb + n_pieces], counts)
    outs = rest[nb + n_pieces :]
    width = outs[0].shape[1]
    for n in reversed(range(nb)):
        rows = outs[n].shape[0]
        for b in range(rows // RB):
            r0 = b * RB
            t0 = base + n * rows + r0
            grp = wide(grp_ref[t0 : t0 + RB, :], width)
            lo = max(0, r0 - MOST)
            acc = jnp.dot(
                near_ref[t0 : t0 + RB, 0 : r0 + RB - lo],
                sufs[n][2, lo : r0 + RB, col : col + width],
                preferred_element_type=jnp.float32,
            )
            for d in range(SLOTS):
                g = place_ref[d] // OWNERS
                o = place_ref[d] % OWNERS
                part = jnp.dot(
                    p_ref[t0 : t0 + RB, pl.ds(pl.multiple_of(o * BLK, BLK), BLK)],
                    pieces[d][...],
                    preferred_element_type=jnp.float32,
                )
                acc = acc + jnp.where(grp == g, part, 0.0)
            den = wide(den_ref[t0 : t0 + RB, :], width)
            outs[n][r0 : r0 + RB, :] = (acc / den).astype(jnp.bfloat16)


def mix(col, width, place, grp, scored, sufs, pieces, base=0):
    rows = sufs[0].shape[1]
    nb = len(sufs)
    return pl.pallas_call(
        functools.partial(mix_kernel, nb, base, tuple(p.shape[0] for p in pieces), col),
        out_shape=[jax.ShapeDtypeStruct((rows, width), jnp.bfloat16)] * nb,
        in_specs=[SMEM] + [VMEM] * (4 + nb + len(pieces)),
        out_specs=[VMEM] * nb,
        compiler_params=pltpu.CompilerParams(vmem_limit_bytes=4 << 20),
        name="mix",
    )(place, grp, *scored, *sufs, *pieces)


def proj_kernel(steps, last, where_ref, *refs):
    att = refs[: 2 * len(steps)]
    own, *far = refs[2 * len(steps) : 2 * len(steps) + 3]
    o_ref = refs[-1]
    cols = o_ref.shape[1] // 4
    core = where_ref[1]
    for x in range(4):
        c = pl.ds(pl.multiple_of(lax.bitwise_xor(where_ref[2], x) * cols, cols), cols)
        acc = refs[-2][:, c] if last else jnp.zeros((o_ref.shape[0], cols), jnp.float32)
        for h in range(2):
            head = lax.bitwise_xor(core, h)
            lines = [(m, att[h * len(steps) + i][...]) for i, m in enumerate(steps)]
            if last:
                lines = [(3, lines[0][1] + lines[1][1])]
            for m, a in lines:
                if m == 0:
                    w = own[pl.ds(pl.multiple_of(head * HD, HD), HD), c]
                else:
                    w = far[h][3 * x + m - 1]
                acc = acc + jnp.dot(a, w, preferred_element_type=jnp.float32)
        o_ref[:, c] = acc.astype(o_ref.dtype)


def project(where, steps, att, own, far, add=None):
    rows = att[0].shape[0]
    cols = own.shape[1]
    extra = [] if add is None else [add]
    return pl.pallas_call(
        functools.partial(proj_kernel, steps, add is not None),
        out_shape=jax.ShapeDtypeStruct((rows, cols), jnp.float32 if add is None else jnp.bfloat16),
        in_specs=[SMEM] + [VMEM] * (len(att) + 1 + len(far) + len(extra)),
        out_specs=VMEM,
        compiler_params=pltpu.CompilerParams(vmem_limit_bytes=6 << 20),
        name="project",
    )(where, *att, own, *far, *extra)


def swap(x, axis, mask, size):
    return lax.ppermute(x, axis, [(i, i ^ mask) for i in range(size)])


def after(x, *deps):
    return lax.optimization_barrier((x,) + deps)[0]


over_x = functools.partial(swap, axis="req", mask=2, size=8)
over_y = functools.partial(swap, axis="req", mask=4, size=8)
over_core = functools.partial(swap, axis="req", mask=1, size=8)


def split_heads(suffix_heads, prefix_cache, lengths, groups, owners, out_weight):
    rows = suffix_heads.shape[0]
    me = lax.axis_index("req")
    z = lax.axis_index("tp")
    core = me & 1
    chip = me >> 1
    where = jnp.stack([z, core, chip]).astype(jnp.int32)
    place = jnp.sum(
        jnp.where(
            owners[None] == (me ^ jnp.arange(SLOTS, dtype=jnp.int32))[:, None, None],
            jnp.arange(SLOTS, dtype=jnp.int32).reshape(1, GROUPS, OWNERS),
            0,
        ),
        axis=(1, 2),
    ).astype(jnp.int32)
    tp_size = 4
    first_head = core == 0

    cols = out_weight.shape[1] // tp_size
    z_u, core_u, chip_u = (i.astype(jnp.uint32) for i in (z, core, chip))
    starts = [core_u * HD, z_u * cols]
    starts += [(z_u ^ m) * cols + chip_u * (cols // 4) for m in range(1, tp_size)]
    first_head, *starts = lax.optimization_barrier((first_head, *starts))
    sends = [
        lax.dynamic_slice(out_weight, (starts[0], starts[1 + m]), (HD, cols // 4))
        for m in range(1, tp_size)
    ]
    w_own = lax.dynamic_slice(
        out_weight, (jnp.zeros_like(starts[0]), starts[1]), (out_weight.shape[0], cols)
    )

    k = prefix_cache[:, 0]
    k_own = jnp.where(first_head, k[:, :HD], k[:, HD:])
    k_other = jnp.where(first_head, k[:, HD:], k[:, :HD])
    k_both = jnp.stack([k_own, over_core(k_other)])
    kx = over_x(k_both)
    ky = over_y(k_both)
    w_one, w_two, w_three = (swap(sends[m - 1], "tp", m, tp_size) for m in (1, 2, 3))

    table = jnp.concatenate([lengths, groups], axis=0)
    table_pair = over_core(table)
    suffix = after(suffix_heads, k_both)
    first, grp, mine, other = prepare(
        after(where, k_both), (table, table_pair), suffix[:, 0], suffix[:, 1], suffix[:, 2]
    )
    sufs = [mine, over_core(other)]
    v = after(prefix_cache, k_both)[:, 1]
    v_own = jnp.where(first_head, v[:, :HD], v[:, HD:])
    v_other = jnp.where(first_head, v[:, HD:], v[:, :HD])
    v_both = jnp.stack([v_own, over_core(v_other)])

    kxy = over_y(after(kx[0:1], mine, v_both))
    kyx = over_x(after(ky[1:2], mine, v_both))
    v_both = after(v_both, kxy, kyx, w_one, w_two, w_three, w_own, sufs[1])
    vx = over_x(v_both)
    vy = over_y(v_both)
    scored = score(place, first, grp, sufs, (k_both, kx, ky, kxy, kyx))
    w_far = jnp.stack([after(w_one, scored[0]), w_two, w_three])
    vxy = over_y(after(vx[0:1], scored[0], w_far))
    vyx = over_x(after(vy[1:2], scored[0], w_far))
    v_pieces = (v_both, vx, vy, vxy, vyx)
    (own,) = mix(0, HD, place, grp, scored, sufs[:1], v_pieces)
    (pair,) = mix(0, HD, place, grp, scored, sufs[1:], v_pieces, rows)
    w_x = over_x(after(w_far, vxy, vyx))
    w_y = over_y(after(w_far, vxy, vyx))

    back = over_core(pair)
    two_own = swap(own, "tp", 2, tp_size)
    one_own = swap(own, "tp", 1, tp_size)
    later = after(back, two_own)
    two_back = swap(later, "tp", 2, tp_size)
    one_back = swap(later, "tp", 1, tp_size)
    three_own = lax.ppermute(after(own, two_own, one_own), "tp", [(1, 2), (2, 1)])
    forward_own = lax.ppermute(two_own, "tp", [(2, 3), (1, 0)])
    three_back = lax.ppermute(after(later, two_back), "tp", [(1, 2), (2, 1)])
    forward_back = lax.ppermute(two_back, "tp", [(2, 3), (1, 0)])
    w_xy = over_y(after(w_x, two_own, one_own))
    w_chips = jnp.concatenate([w_far, w_x, w_y, w_xy])
    w_core = over_core(after(w_chips, two_back, one_back, three_own, forward_own))
    far = [w_chips, w_core]
    near = project(where, (0, 1, 2), (own, one_own, two_own, back, one_back, two_back), w_own, far)
    last = (three_own, forward_own, three_back, forward_back)
    return project(where, (3, 3), last, w_own, far, near)


def whole_heads(suffix_heads, prefix_cache, lengths, groups, owners, out_weight):
    heads = suffix_heads.shape[2] // HD
    received = [
        from_root(prefix_cache, "req", owners[i // OWNERS, i % OWNERS]) for i in range(SLOTS)
    ]
    place = jnp.arange(SLOTS, dtype=jnp.int32)
    first, grp, *sufs = prepare(
        jnp.zeros((3,), jnp.int32),
        (jnp.concatenate([lengths, groups], axis=0),),
        suffix_heads[:, 0],
        suffix_heads[:, 1],
        suffix_heads[:, 2],
    )
    attended = []
    for h in range(heads):
        keys = [s[None, :, 0, h * HD : (h + 1) * HD] for s in received]
        values = [s[None, :, 1, h * HD : (h + 1) * HD] for s in received]
        scored = score(place, first, grp, [sufs[h]], keys)
        attended += mix(0, HD, place, grp, scored, [sufs[h]], values)
    partial_out = jnp.dot(
        jnp.concatenate(attended, axis=1), out_weight, preferred_element_type=jnp.float32
    )
    return lax.psum_scatter(partial_out.astype(jnp.bfloat16), "tp", scatter_dimension=1, tiled=True)


def per_device(req_size, tp_size, *args):
    if req_size == 8 and tp_size == 4 and args[0].shape[2] == 2 * HD:
        return split_heads(*args)
    return whole_heads(*args)


def solution(mesh):
    placed = (
        P("req", None, "tp"),
        P("req", None, "tp"),
        P("req", None),
        P("req", None),
        P(),
        P("tp", None),
    )
    return jax.shard_map(
        functools.partial(per_device, mesh.shape["req"], mesh.shape["tp"]),
        mesh=mesh,
        in_specs=placed,
        out_specs=P("req", "tp"),
        check_vma=False,
    )
```

```python
import functools
import jax
import jax.numpy as jnp
import numpy as np
from jax import lax
from jax.experimental import pallas as pl
from jax.experimental.pallas import tpu as pltpu
from jax.sharding import PartitionSpec as P

HD = 256
ROT = 64
BLK = 512
OWNERS = 2
GROUPS = 4
SLOTS = GROUPS * OWNERS
MOST = 128
SEEN = OWNERS * BLK

NEG_FILL = -1e30
ROPE_BASE = 10000.0
FACTOR = HD ** (-0.5) * 1.4426950408889634

RB = 128

VMEM = pl.BlockSpec(memory_space=pltpu.VMEM)
SMEM = pl.BlockSpec(memory_space=pltpu.SMEM)


def from_root(x, axis, root):
    mine = lax.axis_index(axis) == root
    return lax.psum(jnp.where(mine, x, jnp.zeros_like(x)), axis)


def rope_table():
    inverse = np.float32(ROPE_BASE) ** (-2.0 * np.arange(ROT // 2, dtype=np.float32) / ROT)
    inverse = np.concatenate([np.repeat(inverse, 2), np.zeros(128 - ROT)]).astype(np.float32)
    angles = np.arange(SEEN, SEEN + MOST, dtype=np.float32)[:, None] * inverse[None, :]
    angles = angles.astype(np.float64)
    sign = np.where(np.arange(128) % 2 == 0, -1.0, 1.0)
    table = np.concatenate([np.cos(angles), np.sin(angles) * sign[None, :]], axis=1)
    return jnp.asarray(table.astype(np.float32))


def prep_kernel(spans, where_ref, *refs):
    tables = refs[:spans]
    q_ref, k_ref, v_ref, rope_ref = refs[spans : spans + 4]
    first_ref, grp_ref = refs[spans + 4 : spans + 6]
    o_refs = refs[spans + 6 :]
    rows = q_ref.shape[0]
    heads = len(o_refs)
    lane = lax.broadcasted_iota(jnp.int32, (RB, 128), 1)
    even = (lane % 2) == 0
    for n in range(spans):
        requests = tables[n].shape[1]
        for r0 in range(0, rows, RB):
            row = r0 + lax.broadcasted_iota(jnp.int32, (RB, 128), 0)
            start = jnp.int32(0)
            first = jnp.zeros((RB, 128), jnp.int32)
            grp = jnp.zeros((RB, 128), jnp.int32) + tables[n][1, 0]
            for r in range(1, requests):
                start = start + tables[n][0, r - 1]
                later = row >= start
                first = jnp.where(later, start, first)
                grp = jnp.where(later, tables[n][1, r], grp)
            first_ref[n * rows + r0 : n * rows + r0 + RB, :] = first
            grp_ref[n * rows + r0 : n * rows + r0 + RB, :] = grp
    for r0 in range(0, rows, RB):
        at = slice(r0, r0 + RB)
        row = r0 + lax.broadcasted_iota(jnp.int32, (RB, 128), 0)
        chosen = jnp.where(row - first_ref[at, :] == lane, 1.0, 0.0)
        turn = lax.dot_general(
            chosen,
            rope_ref[...],
            (((1,), (0,)), ((), ())),
            precision=lax.Precision.HIGHEST,
            preferred_element_type=jnp.float32,
        )
        cos = turn[:, :128]
        sin = turn[:, 128:]
        for i, o_ref in enumerate(o_refs):
            flip = where_ref[1] > 0
            for n, ref in enumerate((q_ref, k_ref)):
                x = ref[at, i * HD : (i + 1) * HD]
                if heads == 2:
                    x = jnp.where(flip, ref[at, (1 - i) * HD : (2 - i) * HD], x)
                y = x[:, :128].astype(jnp.float32)
                swapped = jnp.where(even, pltpu.roll(y, 127, 1), pltpu.roll(y, 1, 1))
                o_ref[n, at, 0:128] = (y * cos + swapped * sin).astype(jnp.bfloat16)
                o_ref[n, at, 128:HD] = x[:, 128:]
            v = v_ref[at, i * HD : (i + 1) * HD]
            if heads == 2:
                v = jnp.where(flip, v_ref[at, (1 - i) * HD : (2 - i) * HD], v)
            o_ref[2, at, :] = v


def prepare(where, tables, q, k, v):
    rows, feat = q.shape
    heads = feat // HD
    spans = len(tables)
    column = jax.ShapeDtypeStruct((spans * rows, 128), jnp.int32)
    return pl.pallas_call(
        functools.partial(prep_kernel, spans),
        out_shape=[column] * 2 + [jax.ShapeDtypeStruct((3, rows, HD), jnp.bfloat16)] * heads,
        in_specs=[SMEM] * (1 + spans) + [VMEM] * 4,
        out_specs=[VMEM] * (2 + heads),
        compiler_params=pltpu.CompilerParams(vmem_limit_bytes=4 << 20),
        name="prepare",
    )(where, *tables, q, k, v, rope_table())


def wide(x, width):
    return x if width == 128 else jnp.concatenate([x] * (width // 128), axis=1)


def flatten(refs, counts):
    return [ref.at[j] for ref, count in zip(refs, counts) for j in range(count)]


def score_kernel(nb, counts, place_ref, first_ref, grp_ref, *rest):
    sufs = rest[:nb]
    n_pieces = len(counts)
    pieces = flatten(rest[nb : nb + n_pieces], counts)
    p_ref, near_ref, den_ref, sc = rest[nb + n_pieces :]
    half = 256
    for n in range(nb):
        rows = sufs[n].shape[1]
        for b in range(rows // RB):
            r0 = b * RB
            t0 = n * rows + r0
            buf = (t0 // RB) % 2
            q = sufs[n][0, r0 : r0 + RB, :]
            grp = wide(grp_ref[t0 : t0 + RB, :], half)
            for d in range(SLOTS):
                g = place_ref[d] // OWNERS
                o = place_ref[d] % OWNERS
                for j in range(BLK // half):
                    s = lax.dot_general(
                        q,
                        pieces[d][j * half : (j + 1) * half, :],
                        (((1,), (1,)), ((), ())),
                        preferred_element_type=jnp.float32,
                    )
                    at = pl.ds(pl.multiple_of(o * BLK + j * half, half), half)
                    sc[buf, :, at] = jnp.where(grp == g, s, sc[buf, :, at])
            lo = max(0, r0 - MOST)
            width = r0 + RB - lo
            local = lax.dot_general(
                q,
                sufs[n][1, lo : r0 + RB, :],
                (((1,), (1,)), ((), ())),
                preferred_element_type=jnp.float32,
            )
            row = r0 + lax.broadcasted_iota(jnp.int32, (RB, width), 0)
            key = lo + lax.broadcasted_iota(jnp.int32, (RB, width), 1)
            start = wide(first_ref[t0 : t0 + RB, :], width)
            local = jnp.where((key <= row) & (key >= start), local, NEG_FILL)
            top = jnp.max(local, axis=1, keepdims=True)
            whole = sc[buf, :, 0:half]
            for c0 in range(half, SEEN, half):
                whole = jnp.maximum(whole, sc[buf, :, c0 : c0 + half])
            top = jnp.maximum(top, jnp.max(whole, axis=1, keepdims=True))
            e = jnp.exp2((local - top) * FACTOR)
            den = jnp.sum(e, axis=1, keepdims=True)
            near_ref[t0 : t0 + RB, 0:width] = e.astype(jnp.bfloat16)
            total = None
            for c0 in range(0, SEEN, half):
                e = jnp.exp2((sc[buf, :, c0 : c0 + half] - top) * FACTOR)
                p_ref[t0 : t0 + RB, c0 : c0 + half] = e.astype(jnp.bfloat16)
                total = e if total is None else total + e
            den = den + jnp.sum(total, axis=1, keepdims=True)
            den_ref[t0 : t0 + RB, :] = jnp.broadcast_to(den, (RB, 128))


def score(place, first, grp, sufs, pieces):
    rows = sum(s.shape[1] for s in sufs)
    return pl.pallas_call(
        functools.partial(score_kernel, len(sufs), tuple(p.shape[0] for p in pieces)),
        out_shape=[
            jax.ShapeDtypeStruct((rows, SEEN), jnp.bfloat16),
            jax.ShapeDtypeStruct((rows, RB + MOST), jnp.bfloat16),
            jax.ShapeDtypeStruct((rows, 128), jnp.float32),
        ],
        in_specs=[SMEM] + [VMEM] * (2 + len(sufs) + len(pieces)),
        out_specs=[VMEM] * 3,
        scratch_shapes=[pltpu.VMEM((2, RB, SEEN), jnp.float32)],
        compiler_params=pltpu.CompilerParams(vmem_limit_bytes=4 << 20),
        name="score",
    )(place, first, grp, *sufs, *pieces)


def mix_kernel(nb, base, counts, col, place_ref, grp_ref, p_ref, near_ref, den_ref, *rest):
    sufs = rest[:nb]
    n_pieces = len(counts)
    pieces = flatten(rest[nb : nb + n_pieces], counts)
    outs = rest[nb + n_pieces :]
    width = outs[0].shape[1]
    for n in reversed(range(nb)):
        rows = outs[n].shape[0]
        for b in range(rows // RB):
            r0 = b * RB
            t0 = base + n * rows + r0
            grp = wide(grp_ref[t0 : t0 + RB, :], width)
            lo = max(0, r0 - MOST)
            acc = jnp.dot(
                near_ref[t0 : t0 + RB, 0 : r0 + RB - lo],
                sufs[n][2, lo : r0 + RB, col : col + width],
                preferred_element_type=jnp.float32,
            )
            for d in range(SLOTS):
                g = place_ref[d] // OWNERS
                o = place_ref[d] % OWNERS
                part = jnp.dot(
                    p_ref[t0 : t0 + RB, pl.ds(pl.multiple_of(o * BLK, BLK), BLK)],
                    pieces[d][...],
                    preferred_element_type=jnp.float32,
                )
                acc = acc + jnp.where(grp == g, part, 0.0)
            den = wide(den_ref[t0 : t0 + RB, :], width)
            outs[n][r0 : r0 + RB, :] = (acc / den).astype(jnp.bfloat16)


def mix(col, width, place, grp, scored, sufs, pieces, base=0):
    rows = sufs[0].shape[1]
    nb = len(sufs)
    return pl.pallas_call(
        functools.partial(mix_kernel, nb, base, tuple(p.shape[0] for p in pieces), col),
        out_shape=[jax.ShapeDtypeStruct((rows, width), jnp.bfloat16)] * nb,
        in_specs=[SMEM] + [VMEM] * (4 + nb + len(pieces)),
        out_specs=[VMEM] * nb,
        compiler_params=pltpu.CompilerParams(vmem_limit_bytes=4 << 20),
        name="mix",
    )(place, grp, *scored, *sufs, *pieces)


def proj_kernel(steps, last, where_ref, *refs):
    att = refs[: 2 * len(steps)]
    own, *far = refs[2 * len(steps) : 2 * len(steps) + 5]
    o_ref = refs[-1]
    cols = o_ref.shape[1] // 2
    rows = o_ref.shape[0]
    core = where_ref[1]
    side = where_ref[2]
    tall = 256
    for r0 in range(0, rows, tall):
        at = slice(r0, r0 + tall)
        for x in range(2):
            c = pl.ds(pl.multiple_of(lax.bitwise_xor(side, x) * cols, cols), cols)
            acc = refs[-2][at, c] if last else jnp.zeros((tall, cols), jnp.float32)
            for h in range(2):
                head = lax.bitwise_xor(core, h)
                lines = []
                for i, m in enumerate(steps):
                    lines.append((m, att[h * len(steps) + i][at, :]))
                if last:
                    lines = [(3, lines[0][1] + lines[1][1])]
                for m, a in lines:
                    if m == 0:
                        w = own[pl.ds(pl.multiple_of(head * HD, HD), HD), c]
                    else:
                        w = far[2 * h + x][m - 1]
                    acc = acc + jnp.dot(a, w, preferred_element_type=jnp.float32)
            o_ref[at, c] = acc.astype(o_ref.dtype)


def project(where, steps, att, own, far, add=None):
    rows = att[0].shape[0]
    cols = own.shape[1]
    extra = [] if add is None else [add]
    return pl.pallas_call(
        functools.partial(proj_kernel, steps, add is not None),
        out_shape=jax.ShapeDtypeStruct((rows, cols), jnp.float32 if add is None else jnp.bfloat16),
        in_specs=[SMEM] + [VMEM] * (len(att) + 1 + len(far) + len(extra)),
        out_specs=VMEM,
        compiler_params=pltpu.CompilerParams(vmem_limit_bytes=6 << 20),
        name="project",
    )(where, *att, own, *far, *extra)


def swap(x, axis, mask, size):
    return lax.ppermute(x, axis, [(i, i ^ mask) for i in range(size)])


def after(x, *deps):
    return lax.optimization_barrier((x,) + deps)[0]


over_x = functools.partial(swap, axis="req", mask=2, size=8)
over_y = functools.partial(swap, axis="req", mask=4, size=8)
over_core = functools.partial(swap, axis="req", mask=1, size=8)


def split_heads(suffix_heads, prefix_cache, lengths, groups, owners, out_weight):
    rows = suffix_heads.shape[0]
    me = lax.axis_index("req")
    z = lax.axis_index("tp")
    core = me & 1
    side = (me >> 1) & 1
    where = jnp.stack([z, core, side]).astype(jnp.int32)
    place = jnp.sum(
        jnp.where(
            owners[None] == (me ^ jnp.arange(SLOTS, dtype=jnp.int32))[:, None, None],
            jnp.arange(SLOTS, dtype=jnp.int32).reshape(1, GROUPS, OWNERS),
            0,
        ),
        axis=(1, 2),
    ).astype(jnp.int32)
    tp_size = 4
    first_head = core == 0

    cols = out_weight.shape[1] // tp_size
    z_u, core_u, side_u = (i.astype(jnp.uint32) for i in (z, core, side))
    starts = [core_u * HD, z_u * cols]
    starts += [(z_u ^ m) * cols + side_u * (cols // 2) for m in range(1, tp_size)]
    first_head, *starts = lax.optimization_barrier((first_head, *starts))
    sends = [
        lax.dynamic_slice(out_weight, (starts[0], starts[1 + m]), (HD, cols // 2))
        for m in range(1, tp_size)
    ]
    w_own = lax.dynamic_slice(
        out_weight, (jnp.zeros_like(starts[0]), starts[1]), (out_weight.shape[0], cols)
    )

    k = prefix_cache[:, 0]
    k_own = jnp.where(first_head, k[:, :HD], k[:, HD:])
    k_other = jnp.where(first_head, k[:, HD:], k[:, :HD])
    k_both = jnp.stack([k_own, over_core(k_other)])
    kx = over_x(k_both)
    ky = over_y(k_both)
    w_one, w_two = (swap(sends[m - 1], "tp", m, tp_size) for m in (1, 2))

    table = jnp.concatenate([lengths, groups], axis=0)
    table_pair = over_core(table)
    suffix = after(suffix_heads, k_both)
    first, grp, mine, other = prepare(
        after(where, k_both), (table, table_pair), suffix[:, 0], suffix[:, 1], suffix[:, 2]
    )
    sufs = [mine, over_core(other)]
    v = after(prefix_cache, k_both)[:, 1]
    v_own = jnp.where(first_head, v[:, :HD], v[:, HD:])
    v_other = jnp.where(first_head, v[:, HD:], v[:, :HD])
    v_both = jnp.stack([v_own, over_core(v_other)])

    kxy = over_y(after(kx[0:1], mine, v_both))
    kyx = over_x(after(ky[1:2], mine, v_both))
    v_both = after(v_both, kxy, kyx, w_one, w_two, w_own, sufs[1])
    vx = over_x(v_both)
    vy = over_y(v_both)
    w_three = swap(after(sends[2], w_two), "tp", 3, tp_size)
    scored = score(place, first, grp, sufs, (k_both, kx, ky, kxy, kyx))
    w_far = jnp.stack([after(w_one, scored[0]), w_two, w_three])
    w_core = over_core(w_far)
    vxy = over_y(after(vx[0:1], scored[0], w_far))
    vyx = over_x(after(vy[1:2], scored[0], w_far))
    v_pieces = (v_both, vx, vy, vxy, vyx)
    (own,) = mix(0, HD, place, grp, scored, sufs[:1], v_pieces)
    (pair,) = mix(0, HD, place, grp, scored, sufs[1:], v_pieces, rows)
    w_x = over_x(after(w_far, vxy, vyx))

    back = over_core(pair)
    two_own = swap(own, "tp", 2, tp_size)
    one_own = swap(own, "tp", 1, tp_size)
    later = after(back, two_own)
    two_back = swap(later, "tp", 2, tp_size)
    one_back = swap(later, "tp", 1, tp_size)
    three_own = lax.ppermute(after(own, two_own, one_own), "tp", [(1, 2), (2, 1)])
    forward_own = lax.ppermute(two_own, "tp", [(2, 3), (1, 0)])
    three_back = lax.ppermute(after(later, two_back), "tp", [(1, 2), (2, 1)])
    forward_back = lax.ppermute(two_back, "tp", [(2, 3), (1, 0)])
    w_core_x = over_core(after(w_x, two_back, one_back, three_own, forward_own))
    far = [w_far, w_x, w_core, w_core_x]
    near = project(where, (0, 1, 2), (own, one_own, two_own, back, one_back, two_back), w_own, far)
    last = (three_own, forward_own, three_back, forward_back)
    return project(where, (3, 3), last, w_own, far, near)


def whole_heads(suffix_heads, prefix_cache, lengths, groups, owners, out_weight):
    heads = suffix_heads.shape[2] // HD
    received = [
        from_root(prefix_cache, "req", owners[i // OWNERS, i % OWNERS]) for i in range(SLOTS)
    ]
    place = jnp.arange(SLOTS, dtype=jnp.int32)
    first, grp, *sufs = prepare(
        jnp.zeros((3,), jnp.int32),
        (jnp.concatenate([lengths, groups], axis=0),),
        suffix_heads[:, 0],
        suffix_heads[:, 1],
        suffix_heads[:, 2],
    )
    attended = []
    for h in range(heads):
        keys = [s[None, :, 0, h * HD : (h + 1) * HD] for s in received]
        values = [s[None, :, 1, h * HD : (h + 1) * HD] for s in received]
        scored = score(place, first, grp, [sufs[h]], keys)
        attended += mix(0, HD, place, grp, scored, [sufs[h]], values)
    partial_out = jnp.dot(
        jnp.concatenate(attended, axis=1), out_weight, preferred_element_type=jnp.float32
    )
    return lax.psum_scatter(partial_out.astype(jnp.bfloat16), "tp", scatter_dimension=1, tiled=True)


def per_device(req_size, tp_size, *args):
    if req_size == 8 and tp_size == 4 and args[0].shape[2] == 2 * HD:
        return split_heads(*args)
    return whole_heads(*args)


def solution(mesh):
    placed = (
        P("req", None, "tp"),
        P("req", None, "tp"),
        P("req", None),
        P("req", None),
        P(),
        P("tp", None),
    )
    return jax.shard_map(
        functools.partial(per_device, mesh.shape["req"], mesh.shape["tp"]),
        mesh=mesh,
        in_specs=placed,
        out_specs=P("req", "tp"),
        check_vma=False,
    )
```

```python
import functools
import jax
import jax.numpy as jnp
import numpy as np
from jax import lax
from jax.experimental import pallas as pl
from jax.experimental.pallas import tpu as pltpu
from jax.sharding import PartitionSpec as P

HD = 256
ROT = 64
BLK = 512
OWNERS = 2
GROUPS = 4
SLOTS = GROUPS * OWNERS
MOST = 128
SEEN = OWNERS * BLK

NEG_FILL = -1e30
ROPE_BASE = 10000.0
FACTOR = HD ** (-0.5) * 1.4426950408889634

RB = 128

VMEM = pl.BlockSpec(memory_space=pltpu.VMEM)
SMEM = pl.BlockSpec(memory_space=pltpu.SMEM)


def from_root(x, axis, root):
    mine = lax.axis_index(axis) == root
    return lax.psum(jnp.where(mine, x, jnp.zeros_like(x)), axis)


def rope_table():
    inverse = np.float32(ROPE_BASE) ** (-2.0 * np.arange(ROT // 2, dtype=np.float32) / ROT)
    inverse = np.concatenate([np.repeat(inverse, 2), np.zeros(128 - ROT)]).astype(np.float32)
    angles = np.arange(SEEN, SEEN + MOST, dtype=np.float32)[:, None] * inverse[None, :]
    angles = angles.astype(np.float64)
    sign = np.where(np.arange(128) % 2 == 0, -1.0, 1.0)
    table = np.concatenate([np.cos(angles), np.sin(angles) * sign[None, :]], axis=1)
    return jnp.asarray(table.astype(np.float32))


def prep_kernel(spans, where_ref, *refs):
    tables = refs[:spans]
    q_ref, k_ref, v_ref, rope_ref = refs[spans : spans + 4]
    first_ref, grp_ref = refs[spans + 4 : spans + 6]
    o_refs = refs[spans + 6 :]
    rows = q_ref.shape[0]
    heads = len(o_refs)
    lane = lax.broadcasted_iota(jnp.int32, (RB, 128), 1)
    even = (lane % 2) == 0
    for n in range(spans):
        requests = tables[n].shape[1]
        for r0 in range(0, rows, RB):
            row = r0 + lax.broadcasted_iota(jnp.int32, (RB, 128), 0)
            start = jnp.int32(0)
            first = jnp.zeros((RB, 128), jnp.int32)
            grp = jnp.zeros((RB, 128), jnp.int32) + tables[n][1, 0]
            for r in range(1, requests):
                start = start + tables[n][0, r - 1]
                later = row >= start
                first = jnp.where(later, start, first)
                grp = jnp.where(later, tables[n][1, r], grp)
            first_ref[n * rows + r0 : n * rows + r0 + RB, :] = first
            grp_ref[n * rows + r0 : n * rows + r0 + RB, :] = grp
    for r0 in range(0, rows, RB):
        at = slice(r0, r0 + RB)
        row = r0 + lax.broadcasted_iota(jnp.int32, (RB, 128), 0)
        chosen = jnp.where(row - first_ref[at, :] == lane, 1.0, 0.0)
        turn = lax.dot_general(
            chosen,
            rope_ref[...],
            (((1,), (0,)), ((), ())),
            precision=lax.Precision.HIGHEST,
            preferred_element_type=jnp.float32,
        )
        cos = turn[:, :128]
        sin = turn[:, 128:]
        for i, o_ref in enumerate(o_refs):
            flip = where_ref[1] > 0
            for n, ref in enumerate((q_ref, k_ref)):
                x = ref[at, i * HD : (i + 1) * HD]
                if heads == 2:
                    x = jnp.where(flip, ref[at, (1 - i) * HD : (2 - i) * HD], x)
                y = x[:, :128].astype(jnp.float32)
                swapped = jnp.where(even, pltpu.roll(y, 127, 1), pltpu.roll(y, 1, 1))
                o_ref[n, at, 0:128] = (y * cos + swapped * sin).astype(jnp.bfloat16)
                o_ref[n, at, 128:HD] = x[:, 128:]
            v = v_ref[at, i * HD : (i + 1) * HD]
            if heads == 2:
                v = jnp.where(flip, v_ref[at, (1 - i) * HD : (2 - i) * HD], v)
            o_ref[2, at, :] = v


def prepare(where, tables, q, k, v):
    rows, feat = q.shape
    heads = feat // HD
    spans = len(tables)
    column = jax.ShapeDtypeStruct((spans * rows, 128), jnp.int32)
    return pl.pallas_call(
        functools.partial(prep_kernel, spans),
        out_shape=[column] * 2 + [jax.ShapeDtypeStruct((3, rows, HD), jnp.bfloat16)] * heads,
        in_specs=[SMEM] * (1 + spans) + [VMEM] * 4,
        out_specs=[VMEM] * (2 + heads),
        compiler_params=pltpu.CompilerParams(vmem_limit_bytes=4 << 20),
        name="prepare",
    )(where, *tables, q, k, v, rope_table())


def wide(x, width):
    return x if width == 128 else jnp.concatenate([x] * (width // 128), axis=1)


def flatten(refs, counts):
    return [ref.at[j] for ref, count in zip(refs, counts) for j in range(count)]


def score_kernel(nb, counts, place_ref, first_ref, grp_ref, *rest):
    sufs = rest[:nb]
    n_pieces = len(counts)
    pieces = flatten(rest[nb : nb + n_pieces], counts)
    p_ref, near_ref, den_ref, sc = rest[nb + n_pieces :]
    half = 256
    for n in range(nb):
        rows = sufs[n].shape[1]
        for b in range(rows // RB):
            r0 = b * RB
            t0 = n * rows + r0
            buf = (t0 // RB) % 2
            q = sufs[n][0, r0 : r0 + RB, :]
            grp = wide(grp_ref[t0 : t0 + RB, :], half)
            for d in range(SLOTS):
                g = place_ref[d] // OWNERS
                o = place_ref[d] % OWNERS
                for j in range(BLK // half):
                    s = lax.dot_general(
                        q,
                        pieces[d][j * half : (j + 1) * half, :],
                        (((1,), (1,)), ((), ())),
                        preferred_element_type=jnp.float32,
                    )
                    at = pl.ds(pl.multiple_of(o * BLK + j * half, half), half)
                    sc[buf, :, at] = jnp.where(grp == g, s, sc[buf, :, at])
            lo = max(0, r0 - MOST)
            width = r0 + RB - lo
            local = lax.dot_general(
                q,
                sufs[n][1, lo : r0 + RB, :],
                (((1,), (1,)), ((), ())),
                preferred_element_type=jnp.float32,
            )
            row = r0 + lax.broadcasted_iota(jnp.int32, (RB, width), 0)
            key = lo + lax.broadcasted_iota(jnp.int32, (RB, width), 1)
            start = wide(first_ref[t0 : t0 + RB, :], width)
            local = jnp.where((key <= row) & (key >= start), local, NEG_FILL)
            top = jnp.max(local, axis=1, keepdims=True)
            whole = sc[buf, :, 0:half]
            for c0 in range(half, SEEN, half):
                whole = jnp.maximum(whole, sc[buf, :, c0 : c0 + half])
            top = jnp.maximum(top, jnp.max(whole, axis=1, keepdims=True))
            e = jnp.exp2((local - top) * FACTOR)
            den = jnp.sum(e, axis=1, keepdims=True)
            near_ref[t0 : t0 + RB, 0:width] = e.astype(jnp.bfloat16)
            total = None
            for c0 in range(0, SEEN, half):
                e = jnp.exp2((sc[buf, :, c0 : c0 + half] - top) * FACTOR)
                p_ref[t0 : t0 + RB, c0 : c0 + half] = e.astype(jnp.bfloat16)
                total = e if total is None else total + e
            den = den + jnp.sum(total, axis=1, keepdims=True)
            den_ref[t0 : t0 + RB, :] = jnp.broadcast_to(den, (RB, 128))


def score(place, first, grp, sufs, pieces):
    rows = sum(s.shape[1] for s in sufs)
    return pl.pallas_call(
        functools.partial(score_kernel, len(sufs), tuple(p.shape[0] for p in pieces)),
        out_shape=[
            jax.ShapeDtypeStruct((rows, SEEN), jnp.bfloat16),
            jax.ShapeDtypeStruct((rows, RB + MOST), jnp.bfloat16),
            jax.ShapeDtypeStruct((rows, 128), jnp.float32),
        ],
        in_specs=[SMEM] + [VMEM] * (2 + len(sufs) + len(pieces)),
        out_specs=[VMEM] * 3,
        scratch_shapes=[pltpu.VMEM((2, RB, SEEN), jnp.float32)],
        compiler_params=pltpu.CompilerParams(vmem_limit_bytes=4 << 20),
        name="score",
    )(place, first, grp, *sufs, *pieces)


def mix_kernel(nb, base, counts, col, place_ref, grp_ref, p_ref, near_ref, den_ref, *rest):
    sufs = rest[:nb]
    n_pieces = len(counts)
    pieces = flatten(rest[nb : nb + n_pieces], counts)
    outs = rest[nb + n_pieces :]
    width = outs[0].shape[1]
    for n in reversed(range(nb)):
        rows = outs[n].shape[0]
        for b in range(rows // RB):
            r0 = b * RB
            t0 = base + n * rows + r0
            grp = wide(grp_ref[t0 : t0 + RB, :], width)
            lo = max(0, r0 - MOST)
            acc = jnp.dot(
                near_ref[t0 : t0 + RB, 0 : r0 + RB - lo],
                sufs[n][2, lo : r0 + RB, col : col + width],
                preferred_element_type=jnp.float32,
            )
            for d in range(SLOTS):
                g = place_ref[d] // OWNERS
                o = place_ref[d] % OWNERS
                part = jnp.dot(
                    p_ref[t0 : t0 + RB, pl.ds(pl.multiple_of(o * BLK, BLK), BLK)],
                    pieces[d][...],
                    preferred_element_type=jnp.float32,
                )
                acc = acc + jnp.where(grp == g, part, 0.0)
            den = wide(den_ref[t0 : t0 + RB, :], width)
            outs[n][r0 : r0 + RB, :] = (acc / den).astype(jnp.bfloat16)


def mix(col, width, place, grp, scored, sufs, pieces, base=0):
    rows = sufs[0].shape[1]
    nb = len(sufs)
    return pl.pallas_call(
        functools.partial(mix_kernel, nb, base, tuple(p.shape[0] for p in pieces), col),
        out_shape=[jax.ShapeDtypeStruct((rows, width), jnp.bfloat16)] * nb,
        in_specs=[SMEM] + [VMEM] * (4 + nb + len(pieces)),
        out_specs=[VMEM] * nb,
        compiler_params=pltpu.CompilerParams(vmem_limit_bytes=4 << 20),
        name="mix",
    )(place, grp, *scored, *sufs, *pieces)


def proj_kernel(plan, last, where_ref, *refs):
    n_att = sum(len(steps) for steps in plan)
    att = list(refs[:n_att])
    own, *far = refs[n_att : n_att + 5]
    o_ref = refs[-1]
    cols = o_ref.shape[1] // 2
    rows = o_ref.shape[0]
    core = where_ref[1]
    side = where_ref[2]
    tall = 256
    for r0 in range(0, rows, tall):
        at = slice(r0, r0 + tall)
        for x in range(2):
            c = pl.ds(pl.multiple_of(lax.bitwise_xor(side, x) * cols, cols), cols)
            acc = refs[-2][at, c] if last else jnp.zeros((tall, cols), jnp.float32)
            i = 0
            for h, steps in enumerate(plan):
                head = lax.bitwise_xor(core, h)
                lines = {}
                for m in steps:
                    a = att[i][at, :]
                    lines[m] = lines[m] + a if m in lines else a
                    i += 1
                for m, a in lines.items():
                    if m == 0:
                        w = own[pl.ds(pl.multiple_of(head * HD, HD), HD), c]
                    else:
                        w = far[2 * h + x][m - 1]
                    acc = acc + jnp.dot(a, w, preferred_element_type=jnp.float32)
            o_ref[at, c] = acc.astype(o_ref.dtype)


def project(where, plan, att, own, far, add=None):
    rows = att[0].shape[0]
    cols = own.shape[1]
    extra = [] if add is None else [add]
    return pl.pallas_call(
        functools.partial(proj_kernel, plan, add is not None),
        out_shape=jax.ShapeDtypeStruct((rows, cols), jnp.float32 if add is None else jnp.bfloat16),
        in_specs=[SMEM] + [VMEM] * (len(att) + 1 + len(far) + len(extra)),
        out_specs=VMEM,
        compiler_params=pltpu.CompilerParams(vmem_limit_bytes=6 << 20),
        name="project",
    )(where, *att, own, *far, *extra)


def swap(x, axis, mask, size):
    return lax.ppermute(x, axis, [(i, i ^ mask) for i in range(size)])


def after(x, *deps):
    return lax.optimization_barrier((x,) + deps)[0]


over_x = functools.partial(swap, axis="req", mask=2, size=8)
over_y = functools.partial(swap, axis="req", mask=4, size=8)
over_core = functools.partial(swap, axis="req", mask=1, size=8)


def split_heads(suffix_heads, prefix_cache, lengths, groups, owners, out_weight):
    rows = suffix_heads.shape[0]
    me = lax.axis_index("req")
    z = lax.axis_index("tp")
    core = me & 1
    side = (me >> 1) & 1
    where = jnp.stack([z, core, side]).astype(jnp.int32)
    place = jnp.sum(
        jnp.where(
            owners[None] == (me ^ jnp.arange(SLOTS, dtype=jnp.int32))[:, None, None],
            jnp.arange(SLOTS, dtype=jnp.int32).reshape(1, GROUPS, OWNERS),
            0,
        ),
        axis=(1, 2),
    ).astype(jnp.int32)
    tp_size = 4
    first_head = core == 0

    cols = out_weight.shape[1] // tp_size
    z_u, core_u, side_u = (i.astype(jnp.uint32) for i in (z, core, side))
    starts = [core_u * HD, z_u * cols]
    starts += [(z_u ^ m) * cols + side_u * (cols // 2) for m in range(1, tp_size)]
    first_head, *starts = lax.optimization_barrier((first_head, *starts))
    sends = [
        lax.dynamic_slice(out_weight, (starts[0], starts[1 + m]), (HD, cols // 2))
        for m in range(1, tp_size)
    ]
    w_own = lax.dynamic_slice(
        out_weight, (jnp.zeros_like(starts[0]), starts[1]), (out_weight.shape[0], cols)
    )

    k = prefix_cache[:, 0]
    k_own = jnp.where(first_head, k[:, :HD], k[:, HD:])
    k_other = jnp.where(first_head, k[:, HD:], k[:, :HD])
    k_both = jnp.stack([k_own, over_core(k_other)])
    kx = over_x(k_both)
    ky = over_y(k_both)
    w_one, w_two = (swap(sends[m - 1], "tp", m, tp_size) for m in (1, 2))

    table = jnp.concatenate([lengths, groups], axis=0)
    table_pair = over_core(table)
    suffix = after(suffix_heads, k_both)
    first, grp, mine, other = prepare(
        after(where, k_both), (table, table_pair), suffix[:, 0], suffix[:, 1], suffix[:, 2]
    )
    sufs = [mine, over_core(other)]
    v = after(prefix_cache, k_both)[:, 1]
    v_own = jnp.where(first_head, v[:, :HD], v[:, HD:])
    v_other = jnp.where(first_head, v[:, HD:], v[:, :HD])
    v_both = jnp.stack([v_own, over_core(v_other)])

    kxy = over_y(after(kx[0:1], mine, v_both))
    kyx = over_x(after(ky[1:2], mine, v_both))
    v_both = after(v_both, kxy, kyx, w_one, w_two, w_own, sufs[1])
    vx = over_x(v_both)
    vy = over_y(v_both)
    w_three = swap(after(sends[2], w_two), "tp", 3, tp_size)
    scored = score(place, first, grp, sufs, (k_both, kx, ky, kxy, kyx))
    w_far = jnp.stack([after(w_one, scored[0]), w_two, w_three])
    w_core = over_core(w_far)
    vxy = over_y(after(vx[0:1], scored[0], w_far))
    vyx = over_x(after(vy[1:2], scored[0], w_far))
    v_pieces = (v_both, vx, vy, vxy, vyx)
    (own,) = mix(0, HD, place, grp, scored, sufs[:1], v_pieces)
    (pair,) = mix(0, HD, after(place, own), grp, scored, sufs[1:], v_pieces, rows)
    w_x = over_x(after(w_far, vxy, vyx))

    back = over_core(pair)
    two_own = swap(own, "tp", 2, tp_size)
    one_own = swap(own, "tp", 1, tp_size)
    later = after(back, two_own)
    two_back = swap(later, "tp", 2, tp_size)
    one_back = swap(later, "tp", 1, tp_size)
    three_own = lax.ppermute(after(own, two_own, one_own), "tp", [(1, 2), (2, 1)])
    forward_own = lax.ppermute(two_own, "tp", [(2, 3), (1, 0)])
    three_back = lax.ppermute(after(later, two_back), "tp", [(1, 2), (2, 1)])
    forward_back = lax.ppermute(two_back, "tp", [(2, 3), (1, 0)])
    w_core_x = over_core(after(w_x, two_back, one_back, three_own, forward_own))
    far = [w_far, w_x, w_core, w_core_x]
    near = project(
        where,
        ((0, 1, 2, 3, 3), (0, 1, 2)),
        (own, one_own, two_own, three_own, forward_own, back, one_back, two_back),
        w_own,
        far,
    )
    return project(where, ((), (3, 3)), (three_back, forward_back), w_own, far, near)


def whole_heads(suffix_heads, prefix_cache, lengths, groups, owners, out_weight):
    heads = suffix_heads.shape[2] // HD
    received = [
        from_root(prefix_cache, "req", owners[i // OWNERS, i % OWNERS]) for i in range(SLOTS)
    ]
    place = jnp.arange(SLOTS, dtype=jnp.int32)
    first, grp, *sufs = prepare(
        jnp.zeros((3,), jnp.int32),
        (jnp.concatenate([lengths, groups], axis=0),),
        suffix_heads[:, 0],
        suffix_heads[:, 1],
        suffix_heads[:, 2],
    )
    attended = []
    for h in range(heads):
        keys = [s[None, :, 0, h * HD : (h + 1) * HD] for s in received]
        values = [s[None, :, 1, h * HD : (h + 1) * HD] for s in received]
        scored = score(place, first, grp, [sufs[h]], keys)
        attended += mix(0, HD, place, grp, scored, [sufs[h]], values)
    partial_out = jnp.dot(
        jnp.concatenate(attended, axis=1), out_weight, preferred_element_type=jnp.float32
    )
    return lax.psum_scatter(partial_out.astype(jnp.bfloat16), "tp", scatter_dimension=1, tiled=True)


def per_device(req_size, tp_size, *args):
    if req_size == 8 and tp_size == 4 and args[0].shape[2] == 2 * HD:
        return split_heads(*args)
    return whole_heads(*args)


def solution(mesh):
    placed = (
        P("req", None, "tp"),
        P("req", None, "tp"),
        P("req", None),
        P("req", None),
        P(),
        P("tp", None),
    )
    return jax.shard_map(
        functools.partial(per_device, mesh.shape["req"], mesh.shape["tp"]),
        mesh=mesh,
        in_specs=placed,
        out_specs=P("req", "tp"),
        check_vma=False,
    )
```
